32 devices in a mesh: shard: 2 (over x), ctx: 4 (over y, core), tp: 4 (over z).
Axes of the slice: x: 2, y: 2, z: 4, core: 2. Of those that a mesh axis runs over, the one named last changes fastest.
Arguments:
- inputs: bfloat16 [2, 2, 4096, 768], P('shard', None, 'ctx'), may hold values from -6 to 6
- lengths: int32 [2, 2], P('shard'), may hold values from 2048 to 4096, as said below
- attn_gain: bfloat16 [768], P('shard'), may hold values from 0.099609375 to 1.8984375
- mlp_gain: bfloat16 [768], P('shard'), may hold values from 0.099609375 to 1.8984375
- qkv_weight: bfloat16 [768, 3, 768], P('shard', None, 'tp'), may hold values from -0.21875 to 0.21875
- attn_weight: bfloat16 [768, 768], P('tp', 'shard'), may hold values from -0.875 to 0.875
- mlp_in_weight: bfloat16 [768, 2, 1152], P('shard', None, 'tp'), may hold values from -0.21875 to 0.21875
- mlp_out_weight: bfloat16 [1152, 768], P('tp', 'shard'), may hold values from -0.1875 to 0.1875
- cotangent: bfloat16 [2, 2, 4096, 768], P('shard', None, 'ctx'), may hold values from -6 to 6
Outputs:
- layer_out: bfloat16 [2, 2, 4096, 768], P('shard', None, 'ctx')
- input_grad: bfloat16 [2, 2, 4096, 768], P('shard', None, 'ctx')
- qkv_grad: float32 [768, 3, 768], P('shard', None, 'tp')
- attn_grad: float32 [768, 768], P('tp', 'shard')
- mlp_in_grad: float32 [768, 2, 1152], P('shard', None, 'tp')
- mlp_out_grad: float32 [1152, 768], P('tp', 'shard')
- attn_gain_grad: float32 [768], P(('shard', 'tp'))
- mlp_gain_grad: float32 [768], P(('shard', 'tp'))
The draws below stay inside these ranges and needn't reach their ends.
Inputs may be any that keep to these rules, and one draw needn't show every extreme that they name: `lengths`: among the 2 sequences of each index of shard one has length 4096; some sequence has length 2048.
All inputs are finite; a program needn't handle non-finite values.
Results may differ from the reference program's by a relative error of at most 0.017.
Values may be sent and summed in bfloat16 or wider, within the bound.
A program may use at most 192 MiB of HBM per device.

```python
import math
import jax
import jax.numpy as jnp
from jax import lax

D = 768
H = 12
HD = 64
FF = 1152
HALF = 64
MB = 2
SEQ = 4096
N_SHARD = 2


def draw_lengths(key, part):
    key_drawn = jax.random.fold_in(key, 11)
    key_full = jax.random.fold_in(key, 12)
    key_least = jax.random.fold_in(key, 13)
    drawn = jax.random.randint(key_drawn, (N_SHARD, MB), SEQ // 2, SEQ + 1)
    full_slot = jax.random.randint(key_full, (N_SHARD,), 0, MB)
    columns = jnp.arange(MB)[None, :]
    lengths_all = jnp.where(columns == full_slot[:, None], SEQ, drawn)
    least_row = jax.random.randint(key_least, (), 0, N_SHARD)
    rows_index = jnp.arange(N_SHARD)[:, None]
    least_slot = (full_slot[:, None] + 1) % MB
    chosen_cell = (rows_index == least_row) & (columns == least_slot)
    lengths_all = jnp.where(chosen_cell, SEQ // 2, lengths_all)
    return lengths_all.astype(jnp.int32)


def level_of(key, shape, split, low, top_value):
    loudness = 1.0
    for axis_at, parts in split:
        heights = jax.random.uniform(jax.random.fold_in(jax.random.fold_in(key, 6), axis_at), (parts,), jnp.float32, low / len(split), top_value / len(split))
        loudness = loudness * jnp.repeat(jnp.exp(heights), shape[axis_at] // parts).reshape((-1,) + (1,) * (len(shape) - 1 - axis_at))
    return loudness


def bell_draw(rng, shape, scale, bound, split=(), held_as=jnp.bfloat16):
    entries = jax.random.normal(rng, shape, jnp.float32) * scale
    if len(split) > 0:
        entries = level_of(rng, shape, split, -0.22, 0.18) * entries
    return jnp.clip(entries, min=-bound, max=bound).astype(held_as)


def setup_inputs(seed: int = 0) -> dict:
    keys = jax.random.split(jax.random.key(seed), 10)
    return {
        "inputs": bell_draw(keys[0], (N_SHARD, MB, SEQ, D), 1.0, 6.0, ((0, 2), (2, 4))),
        "lengths": draw_lengths(jax.random.fold_in(keys[9], 71), 0),
        "attn_gain": jnp.clip(1.0 + 0.18 * jax.random.normal(keys[2], (D,), jnp.float32), 0.099609375, 1.8984375).astype(jnp.bfloat16),
        "mlp_gain": jnp.clip(1.0 + 0.18 * jax.random.normal(keys[3], (D,), jnp.float32), 0.099609375, 1.8984375).astype(jnp.bfloat16),
        "qkv_weight": bell_draw(keys[4], (D, 3, D), D ** -0.5, 0.21875, ((0, 2), (2, 4))),
        "attn_weight": bell_draw(keys[5], (D, D), (D // 16) ** -0.5, 0.875, ((0, 4), (1, 2))),
        "mlp_in_weight": bell_draw(keys[6], (D, 2, FF), D ** -0.5, 0.21875, ((0, 2), (2, 4))),
        "mlp_out_weight": bell_draw(keys[7], (FF, D), FF ** -0.5, 0.1875, ((0, 4), (1, 2))),
        "cotangent": bell_draw(keys[8], (N_SHARD, MB, SEQ, D), 1.0, 6.0, ((0, 2), (2, 4))),
    }


norm_eps = 1e-05
rope_base = 10000.0
masked_score = -1e+30

@jax.custom_vjp
def low(v):
    return lax.optimization_barrier(v.astype(jnp.bfloat16)).astype(jnp.float32)

@jax.custom_vjp
def low_back(v):
    return v

def low_keep(v):
    return (low(v), None)

def low_pass(kept, grad):
    return (grad,)

def back_keep(v):
    return (v, None)

def back_low(kept, grad):
    return (low(grad),)
low.defvjp(low_keep, low_pass)
low_back.defvjp(back_keep, back_low)

def layer_norm(values, gain_row):
    center = values - lax.optimization_barrier(jnp.mean(values, axis=-1, keepdims=True))
    variance = lax.optimization_barrier(jnp.mean(center * center, axis=-1, keepdims=True))
    return center * lax.rsqrt(variance + norm_eps) * gain_row

def rope_tables(positions):
    exponents = jnp.arange(0, HD, 2).astype(jnp.float32) / HD
    inverse = jnp.power(rope_base, -exponents)
    angles = positions[:, None] * inverse[None, :]
    angles = jnp.concatenate([angles, angles], axis=-1)[:, None, :]
    return (jnp.cos(angles), jnp.sin(angles))

def rotate(vector, cosine, sine_table):
    half_size = vector.shape[-1] // 2
    turned = jnp.concatenate([-vector[..., half_size:], vector[..., :half_size]], axis=-1)
    return vector * cosine + turned * sine_table

def geglu(gate_up):
    return jax.nn.gelu(gate_up[..., 0, :], approximate=False) * gate_up[..., 1, :]

def product(form, left, right):
    return jnp.einsum(form, left, right, precision=lax.Precision.HIGHEST)

def forward(seq_in, attn_gain, mlp_gain, qkv_weight, attn_weight, mlp_in_weight, mlp_out_weight, length):
    positions = jnp.arange(SEQ)
    valid_rows = (positions < length).astype(jnp.float32)[:, None]
    normed = low(layer_norm(seq_in, attn_gain))
    qkv_raw = low_back(product('td,dcf->tcf', normed, qkv_weight))
    heads_raw = qkv_raw.reshape(SEQ, 3, H, HD)
    cosine, sine_table = rope_tables(positions.astype(jnp.float32))
    queries = low(rotate(heads_raw[:, 0], cosine, sine_table))
    keys_all = low(rotate(heads_raw[:, 1], cosine, sine_table))
    values_all = low(heads_raw[:, 2])
    scores = low_back(product('qhd,khd->hqk', queries, keys_all) * (1.0 / math.sqrt(HD)))
    distance = positions[:, None] - positions[None, :]
    allowed = (jnp.abs(distance) <= HALF) & ((positions[None, :] < length) | (distance == 0))
    scores = jnp.where(allowed[None], scores, masked_score)
    top_score = lax.optimization_barrier(jnp.max(scores, axis=-1, keepdims=True))
    exponent_terms = jnp.exp(scores - top_score)
    soft_weights = exponent_terms / lax.optimization_barrier(jnp.sum(exponent_terms, axis=-1, keepdims=True))
    context = low(low_back(product('hqk,khd->qhd', low(soft_weights), values_all)))
    attn_out = low_back(product('tf,fd->td', context.reshape(SEQ, D), attn_weight))
    middle = seq_in + attn_out
    normed_mlp = low(layer_norm(middle, mlp_gain))
    gate_up = low_back(product('td,dcf->tcf', normed_mlp, mlp_in_weight))
    hidden = low(geglu(gate_up))
    mlp_out = low_back(product('tf,fd->td', hidden, mlp_out_weight))
    return (middle + mlp_out) * valid_rows

def reference(inputs, lengths, attn_gain, mlp_gain, qkv_weight, attn_weight, mlp_in_weight, mlp_out_weight, cotangent):
    weights = tuple((weight_item.astype(jnp.float32) for weight_item in (attn_gain, mlp_gain, qkv_weight, attn_weight, mlp_in_weight, mlp_out_weight)))
    seq_inputs = inputs.reshape(N_SHARD * MB, SEQ, D).astype(jnp.float32)
    seq_cotangent = cotangent.reshape(N_SHARD * MB, SEQ, D).astype(jnp.float32)
    seq_lengths = lengths.reshape(N_SHARD * MB).astype(jnp.int32)

    def one_sequence(totals, sequence_items):
        seq_in, seq_grad, length = sequence_items

        def run_forward(seq_values, *params):
            return forward(seq_values, *params, length)
        result, backward = jax.vjp(run_forward, seq_in, *weights)
        gradients = backward(seq_grad)
        totals = tuple((running + increment for running, increment in zip(totals, gradients[1:])))
        return (totals, (result.astype(jnp.bfloat16), gradients[0].astype(jnp.bfloat16)))
    zero_totals = tuple((jnp.zeros_like(weight_item) for weight_item in weights))
    totals, (out_rows, grad_rows) = lax.scan(one_sequence, zero_totals, (seq_inputs, seq_cotangent, seq_lengths))
    return (out_rows.reshape(inputs.shape), grad_rows.reshape(inputs.shape), totals[2], totals[3], totals[4], totals[5], totals[0], totals[1])
```

```python
import math

import numpy as np

import jax
import jax.numpy as jnp
from jax import lax
from jax.experimental import pallas as pl
from jax.experimental.pallas import tpu as pltpu
from jax.sharding import PartitionSpec as P

HD = 64
HALF = 64
TILE = 128
LANES = 128
norm_eps = 1e-05
rope_base = 10000.0
masked_score = -1e30
F32 = jnp.float32
BF16 = jnp.bfloat16
VMEM_LIMIT = 60 * 1024 * 1024


def nt(a, b):
    return lax.dot_general(a, b, (((1,), (1,)), ((), ())), preferred_element_type=F32)


def nn(a, b):
    return lax.dot_general(a, b, (((1,), (0,)), ((), ())), preferred_element_type=F32)


def tn(a, b):
    return lax.dot_general(a, b, (((0,), (0,)), ((), ())), preferred_element_type=F32)


def rope_constants(seq):
    w = rope_base ** (-np.arange(0, HD, 2) / HD)
    w = np.tile(w, 2 * LANES // HD)
    rows = np.arange(TILE)[:, None] * w
    blocks = (np.arange(seq // HALF + 4)[:, None] - 1) * HALF * w
    tables = (np.cos(rows), np.sin(rows), np.cos(blocks), np.sin(blocks))
    return tuple(t.astype(np.float32) for t in tables)


def rope_tile(tables, block):
    cos_r, sin_r, cos_b, sin_b = tables
    cb = cos_b[pl.ds(block + 1, 1), :]
    sb = sin_b[pl.ds(block + 1, 1), :]
    cr = cos_r[...]
    sr = sin_r[...]
    cosine = cr * cb - sr * sb
    sine = sr * cb + cr * sb
    first = lax.broadcasted_iota(jnp.int32, sine.shape, 1) % HD < HD // 2
    return cosine, jnp.where(first, -sine, sine), first


def turn(u, cosine, sine, first):
    other = jnp.where(first, pltpu.roll(u, LANES - HD // 2, 1), pltpu.roll(u, HD // 2, 1))
    return u * cosine + other * sine


def layer_stats(z):
    center = z - jnp.mean(z, axis=-1, keepdims=True)
    inv = lax.rsqrt(jnp.mean(center * center, axis=-1, keepdims=True) + norm_eps)
    return center * inv, inv


def layer_back(e, xhat, inv):
    return (e - jnp.mean(e, axis=-1, keepdims=True) - xhat * jnp.mean(e * xhat, axis=-1, keepdims=True)) * inv


def head_masks(shape):
    lane = lax.broadcasted_iota(jnp.int32, shape, 1)
    return lane < HD


def split_heads(c, low_head):
    zero = jnp.zeros_like(c)
    return jnp.concatenate([jnp.where(low_head, c, zero), jnp.where(low_head, zero, c)], axis=0)


def phase_qkv(x_ref, gain_ref, w_ref, tables, normed_ref, q_ref, k_ref, v_ref, block0, rows):
    width = x_ref.shape[1]
    scaling = 1.0 / math.sqrt(HD)

    def body(t, carry):
        r0 = pl.multiple_of(t * rows, rows)
        xhat, _ = layer_stats(x_ref[pl.ds(r0, rows), :].astype(F32))
        normed = (xhat * gain_ref[...].astype(F32)).astype(BF16)
        normed_ref[pl.ds(r0, rows), :] = normed
        for part, ref in enumerate((q_ref, k_ref, v_ref)):
            out = nt(normed, w_ref[part * width : (part + 1) * width, :])
            if part == 2:
                ref[pl.ds(r0, rows), :] = out.astype(BF16)
                continue
            for s in range(rows // TILE):
                cosine, sine, first = rope_tile(tables, block0 + t * (rows // HALF) + s * (TILE // HALF))
                if part == 0:
                    cosine, sine = cosine * scaling, sine * scaling
                for j in range(width // LANES):
                    u = out[s * TILE : (s + 1) * TILE, j * LANES : (j + 1) * LANES]
                    ref[pl.ds(r0 + s * TILE, TILE), j * LANES : (j + 1) * LANES] = turn(u, cosine, sine, first).astype(BF16)
        return carry

    lax.fori_loop(0, x_ref.shape[0] // rows, body, 0)


def phase_attend(q_ref, k_ref, v_ref, p_ref, ctx_ref, pos0, length):
    width = q_ref.shape[1]
    span = TILE + 2 * HALF

    def body(t, carry):
        r0 = pl.multiple_of(t * TILE, TILE)
        row = lax.broadcasted_iota(jnp.int32, (TILE, span), 0)
        col = lax.broadcasted_iota(jnp.int32, (TILE, span), 1)
        offset = col - row
        key_pos = pos0 + t * TILE - HALF + col
        allowed = (offset >= 0) & (offset <= 2 * HALF) & (key_pos >= 0) & ((key_pos < length) | (offset == HALF))
        bias = jnp.where(allowed, 0.0, masked_score).astype(F32)
        bias = jnp.concatenate([bias, bias], axis=0)
        low_head = head_masks((TILE, LANES))
        for j in range(width // LANES):
            lanes = slice(j * LANES, (j + 1) * LANES)
            q2 = split_heads(q_ref[pl.ds(r0 + HALF, TILE), lanes], low_head)
            scores = nt(q2, k_ref[pl.ds(r0, span), lanes]) + bias
            terms = jnp.exp(scores - jnp.max(scores, axis=-1, keepdims=True))
            probs = (terms * (1.0 / jnp.sum(terms, axis=-1, keepdims=True))).astype(BF16)
            p_ref[t, j] = probs
            out = nn(probs, v_ref[pl.ds(r0, span), lanes])
            ctx_ref[pl.ds(r0, TILE), lanes] = jnp.where(low_head, out[:TILE], out[TILE:]).astype(BF16)
        return carry

    lax.fori_loop(0, ctx_ref.shape[0] // TILE, body, 0)


def phase_mlp(x_ref, cot_ref, ctx_ref, gain_ref, wo_ref, wi_ref, wm_ref, out_ref, gm_ref, gml_ref, go_ref, nm_ref, hid_ref, dgu_ref, dctx_ref, gg_ref, pos0, length, rows):
    ff = wm_ref.shape[0]
    half = hid_ref.shape[1]
    gg_ref[...] = jnp.zeros_like(gg_ref)

    def body(t, carry):
        r0 = pl.multiple_of(t * rows, rows)
        here = pl.ds(r0, rows)
        gain = gain_ref[...].astype(F32)
        middle = x_ref[pl.ds(r0 + HALF, rows), :].astype(F32) + nn(ctx_ref[here, :], wo_ref[...])
        xhat, inv = layer_stats(middle)
        nm = (xhat * gain).astype(BF16)
        nm_ref[here, :] = nm
        gate = nt(nm, wi_ref[:ff, :])
        up = nt(nm, wi_ref[ff:, :])
        cdf = 0.5 + 0.5 * lax.erf(gate * math.sqrt(0.5))
        gelu = gate * cdf
        slope = cdf + gate * (jnp.exp(-0.5 * gate * gate) * (1.0 / math.sqrt(2.0 * math.pi)))
        hidden = (gelu * up).astype(BF16)
        hid_ref[here, :] = hidden[:, :half]
        valid = pos0 + r0 + lax.broadcasted_iota(jnp.int32, (rows, 1), 0) < length
        out_ref[here, :] = jnp.where(valid, middle + nn(hidden, wm_ref[...]), 0.0).astype(BF16)
        grad_out = jnp.where(valid, cot_ref[here, :].astype(F32), 0.0)
        grad_low = grad_out.astype(BF16)
        go_ref[here, :] = grad_low
        grad_hidden = nt(grad_low, wm_ref[...])
        grad_gate = (grad_hidden * up * slope).astype(BF16)
        grad_up = (grad_hidden * gelu).astype(BF16)
        dgu_ref[here, :half] = grad_gate[:, :half]
        dgu_ref[here, half:] = grad_up[:, :half]
        grad_nm = nn(grad_gate, wi_ref[:ff, :]) + nn(grad_up, wi_ref[ff:, :])
        gg_ref[...] += jnp.sum((grad_nm * xhat).reshape(rows // 8, 8, -1), axis=0)
        grad_middle = grad_out + layer_back(grad_nm * gain, xhat, inv)
        gm_ref[here, :] = grad_middle
        gm_low = grad_middle.astype(BF16)
        gml_ref[here, :] = gm_low
        dctx_ref[here, :] = nt(gm_low, wo_ref[...]).astype(BF16)
        return carry

    lax.fori_loop(0, ctx_ref.shape[0] // rows, body, 0)


def phase_attend_back(q_ref, k_ref, v_ref, p_ref, ctx_ref, dctx_ref, tables, dq_ref, dk_ref, dv_ref, block0):
    width = q_ref.shape[1]
    span = TILE + 2 * HALF
    scaling = 1.0 / math.sqrt(HD)
    dk_ref[...] = jnp.zeros_like(dk_ref)
    dv_ref[...] = jnp.zeros_like(dv_ref)

    def body(t, carry):
        r0 = pl.multiple_of(t * TILE, TILE)
        low_head = head_masks((TILE, LANES))
        cosine, sine, first = rope_tile(tables, block0 + 1 + t * (TILE // HALF))
        cosine, sine = cosine * scaling, sine * -scaling
        keys = pl.ds(r0, span)
        for j in range(width // LANES):
            lanes = slice(j * LANES, (j + 1) * LANES)
            probs = p_ref[t, j]
            kc = k_ref[keys, lanes]
            dc = dctx_ref[pl.ds(r0, TILE), lanes]
            row_term = dc.astype(F32) * ctx_ref[pl.ds(r0, TILE), lanes].astype(F32)
            row_low = jnp.sum(jnp.where(low_head, row_term, 0.0), axis=-1, keepdims=True)
            row_high = jnp.sum(jnp.where(low_head, 0.0, row_term), axis=-1, keepdims=True)
            row_term = jnp.concatenate([row_low, row_high], axis=0)
            dc2 = split_heads(dc, low_head)
            grad_probs = nt(dc2, v_ref[keys, lanes])
            grad_scores = (probs.astype(F32) * (grad_probs - row_term)).astype(BF16)
            dq2 = nn(grad_scores, kc)
            dq = jnp.where(low_head, dq2[:TILE], dq2[TILE:])
            dq_ref[pl.ds(r0, TILE), lanes] = turn(dq, cosine, sine, first).astype(BF16)
            q2 = split_heads(q_ref[pl.ds(r0 + HALF, TILE), lanes], low_head)
            dk_ref[keys, lanes] += tn(grad_scores, q2)
            dv_ref[keys, lanes] += tn(probs, dc2)
        return carry

    lax.fori_loop(0, dq_ref.shape[0] // TILE, body, 0)


def phase_input(x_ref, gm_ref, dq_ref, dk_ref, dv_ref, gain_ref, w_ref, tables, dqkv_ref, out_ref, gg_ref, block0, rows, half):
    width = x_ref.shape[1]
    gg_ref[...] = jnp.zeros_like(gg_ref)

    def body(t, carry):
        r0 = pl.multiple_of(t * rows, rows)
        here = pl.ds(r0, rows)
        gain = gain_ref[...].astype(F32)
        pieces = []
        for s in range(rows // TILE):
            cosine, sine, first = rope_tile(tables, block0 + 1 + t * (rows // HALF) + s * (TILE // HALF))
            sub = pl.ds(r0 + s * TILE, TILE)
            chunk = [turn(dk_ref[sub, j * LANES : (j + 1) * LANES], cosine, -sine, first).astype(BF16) for j in range(width // LANES)]
            pieces.append(jnp.concatenate(chunk, axis=1))
        dk = jnp.concatenate(pieces, axis=0)
        dq = dq_ref[here, :]
        dv = dv_ref[here, :].astype(BF16)
        for part, piece in enumerate((dq, dk, dv)):
            dqkv_ref[here, part * half : (part + 1) * half] = piece[:, :half]
        grad_normed = nn(dq, w_ref[:width, :]) + nn(dk, w_ref[width : 2 * width, :]) + nn(dv, w_ref[2 * width :, :])
        xhat, inv = layer_stats(x_ref[here, :].astype(F32))
        gg_ref[...] += jnp.sum((grad_normed * xhat).reshape(rows // 8, 8, -1), axis=0)
        out_ref[here, :] = (gm_ref[here, :] + layer_back(grad_normed * gain, xhat, inv)).astype(BF16)
        return carry

    lax.fori_loop(0, x_ref.shape[0] // rows, body, 0)


def weight_grad(a_ref, b_ref, out_ref, columns):
    for c in range(0, a_ref.shape[1], columns):
        out_ref[c : c + columns, :] = tn(a_ref[:, c : c + columns], b_ref[...]).astype(out_ref.dtype)


def call(kernel, outs, *args, scratch=(), name=None):
    vmem = pl.BlockSpec(memory_space=pltpu.VMEM)
    smem = pl.BlockSpec(memory_space=pltpu.SMEM)
    return pl.pallas_call(
        kernel,
        out_shape=[jax.ShapeDtypeStruct(s, d) for s, d in outs],
        in_specs=[smem if a.dtype == jnp.int32 else vmem for a in args],
        out_specs=[vmem] * len(outs),
        scratch_shapes=list(scratch),
        compiler_params=pltpu.CompilerParams(vmem_limit_bytes=VMEM_LIMIT),
        name=name,
    )(*args)


def on_device(inputs, lengths, attn_gain, mlp_gain, qkv_weight, attn_weight, mlp_in_weight, mlp_out_weight, cotangent):
    n_tp = lax.axis_size("tp")
    n_ctx = lax.axis_size("ctx")
    tp = lax.axis_index("tp")
    ctx = lax.axis_index("ctx")
    seqs, local = inputs.shape[1], inputs.shape[2]
    width = inputs.shape[3]
    group = n_tp // 2
    mine = tp % seqs
    pair = tp // 2
    tables = tuple(jnp.asarray(t) for t in rope_constants(local * n_ctx))

    def gather(shard):
        full = lax.all_gather(shard, "shard", axis=2, tiled=True)
        full = lax.all_gather(full, "tp", axis=1, tiled=False)
        k, _, own, cols = full.shape
        full = full.reshape(k, 2, 2 * own, cols)
        first = lax.dynamic_index_in_dim(full, pair, 1, keepdims=False)
        second = lax.dynamic_index_in_dim(full, 1 - pair, 1, keepdims=False)
        return jnp.concatenate([first, second], axis=1).reshape(k * n_tp * own, cols)

    wqkv = gather(jnp.transpose(qkv_weight, (1, 2, 0)))
    wo = gather(attn_weight[None])
    wi = gather(jnp.transpose(mlp_in_weight, (1, 2, 0)))
    wm = gather(mlp_out_weight[None])
    gain1 = lax.all_gather(attn_gain, "shard", axis=0, tiled=True)[None]
    gain2 = lax.all_gather(mlp_gain, "shard", axis=0, tiled=True)[None]

    x_own = lax.dynamic_index_in_dim(inputs[0], mine, 0, keepdims=False)
    cot = lax.dynamic_index_in_dim(cotangent[0], mine, 0, keepdims=False)
    length = lax.dynamic_index_in_dim(lengths[0], mine, 0, keepdims=True)
    up = [(i, i + 1) for i in range(n_ctx - 1)]
    down = [(i + 1, i) for i in range(n_ctx - 1)]
    before = lax.ppermute(x_own[local - HALF :], "ctx", up)
    after = lax.ppermute(x_own[:HALF], "ctx", down)
    x_ext = jnp.concatenate([before, x_own, after], axis=0)
    ext = local + 2 * HALF
    block0 = ctx * (local // HALF) - 1
    pos0 = ctx * local
    scalars = jnp.stack([length[0], pos0.astype(jnp.int32), block0.astype(jnp.int32)])
    tiles = local // TILE
    chunks = width // LANES
    span = TILE + 2 * HALF

    def kernel_a(s_ref, x_ref, g_ref, w_ref, c0, s0, c1, s1, normed, q, k, v, p, ctx_out):
        phase_qkv(x_ref, g_ref, w_ref, (c0, s0, c1, s1), normed, q, k, v, s_ref[2], 384)
        phase_attend(q, k, v, p, ctx_out, s_ref[1], s_ref[0])

    wide = ((ext, width), BF16)
    tall = ((local, width), BF16)
    normed, q, k, v, probs, context = call(
        kernel_a,
        [wide, wide, wide, wide, ((tiles, chunks, 2 * TILE, span), BF16), tall],
        scalars, x_ext, gain1, wqkv, *tables,
        name="attend",
    )
    ff = wm.shape[0]
    ff_half = ff // 2

    def kernel_d(s_ref, x_ref, cot_ref, ctx_ref, g_ref, wo_ref, wi_ref, wm_ref, out, gm, gml, dctx, gg, dwm, dwi, go, nm, hid, dgu):
        phase_mlp(x_ref, cot_ref, ctx_ref, g_ref, wo_ref, wi_ref, wm_ref, out, gm, gml, go, nm, hid, dgu, dctx, gg, s_ref[1], s_ref[0], 256)
        weight_grad(hid, go, dwm, 192)
        weight_grad(dgu, nm, dwi, 384)

    layer_out, gm, gml, dctx, gain2_part, dwm, dwi = call(
        kernel_d,
        [tall, ((local, width), F32), tall, tall, ((8, width), F32), ((ff_half, width), F32), ((2 * ff_half, width), F32)],
        scalars, x_ext, cot, context, gain2, wo, wi, wm,
        scratch=[pltpu.VMEM((local, width), BF16), pltpu.VMEM((local, width), BF16), pltpu.VMEM((local, ff_half), BF16), pltpu.VMEM((local, 2 * ff_half), BF16)],
        name="feed_forward",
    )
    width_half = width // 2

    def kernel_e(s_ref, q_ref, k_ref, v_ref, p_ref, ctx_ref, dctx_ref, gml_ref, c0, s0, c1, s1, dq, dk, dv, dwo):
        phase_attend_back(q_ref, k_ref, v_ref, p_ref, ctx_ref, dctx_ref, (c0, s0, c1, s1), dq, dk, dv, s_ref[2])
        for c in range(0, width_half, LANES):
            dwo[c : c + LANES, :] = tn(ctx_ref[:, c : c + LANES], gml_ref[...])

    dq, dk, dv, dwo = call(
        kernel_e,
        [tall, ((ext, width), F32), ((ext, width), F32), ((width_half, width), F32)],
        scalars, q, k, v, probs, context, dctx, gml, *tables,
        name="attend_back",
    )
    rims = jnp.stack([dk, dv])
    to_lower = lax.ppermute(rims[:, :HALF], "ctx", down)
    to_upper = lax.ppermute(rims[:, ext - HALF :], "ctx", up)
    rims = rims[:, HALF : HALF + local]
    rims = jnp.concatenate([rims[:, :HALF] + to_upper, rims[:, HALF : local - HALF], rims[:, local - HALF :] + to_lower], axis=1)

    def kernel_g(s_ref, x_ref, n_ref, gm_ref, dq_ref, dk_ref, dv_ref, g_ref, w_ref, c0, s0, c1, s1, out, gg, dw, dqkv):
        phase_input(x_ref, gm_ref, dq_ref, dk_ref, dv_ref, g_ref, w_ref, (c0, s0, c1, s1), dqkv, out, gg, s_ref[2], 256, width_half)
        weight_grad(dqkv, n_ref, dw, 384)

    input_grad, gain1_part, dwqkv = call(
        kernel_g,
        [tall, ((8, width), F32), ((3 * width_half, width), F32)],
        scalars, x_own, normed[HALF : HALF + local], gm, dq, rims[0], rims[1], gain1, wqkv, *tables,
        scratch=[pltpu.VMEM((local, 3 * width_half), BF16)],
        name="input_back",
    )

    def both(own):
        turn_z = [(i, (i + 1) % n_tp) for i in range(n_tp)]
        other = lax.ppermute(own, "tp", turn_z)
        low = jnp.where(mine == 0, own, other)
        high = jnp.where(mine == 0, other, own)
        return jnp.stack([low, high])[None]

    def owned(grad, parts):
        g = grad.reshape(parts, 2, -1, grad.shape[-1])
        keep = lax.dynamic_index_in_dim(g, tp % 2, 1, keepdims=False)
        send = lax.dynamic_index_in_dim(g, 1 - tp % 2, 1, keepdims=False)
        swap = [(i, i ^ 1) for i in range(n_tp)]
        g = keep + lax.ppermute(send.astype(BF16), "tp", swap).astype(F32)
        g = lax.psum(g, "ctx")
        return lax.psum_scatter(g, "shard", scatter_dimension=2, tiled=True)

    qkv_grad = jnp.transpose(owned(dwqkv, 3), (2, 0, 1))
    attn_grad = owned(dwo, 1)[0]
    mlp_in_grad = jnp.transpose(owned(dwi, 2), (2, 0, 1))
    mlp_out_grad = owned(dwm, 1)[0]
    gains = jnp.stack([jnp.sum(gain1_part, 0), jnp.sum(gain2_part, 0)])
    gains = jnp.where(tp < 2, gains, 0.0)
    gains = lax.psum(gains, ("shard", "ctx", "tp"))
    share = width // (lax.axis_size("shard") * n_tp)
    gains = lax.dynamic_slice_in_dim(gains, (lax.axis_index("shard") * n_tp + tp) * share, share, axis=1)
    return (both(layer_out), both(input_grad), qkv_grad, attn_grad, mlp_in_grad, mlp_out_grad, gains[0], gains[1])


def solution(mesh):
    in_specs = (
        P("shard", None, "ctx", None),
        P("shard", None),
        P("shard"),
        P("shard"),
        P("shard", None, "tp"),
        P("tp", "shard"),
        P("shard", None, "tp"),
        P("tp", "shard"),
        P("shard", None, "ctx", None),
    )
    out_specs = (
        P("shard", None, "ctx", None),
        P("shard", None, "ctx", None),
        P("shard", None, "tp"),
        P("tp", "shard"),
        P("shard", None, "tp"),
        P("tp", "shard"),
        P(("shard", "tp")),
        P(("shard", "tp")),
    )
    return jax.shard_map(on_device, mesh=mesh, in_specs=in_specs, out_specs=out_specs, check_vma=False)
```

```python
import functools
import math

import numpy as np

import jax
import jax.numpy as jnp
from jax import lax
from jax.experimental import pallas as pl
from jax.experimental.pallas import tpu as pltpu
from jax.sharding import PartitionSpec as P

HD = 64
HALF = 64
TILE = 128
LANES = 128
norm_eps = 1e-05
rope_base = 10000.0
masked_score = -1e30
F32 = jnp.float32
BF16 = jnp.bfloat16
VMEM_LIMIT = 60 * 1024 * 1024


def nt(a, b):
    return lax.dot_general(a, b, (((1,), (1,)), ((), ())), preferred_element_type=F32)


def nn(a, b):
    return lax.dot_general(a, b, (((1,), (0,)), ((), ())), preferred_element_type=F32)


def tn(a, b):
    return lax.dot_general(a, b, (((0,), (0,)), ((), ())), preferred_element_type=F32)


def rope_constants(seq):
    w = rope_base ** (-np.arange(0, HD, 2) / HD)
    w = np.tile(w, 2 * LANES // HD)
    rows = np.arange(TILE)[:, None] * w
    blocks = (np.arange(seq // HALF + 4)[:, None] - 1) * HALF * w
    tables = (np.cos(rows), np.sin(rows), np.cos(blocks), np.sin(blocks))
    return tuple(t.astype(np.float32) for t in tables)


def rope_tile(tables, block):
    cos_r, sin_r, cos_b, sin_b = tables
    cb = cos_b[pl.ds(block + 1, 1), :]
    sb = sin_b[pl.ds(block + 1, 1), :]
    cr = cos_r[...]
    sr = sin_r[...]
    cosine = cr * cb - sr * sb
    sine = sr * cb + cr * sb
    first = lax.broadcasted_iota(jnp.int32, sine.shape, 1) % HD < HD // 2
    return cosine, jnp.where(first, -sine, sine), first


def turn(u, cosine, sine, first):
    other = jnp.where(first, pltpu.roll(u, LANES - HD // 2, 1), pltpu.roll(u, HD // 2, 1))
    return u * cosine + other * sine


def layer_stats(z):
    center = z - jnp.mean(z, axis=-1, keepdims=True)
    inv = lax.rsqrt(jnp.mean(center * center, axis=-1, keepdims=True) + norm_eps)
    return center * inv, inv


def layer_back(e, xhat, inv):
    return (e - jnp.mean(e, axis=-1, keepdims=True) - xhat * jnp.mean(e * xhat, axis=-1, keepdims=True)) * inv


def head_masks(shape):
    lane = lax.broadcasted_iota(jnp.int32, shape, 1)
    return lane < HD


def split_heads(c, low_head):
    zero = jnp.zeros_like(c)
    return jnp.concatenate([jnp.where(low_head, c, zero), jnp.where(low_head, zero, c)], axis=0)


def phase_norm(x_ref, gain_ref, normed_ref):
    def body(t, carry):
        r0 = pl.multiple_of(t * TILE, TILE)
        xhat, _ = layer_stats(x_ref[pl.ds(r0, TILE), :].astype(F32))
        normed_ref[pl.ds(r0, TILE), :] = (xhat * gain_ref[:1, :].astype(F32)).astype(BF16)
        return carry

    lax.fori_loop(0, x_ref.shape[0] // TILE, body, 0)


def phase_qkv(normed_ref, w_ref, tables, q_ref, k_ref, v_ref, block0, rows, which):
    width = normed_ref.shape[1]
    half = width // 2
    scaling = 1.0 / math.sqrt(HD)

    def body(t, carry):
        r0 = pl.multiple_of(t * rows, rows)
        out = nt(normed_ref[pl.ds(r0, rows), :], w_ref[which].reshape(3 * half, width))
        for s in range(rows // TILE):
            here = pl.ds(r0 + s * TILE, TILE)
            cosine, sine, first = rope_tile(tables, block0 + t * (rows // HALF) + s * (TILE // HALF))
            for part, ref in enumerate((q_ref, k_ref)):
                if part == 0:
                    turns = cosine * scaling, sine * scaling, first
                else:
                    turns = cosine, sine, first
                for j in range(half // LANES):
                    u = out[s * TILE : (s + 1) * TILE, part * half + j * LANES : part * half + (j + 1) * LANES]
                    ref[here, which * half + j * LANES : which * half + (j + 1) * LANES] = turn(u, *turns).astype(BF16)
        v_ref[pl.ds(r0, rows), which * half : (which + 1) * half] = out[:, 2 * half :].astype(BF16)
        return carry

    lax.fori_loop(0, normed_ref.shape[0] // rows, body, 0)


def phase_attend(q_ref, k_ref, v_ref, p_ref, ctx_ref, pos0, length, chunks, lo, hi):
    span = TILE + 2 * HALF

    def body(t, carry):
        r0 = pl.multiple_of(t * TILE, TILE)
        row = lax.broadcasted_iota(jnp.int32, (TILE, span), 0)
        col = lax.broadcasted_iota(jnp.int32, (TILE, span), 1)
        offset = col - row
        key_pos = pos0 + t * TILE - HALF + col
        allowed = (offset >= 0) & (offset <= 2 * HALF) & (key_pos >= 0) & ((key_pos < length) | (offset == HALF))
        bias = jnp.where(allowed, 0.0, masked_score).astype(F32)
        bias = jnp.concatenate([bias, bias], axis=0)
        low_head = head_masks((TILE, LANES))
        for j in chunks:
            lanes = slice(j * LANES, (j + 1) * LANES)
            q2 = split_heads(q_ref[pl.ds(r0 + HALF, TILE), lanes], low_head)
            scores = nt(q2, k_ref[pl.ds(r0, span), lanes]) + bias
            terms = jnp.exp(scores - jnp.max(scores, axis=-1, keepdims=True))
            probs = (terms * (1.0 / jnp.sum(terms, axis=-1, keepdims=True))).astype(BF16)
            p_ref[t, j] = probs
            out = nn(probs, v_ref[pl.ds(r0, span), lanes])
            ctx_ref[pl.ds(r0, TILE), lanes] = jnp.where(low_head, out[:TILE], out[TILE:]).astype(BF16)
        return carry

    lax.fori_loop(lo, hi, body, 0)


def phase_mlp(x_ref, cot_ref, ctx_ref, gain_ref, wo_ref, wi_ref, wm_ref, out_ref, gm_ref, gml_ref, go_ref, nm_ref, hid_ref, dgu_ref, dctx_ref, gg_ref, pos0, length, rows):
    ff = wm_ref.shape[0]
    half = hid_ref.shape[1]
    gg_ref[...] = jnp.zeros_like(gg_ref)

    def body(t, carry):
        r0 = pl.multiple_of(t * rows, rows)
        here = pl.ds(r0, rows)
        gain = gain_ref[...].astype(F32)
        middle = x_ref[here, :].astype(F32) + nn(ctx_ref[here, :], wo_ref[...])
        xhat, inv = layer_stats(middle)
        nm = (xhat * gain).astype(BF16)
        nm_ref[here, :] = nm
        gate = nt(nm, wi_ref[:ff, :])
        up = nt(nm, wi_ref[ff:, :])
        cdf = 0.5 + 0.5 * lax.erf(gate * math.sqrt(0.5))
        gelu = gate * cdf
        slope = cdf + gate * (jnp.exp(-0.5 * gate * gate) * (1.0 / math.sqrt(2.0 * math.pi)))
        hidden = (gelu * up).astype(BF16)
        hid_ref[here, :] = hidden[:, :half]
        valid = pos0 + r0 + lax.broadcasted_iota(jnp.int32, (rows, 1), 0) < length
        out_ref[here, :] = jnp.where(valid, middle + nn(hidden, wm_ref[...]), 0.0).astype(BF16)
        grad_out = jnp.where(valid, cot_ref[here, :].astype(F32), 0.0)
        grad_low = grad_out.astype(BF16)
        go_ref[here, :] = grad_low
        grad_hidden = nt(grad_low, wm_ref[...])
        grad_gate = (grad_hidden * up * slope).astype(BF16)
        grad_up = (grad_hidden * gelu).astype(BF16)
        dgu_ref[here, :half] = grad_gate[:, :half]
        dgu_ref[here, half:] = grad_up[:, :half]
        grad_nm = nn(grad_gate, wi_ref[:ff, :]) + nn(grad_up, wi_ref[ff:, :])
        gg_ref[...] += jnp.sum((grad_nm * xhat).reshape(rows // 8, 8, -1), axis=0)
        grad_middle = grad_out + layer_back(grad_nm * gain, xhat, inv)
        gm_ref[here, :] = grad_middle
        gm_low = grad_middle.astype(BF16)
        gml_ref[here, :] = gm_low
        dctx_ref[here, :] = nt(gm_low, wo_ref[...]).astype(BF16)
        return carry

    lax.fori_loop(0, ctx_ref.shape[0] // rows, body, 0)


def phase_attend_back(q_ref, k_ref, v_ref, p_ref, ctx_ref, dctx_ref, tables, dq_ref, dk_ref, dv_ref, block0):
    width = q_ref.shape[1]
    span = TILE + 2 * HALF
    scaling = 1.0 / math.sqrt(HD)
    dk_ref[...] = jnp.zeros_like(dk_ref)
    dv_ref[...] = jnp.zeros_like(dv_ref)

    def body(t, carry):
        r0 = pl.multiple_of(t * TILE, TILE)
        low_head = head_masks((TILE, LANES))
        cosine, sine, first = rope_tile(tables, block0 + 1 + t * (TILE // HALF))
        cosine, sine = cosine * scaling, sine * -scaling
        keys = pl.ds(r0, span)
        for j in range(width // LANES):
            lanes = slice(j * LANES, (j + 1) * LANES)
            probs = p_ref[t, j]
            kc = k_ref[keys, lanes]
            dc = dctx_ref[pl.ds(r0, TILE), lanes]
            row_term = dc.astype(F32) * ctx_ref[pl.ds(r0, TILE), lanes].astype(F32)
            row_low = jnp.sum(jnp.where(low_head, row_term, 0.0), axis=-1, keepdims=True)
            row_high = jnp.sum(jnp.where(low_head, 0.0, row_term), axis=-1, keepdims=True)
            row_term = jnp.concatenate([row_low, row_high], axis=0)
            dc2 = split_heads(dc, low_head)
            grad_probs = nt(dc2, v_ref[keys, lanes])
            grad_scores = (probs.astype(F32) * (grad_probs - row_term)).astype(BF16)
            dq2 = nn(grad_scores, kc)
            dq = jnp.where(low_head, dq2[:TILE], dq2[TILE:])
            dq_ref[pl.ds(r0, TILE), lanes] = turn(dq, cosine, sine, first).astype(BF16)
            q2 = split_heads(q_ref[pl.ds(r0 + HALF, TILE), lanes], low_head)
            dk_ref[keys, lanes] += tn(grad_scores, q2)
            dv_ref[keys, lanes] += tn(probs, dc2)
        return carry

    lax.fori_loop(0, dq_ref.shape[0] // TILE, body, 0)


def phase_input(x_ref, gm_ref, dq_ref, dk_ref, dv_ref, gain_ref, w_ref, tables, dqkv_ref, out_ref, gg_ref, block0, rows):
    width = x_ref.shape[1]
    half = width // 2
    gg_ref[...] = jnp.zeros_like(gg_ref)

    def body(t, carry):
        r0 = pl.multiple_of(t * rows, rows)
        here = pl.ds(r0, rows)
        gain = gain_ref[...].astype(F32)
        pieces = []
        for s in range(rows // TILE):
            cosine, sine, first = rope_tile(tables, block0 + 1 + t * (rows // HALF) + s * (TILE // HALF))
            sub = pl.ds(r0 + s * TILE, TILE)
            chunk = [turn(dk_ref[sub, j * LANES : (j + 1) * LANES], cosine, -sine, first).astype(BF16) for j in range(width // LANES)]
            pieces.append(jnp.concatenate(chunk, axis=1))
        dk = jnp.concatenate(pieces, axis=0)
        dq = dq_ref[here, :]
        dv = dv_ref[here, :].astype(BF16)
        own = jnp.concatenate([g[:, :half] for g in (dq, dk, dv)], axis=1)
        other = jnp.concatenate([g[:, half:] for g in (dq, dk, dv)], axis=1)
        dqkv_ref[here, :] = own
        grad_normed = nn(jnp.concatenate([own, other], axis=1), w_ref[...])
        xhat, inv = layer_stats(x_ref[here, :].astype(F32))
        gg_ref[...] += jnp.sum((grad_normed * xhat).reshape(rows // 8, 8, -1), axis=0)
        out_ref[here, :] = (gm_ref[here, :] + layer_back(grad_normed * gain, xhat, inv)).astype(BF16)
        return carry

    lax.fori_loop(0, x_ref.shape[0] // rows, body, 0)


def weight_grad(a_ref, b_ref, out_ref, columns):
    for c in range(0, a_ref.shape[1], columns):
        out_ref[c : c + columns, :] = tn(a_ref[:, c : c + columns], b_ref[...]).astype(out_ref.dtype)


def slot_of(at, of):
    return (of + 2 * (at // 2)) % 4


class Place:
    def __init__(self, n_shard):
        self.split = n_shard == 2
        self.x = lax.axis_index("shard")
        self.c = lax.axis_index("ctx")
        self.z = lax.axis_index("tp")
        self.k = self.c % 2
        self.y = self.c // 2
        self.up = (self.z + 1) % 4
        self.down = (self.z + 3) % 4
        self.mate = self.z + 1 - 2 * (self.z % 2)
        self.core = self.c + 1 - 2 * self.k
        self.across = (self.c + 2) % 4
        self.to_x = {"shard": 1 - self.x}
        self.to_up = {"tp": self.up}
        self.to_down = {"tp": self.down}
        self.to_mate = {"tp": self.mate}
        self.to_core = {"ctx": self.core}
        self.to_y = {"ctx": self.across}
        self.to_next = {"ctx": (self.c + 1) % 4}
        self.to_prev = {"ctx": (self.c + 3) % 4}

    def meet(self, partners):
        barrier = pltpu.get_barrier_semaphore()
        for device in partners:
            pl.semaphore_signal(barrier, inc=1, device_id=device, device_id_type=pl.DeviceIdType.MESH)
        pl.semaphore_wait(barrier, len(partners))


class Wires:
    def __init__(self, send, recv, base=0):
        self.send, self.recv, self.next, self.open = send, recv, base, []

    def go(self, src, dst, device):
        i = self.next
        self.next += 1
        copy = pltpu.make_async_remote_copy(
            src_ref=src, dst_ref=dst, send_sem=self.send.at[i], recv_sem=self.recv.at[i], device_id=device, device_id_type=pl.DeviceIdType.MESH
        )
        copy.start()
        self.open.append(copy)
        return copy

    def own(self, src, dst):
        i = self.next
        self.next += 1
        copy = pltpu.make_async_copy(src, dst, self.recv.at[i])
        copy.start()
        return copy

    def close(self):
        for copy in self.open:
            copy.wait_send()
        self.open = []


def landed(copies):
    for copy in copies:
        copy.wait_recv()


class Gather:
    def __init__(self, shard, full, which, wires, here):
        self.shard, self.full, self.which, self.wires, self.here = shard, full, which, wires, here
        rows = shard.shape[0] // 6
        self.mine = pl.ds(rows * here.c, rows)
        self.rest = pl.ds(rows * (4 + here.k), rows)
        self.theirs = pl.ds(rows * here.across, rows)
        other = (here.z + 2) % 4
        self.to = ([here.mate] if which != 1 else []) + ([other, other + 1 - 2 * (other % 2)] if which != 0 else [])
        self.base = 2 if which == 1 else 0

    def cols(self, x):
        cols = self.shard.shape[1]
        return pl.ds(pl.multiple_of(x * cols, LANES), cols) if self.here.split else pl.ds(0, cols)

    def begin(self):
        h, go = self.here, self.wires.go
        cols = self.cols(h.x)
        self.kept, self.spread = [], []
        for rows in (self.rest, self.mine):
            src = self.shard.at[rows, :]
            for to in self.to:
                self.spread.append(go(src, self.full.at[slot_of(to, h.z) - self.base, rows, cols], {"tp": to}))
            if self.which != 1:
                self.kept.append(self.wires.own(src, self.full.at[slot_of(h.z, h.z), rows, cols]))

    def cross(self):
        landed(self.spread)
        for copy in self.kept:
            copy.wait()
        self.crossed = []
        if self.here.split:
            cols = self.cols(self.here.x)
            for rows in (self.rest, self.mine):
                block = self.full.at[:, rows, cols]
                self.crossed.append(self.wires.go(block, block, self.here.to_x))

    def share(self):
        h, go = self.here, self.wires.go
        landed(self.crossed)
        mine, rest = self.full.at[:, self.mine, :], self.full.at[:, self.rest, :]
        self.level = go(mine, mine, h.to_y)
        self.pooled = [go(rest, rest, h.to_core), go(mine, mine, h.to_core)]

    def relay(self):
        landed([self.level])
        theirs = self.full.at[:, self.theirs, :]
        self.pooled.append(self.wires.go(theirs, theirs, self.here.to_core))

    def end(self):
        landed(self.pooled)


class Reduce:
    def __init__(self, grad, out, bufs, wires, here, x_first):
        self.grad, self.out, self.wires, self.here = grad, out, wires, here
        self.a, self.b, self.d, self.e, self.s1, self.s2, self.s3 = bufs
        self.x_first = x_first and here.split
        rows = grad.shape[2] // 2
        self.keep = pl.ds(rows * here.k, rows)
        self.give = pl.ds(rows * (1 - here.k), rows)
        self.zs = here.z % 2

    @staticmethod
    def scratch(shape, n_shard, x_first):
        k, two, rows, width = shape
        split = n_shard == 2
        cols = width // n_shard if split else width
        half = rows // 2
        if split and x_first:
            middle = (k, two, half, cols)
        else:
            middle = (k, half, width)
        last = (k, half, cols)
        shapes = [(k, two, half, width), middle, last, last, (k, two, half, width), middle, last]
        return [pltpu.VMEM(s, BF16) for s in shapes]

    def cols(self, x):
        cols = self.out.shape[2]
        return pl.ds(pl.multiple_of(x * cols, LANES), cols)

    def begin(self):
        self.copy = self.wires.go(self.grad.at[:, :, self.give, :], self.a, self.here.to_core)

    def first(self):
        h = self.here
        landed([self.copy])
        self.s1[...] = (self.grad[:, :, self.keep, :].astype(F32) + self.a[...].astype(F32)).astype(BF16)
        if self.x_first:
            self.copy = self.wires.go(self.s1.at[:, :, :, self.cols(1 - h.x)], self.b, h.to_x)
        else:
            self.copy = self.wires.go(self.s1.at[:, 1 - self.zs, :, :], self.b, h.to_mate)

    def second(self):
        h = self.here
        landed([self.copy])
        if self.x_first:
            own = self.s1[:, :, :, self.cols(h.x)]
        else:
            own = self.s1[:, self.zs, :, :]
        total = (own.astype(F32) + self.b[...].astype(F32)).astype(BF16)
        if not h.split:
            self.s3[...] = total
            self.copy = None
            return
        self.s2[...] = total
        if self.x_first:
            self.copy = self.wires.go(self.s2.at[:, 1 - self.zs, :, :], self.d, h.to_mate)
        else:
            self.copy = self.wires.go(self.s2.at[:, :, self.cols(1 - h.x)], self.d, h.to_x)

    def third(self):
        h = self.here
        if self.copy is not None:
            landed([self.copy])
            if self.x_first:
                own = self.s2[:, self.zs, :, :]
            else:
                own = self.s2[:, :, self.cols(h.x)]
            self.s3[...] = (own.astype(F32) + self.d[...].astype(F32)).astype(BF16)
        self.copy = self.wires.go(self.s3, self.e, h.to_y)

    def fourth(self):
        landed([self.copy])
        self.out[:, self.keep, :] = (self.s3[...].astype(F32) + self.e[...].astype(F32)).astype(BF16)
        done = self.out.at[:, self.keep, :]
        self.copy = self.wires.go(done, done, self.here.to_core)

    def end(self):
        landed([self.copy])


REDUCE_COPIES = 5


def wavefront(jobs, names):
    for step in range(len(jobs) + len(names) - 1):
        for i, job in enumerate(jobs):
            if 0 <= step - i < len(names):
                getattr(job, names[step - i])()


REDUCE_STAGES = ("begin", "first", "second", "third", "fourth", "end")


def attend_kernel(n_shard, s_ref, x_ref, gains_ref, *refs):
    shards, tables, refs = refs[:4], refs[4:8], refs[8:]
    wqkv, wo, wi, wm, gains, normed, q, k, v, p, ctx, ext, send, recv = refs
    h = Place(n_shard)
    near = [{"tp": (h.z + i) % 4} for i in (1, 2, 3)] + [{"ctx": (h.c + i) % 4} for i in (1, 2, 3)]
    if h.split:
        near.append(h.to_x)
    h.meet(near)
    wires = Wires(send, recv)
    local = x_ref.shape[2]
    seq = x_ref.at[0, h.z % 2]
    kept = [wires.own(seq, ext.at[pl.ds(HALF, local), :])]
    rims = [
        wires.go(seq.at[pl.ds(0, HALF), :], ext.at[pl.ds(HALF + local, HALF), :], h.to_prev),
        wires.go(seq.at[pl.ds(local - HALF, HALF), :], ext.at[pl.ds(0, HALF), :], h.to_next),
    ]
    if h.split:
        cols = gains_ref.shape[1]
        mine = gains.at[:, pl.ds(pl.multiple_of(h.x * cols, LANES), cols)]
        kept.append(wires.own(gains_ref, mine))
        rims.append(wires.go(gains_ref, mine, h.to_x))
    else:
        kept.append(wires.own(gains_ref, gains))
    near_jobs = [Gather(shards[0].at[i], wqkv.at[0, i], 0, wires, h) for i in range(3)]
    far_jobs = [Gather(shards[0].at[i], wqkv.at[1, i], 1, wires, h) for i in range(3)]
    late = [(1, wo, 0), (2, wi, 0), (2, wi, 1), (3, wm, 0)]
    late = [Gather(shards[i].at[part], full.at[part], None, wires, h) for i, full, part in late]
    run(near_jobs, "begin")
    run(far_jobs, "begin")
    run(late, "begin")
    for copy in kept:
        copy.wait()
    landed(rims)
    phase_norm(ext, gains, normed)
    run(near_jobs, "cross")
    run(near_jobs, "share")
    run(near_jobs, "relay")
    run(near_jobs, "end")
    run(far_jobs, "cross")
    qkv = functools.partial(phase_qkv, normed, wqkv, tables, q, k, v, s_ref[2], 384)
    attend = functools.partial(phase_attend, q, k, v, p, ctx, s_ref[1], s_ref[0])
    tiles = local // TILE
    half = p.shape[1] // 2
    qkv(0)
    run(far_jobs, "share")
    run(late[:1], "cross")
    attend(range(half), 0, tiles // 2)
    run(far_jobs, "relay")
    run(late[:1], "share")
    run(late[1:2], "cross")
    attend(range(half), tiles // 2, tiles)
    run(far_jobs, "end")
    run(late[:1], "relay")
    run(late[1:2], "share")
    run(late[2:3], "cross")
    qkv(1)
    run(late[:1], "end")
    run(late[1:2], "relay")
    run(late[2:3], "share")
    run(late[3:4], "cross")
    attend(range(half, 2 * half), 0, tiles // 2)
    run(late[2:3], "relay")
    run(late[3:4], "share")
    attend(range(half, 2 * half), tiles // 2, tiles)
    run(late[3:4], "relay")
    run(late[1:4], "end")
    wires.close()


def run(jobs, stage):
    for job in jobs:
        getattr(job, stage)()


def reduce_kernel(n_shard, n, *refs):
    grads, outs, (send, recv), bufs = refs[:n], refs[n : 2 * n], refs[2 * n : 2 * n + 2], refs[2 * n + 2 :]
    h = Place(n_shard)
    near = [h.to_mate, h.to_core, h.to_y]
    if h.split:
        near.append(h.to_x)
    h.meet(near)
    wires = Wires(send, recv)
    jobs = [Reduce(g, o, bufs[7 * i : 7 * i + 7], wires, h, i % 2 == 0) for i, (g, o) in enumerate(zip(grads, outs))]
    wavefront(jobs, REDUCE_STAGES)
    wires.close()


def call(kernel, outs, *args, scratch=(), name=None):
    vmem = pl.BlockSpec(memory_space=pltpu.VMEM)
    smem = pl.BlockSpec(memory_space=pltpu.SMEM)
    return pl.pallas_call(
        kernel,
        out_shape=[jax.ShapeDtypeStruct(s, d) for s, d in outs],
        in_specs=[smem if a.dtype == jnp.int32 else vmem for a in args],
        out_specs=[vmem] * len(outs),
        scratch_shapes=list(scratch),
        compiler_params=pltpu.CompilerParams(vmem_limit_bytes=VMEM_LIMIT),
        name=name,
    )(*args)


def on_device(inputs, lengths, attn_gain, mlp_gain, qkv_weight, attn_weight, mlp_in_weight, mlp_out_weight, cotangent):
    n_tp = lax.axis_size("tp")
    n_ctx = lax.axis_size("ctx")
    tp = lax.axis_index("tp")
    ctx = lax.axis_index("ctx")
    seqs, local = inputs.shape[1], inputs.shape[2]
    width = inputs.shape[3]
    group = n_tp // 2
    mine = tp % seqs
    pair = tp // 2
    tables = tuple(jnp.asarray(t) for t in rope_constants(local * n_ctx))

    n_shard = lax.axis_size("shard")
    shards = [jnp.transpose(qkv_weight, (1, 2, 0)), attn_weight[None], jnp.transpose(mlp_in_weight, (1, 2, 0)), mlp_out_weight[None]]
    gains = jnp.pad(jnp.stack([attn_gain, mlp_gain]), ((0, 14), (0, 0)))
    if n_shard != 2:
        shards = [lax.all_gather(s, "shard", axis=2, tiled=True) for s in shards]
        gains = lax.all_gather(gains, "shard", axis=1, tiled=True)
    hbm = pl.BlockSpec(memory_space=pl.ANY)
    vmem = pl.BlockSpec(memory_space=pltpu.VMEM)
    smem = pl.BlockSpec(memory_space=pltpu.SMEM)
    length = lax.dynamic_index_in_dim(lengths[0], mine, 0, keepdims=True)
    block0 = ctx * (local // HALF) - 1
    pos0 = ctx * local
    scalars = jnp.stack([length[0], pos0.astype(jnp.int32), block0.astype(jnp.int32)])
    ext = local + 2 * HALF
    tiles = local // TILE
    chunks = width // LANES
    span = TILE + 2 * HALF
    wide = ((ext, width), BF16)
    tall = ((local, width), BF16)
    outs = [
        ((2, 3, 2, shards[0].shape[1], width), BF16),
        *(((s.shape[0], n_tp, s.shape[1], width), BF16) for s in shards[1:]),
        ((16, width), BF16),
        wide, wide, wide, wide,
        ((tiles, chunks, 2 * TILE, span), BF16),
        tall,
    ]
    copies = 124
    wqkv, wo, wi, wm, gains, normed, q, k, v, probs, context = pl.pallas_call(
        functools.partial(attend_kernel, n_shard),
        out_shape=[jax.ShapeDtypeStruct(*o) for o in outs],
        in_specs=[smem] + [hbm] * 6 + [vmem] * 4,
        out_specs=[vmem] + [hbm] * 3 + [vmem] * 7,
        scratch_shapes=[pltpu.VMEM((ext, width), BF16), pltpu.SemaphoreType.DMA((copies,)), pltpu.SemaphoreType.DMA((copies,))],
        compiler_params=pltpu.CompilerParams(collective_id=0, has_side_effects=True, vmem_limit_bytes=VMEM_LIMIT),
        name="attend",
    )(scalars, inputs, gains, *shards, *tables)
    wqkv, wo, wi, wm = (f.reshape(-1, width) for f in (wqkv, wo, wi, wm))
    gain1, gain2 = gains[:1], gains[1:2]
    x_own = lax.dynamic_index_in_dim(inputs[0], mine, 0, keepdims=False)
    cot = lax.dynamic_index_in_dim(cotangent[0], mine, 0, keepdims=False)
    up = [(i, i + 1) for i in range(n_ctx - 1)]
    down = [(i + 1, i) for i in range(n_ctx - 1)]
    ff = wm.shape[0]
    ff_half = ff // 2

    def kernel_d(s_ref, x_ref, cot_ref, ctx_ref, g_ref, wo_ref, wi_ref, wm_ref, out, gm, gml, dctx, gg, dwm, dwi, go, nm, hid, dgu):
        phase_mlp(x_ref, cot_ref, ctx_ref, g_ref, wo_ref, wi_ref, wm_ref, out, gm, gml, go, nm, hid, dgu, dctx, gg, s_ref[1], s_ref[0], 256)
        weight_grad(hid, go, dwm, 192)
        weight_grad(dgu, nm, dwi, 384)

    layer_out, gm, gml, dctx, gain2_part, dwm, dwi = call(
        kernel_d,
        [tall, ((local, width), F32), tall, tall, ((8, width), F32), ((ff_half, width), BF16), ((2 * ff_half, width), BF16)],
        scalars, x_own, cot, context, gain2, wo, wi, wm,
        scratch=[pltpu.VMEM((local, width), BF16), pltpu.VMEM((local, width), BF16), pltpu.VMEM((local, ff_half), BF16), pltpu.VMEM((local, 2 * ff_half), BF16)],
        name="feed_forward",
    )
    width_half = width // 2

    def kernel_e(s_ref, q_ref, k_ref, v_ref, p_ref, ctx_ref, dctx_ref, gml_ref, c0, s0, c1, s1, dq, dk, dv, dwo):
        phase_attend_back(q_ref, k_ref, v_ref, p_ref, ctx_ref, dctx_ref, (c0, s0, c1, s1), dq, dk, dv, s_ref[2])
        for c in range(0, width_half, LANES):
            dwo[c : c + LANES, :] = tn(ctx_ref[:, c : c + LANES], gml_ref[...]).astype(BF16)

    dq, dk, dv, dwo = call(
        kernel_e,
        [tall, ((ext, width), F32), ((ext, width), F32), ((width_half, width), BF16)],
        scalars, q, k, v, probs, context, dctx, gml, *tables,
        name="attend_back",
    )
    rims = jnp.stack([dk, dv])
    to_lower = lax.ppermute(rims[:, :HALF], "ctx", down)
    to_upper = lax.ppermute(rims[:, ext - HALF :], "ctx", up)
    rims = rims[:, HALF : HALF + local]
    rims = jnp.concatenate([rims[:, :HALF] + to_upper, rims[:, HALF : local - HALF], rims[:, local - HALF :] + to_lower], axis=1)

    def kernel_g(s_ref, x_ref, n_ref, gm_ref, dq_ref, dk_ref, dv_ref, g_ref, w_ref, c0, s0, c1, s1, out, gg, dw, dqkv):
        phase_input(x_ref, gm_ref, dq_ref, dk_ref, dv_ref, g_ref, w_ref, (c0, s0, c1, s1), dqkv, out, gg, s_ref[2], 256)
        weight_grad(dqkv, n_ref, dw, 384)

    input_grad, gain1_part, dwqkv = call(
        kernel_g,
        [tall, ((8, width), F32), ((3 * width_half, width), BF16)],
        scalars, x_own, normed[HALF : HALF + local], gm, dq, rims[0], rims[1], gain1, wqkv, *tables,
        scratch=[pltpu.VMEM((local, 3 * width_half), BF16)],
        name="input_back",
    )

    def both(own):
        other = lax.ppermute(own, "tp", [(i, i ^ 1) for i in range(n_tp)])
        low = jnp.where(mine == 0, own, other)
        high = jnp.where(mine == 0, other, own)
        return jnp.stack([low, high])[None]

    gain_rows = jnp.concatenate([gain1_part, gain2_part]).astype(BF16)
    gain_rows = jnp.broadcast_to(gain_rows[None, None], (1, 2, 16, width))
    grads = [g.reshape(k, 2, -1, width) for g, k in ((dwqkv, 3), (dwi, 2), (dwo, 1), (dwm, 1))]
    grads.append(jnp.concatenate([gain_rows, gain_rows], axis=2))
    cols = width // n_shard if n_shard == 2 else width
    sends = REDUCE_COPIES * len(grads)
    owned = pl.pallas_call(
        functools.partial(reduce_kernel, n_shard, len(grads)),
        out_shape=[jax.ShapeDtypeStruct((g.shape[0], g.shape[2], cols), BF16) for g in grads],
        in_specs=[vmem] * len(grads),
        out_specs=[vmem] * len(grads),
        scratch_shapes=[pltpu.SemaphoreType.DMA((sends,)), pltpu.SemaphoreType.DMA((sends,))]
        + [b for i, g in enumerate(grads) for b in Reduce.scratch(g.shape, n_shard, i % 2 == 0)],
        compiler_params=pltpu.CompilerParams(collective_id=1, has_side_effects=True, vmem_limit_bytes=VMEM_LIMIT),
        name="reduce",
    )(*grads)
    owned = [g.astype(F32) for g in owned]
    if n_shard != 2:
        owned = [lax.psum_scatter(g, "shard", scatter_dimension=2, tiled=True) for g in owned]
    qkv_grad = jnp.transpose(owned[0], (2, 0, 1))
    mlp_in_grad = jnp.transpose(owned[1], (2, 0, 1))
    attn_grad, mlp_out_grad = owned[2][0], owned[3][0]
    share = owned[4].shape[2] // n_tp
    gains = lax.dynamic_slice_in_dim(owned[4][0, :16], tp * share, share, axis=1)
    gains = jnp.sum(gains.reshape(2, 8, share), axis=1)
    return (both(layer_out), both(input_grad), qkv_grad, attn_grad, mlp_in_grad, mlp_out_grad, gains[0], gains[1])


def solution(mesh):
    in_specs = (
        P("shard", None, "ctx", None),
        P("shard", None),
        P("shard"),
        P("shard"),
        P("shard", None, "tp"),
        P("tp", "shard"),
        P("shard", None, "tp"),
        P("tp", "shard"),
        P("shard", None, "ctx", None),
    )
    out_specs = (
        P("shard", None, "ctx", None),
        P("shard", None, "ctx", None),
        P("shard", None, "tp"),
        P("tp", "shard"),
        P("shard", None, "tp"),
        P("tp", "shard"),
        P(("shard", "tp")),
        P(("shard", "tp")),
    )
    return jax.shard_map(on_device, mesh=mesh, in_specs=in_specs, out_specs=out_specs, check_vma=False)
```

```python
import functools
import math

import numpy as np

import jax
import jax.numpy as jnp
from jax import lax
from jax.experimental import pallas as pl
from jax.experimental.pallas import tpu as pltpu
from jax.sharding import PartitionSpec as P

HD = 64
HALF = 64
TILE = 128
LANES = 128
norm_eps = 1e-05
rope_base = 10000.0
masked_score = -1e30
F32 = jnp.float32
BF16 = jnp.bfloat16
VMEM_LIMIT = 60 * 1024 * 1024


def nt(a, b):
    return lax.dot_general(a, b, (((1,), (1,)), ((), ())), preferred_element_type=F32)


def nn(a, b):
    return lax.dot_general(a, b, (((1,), (0,)), ((), ())), preferred_element_type=F32)


def tn(a, b):
    return lax.dot_general(a, b, (((0,), (0,)), ((), ())), preferred_element_type=F32)


def rope_constants(seq):
    w = rope_base ** (-np.arange(0, HD, 2) / HD)
    w = np.tile(w, 2 * LANES // HD)
    rows = np.arange(TILE)[:, None] * w
    blocks = (np.arange(seq // HALF + 4)[:, None] - 1) * HALF * w
    tables = (np.cos(rows), np.sin(rows), np.cos(blocks), np.sin(blocks))
    return tuple(t.astype(np.float32) for t in tables)


def rope_tile(tables, block):
    cos_r, sin_r, cos_b, sin_b = tables
    cb = cos_b[pl.ds(block + 1, 1), :]
    sb = sin_b[pl.ds(block + 1, 1), :]
    cr = cos_r[...]
    sr = sin_r[...]
    cosine = cr * cb - sr * sb
    sine = sr * cb + cr * sb
    first = lax.broadcasted_iota(jnp.int32, sine.shape, 1) % HD < HD // 2
    return cosine, jnp.where(first, -sine, sine), first


def turn(u, cosine, sine, first):
    other = jnp.where(first, pltpu.roll(u, LANES - HD // 2, 1), pltpu.roll(u, HD // 2, 1))
    return u * cosine + other * sine


def layer_stats(z):
    center = z - jnp.mean(z, axis=-1, keepdims=True)
    inv = lax.rsqrt(jnp.mean(center * center, axis=-1, keepdims=True) + norm_eps)
    return center * inv, inv


def layer_back(e, xhat, inv):
    return (e - jnp.mean(e, axis=-1, keepdims=True) - xhat * jnp.mean(e * xhat, axis=-1, keepdims=True)) * inv


def head_masks(shape):
    lane = lax.broadcasted_iota(jnp.int32, shape, 1)
    return lane < HD


def split_heads(c, low_head):
    zero = jnp.zeros_like(c)
    return jnp.concatenate([jnp.where(low_head, c, zero), jnp.where(low_head, zero, c)], axis=0)


def phase_norm(x_ref, gain_ref, normed_ref):
    def body(t, carry):
        r0 = pl.multiple_of(t * TILE, TILE)
        xhat, _ = layer_stats(x_ref[pl.ds(r0, TILE), :].astype(F32))
        normed_ref[pl.ds(r0, TILE), :] = (xhat * gain_ref[:1, :].astype(F32)).astype(BF16)
        return carry

    lax.fori_loop(0, x_ref.shape[0] // TILE, body, 0)


def phase_qkv(normed_ref, w_ref, tables, q_ref, k_ref, v_ref, block0, rows, which):
    width = normed_ref.shape[1]
    half = width // 2
    scaling = 1.0 / math.sqrt(HD)

    def body(t, carry):
        r0 = pl.multiple_of(t * rows, rows)
        out = nt(normed_ref[pl.ds(r0, rows), :], w_ref[which].reshape(3 * half, width))
        for s in range(rows // TILE):
            here = pl.ds(r0 + s * TILE, TILE)
            cosine, sine, first = rope_tile(tables, block0 + t * (rows // HALF) + s * (TILE // HALF))
            for part, ref in enumerate((q_ref, k_ref)):
                if part == 0:
                    turns = cosine * scaling, sine * scaling, first
                else:
                    turns = cosine, sine, first
                for j in range(half // LANES):
                    u = out[s * TILE : (s + 1) * TILE, part * half + j * LANES : part * half + (j + 1) * LANES]
                    ref[here, which * half + j * LANES : which * half + (j + 1) * LANES] = turn(u, *turns).astype(BF16)
        v_ref[pl.ds(r0, rows), which * half : (which + 1) * half] = out[:, 2 * half :].astype(BF16)
        return carry

    lax.fori_loop(0, normed_ref.shape[0] // rows, body, 0)


def phase_attend(q_ref, k_ref, v_ref, p_ref, ctx_ref, pos0, length, chunks, lo, hi):
    span = TILE + 2 * HALF

    def body(t, carry):
        r0 = pl.multiple_of(t * TILE, TILE)
        row = lax.broadcasted_iota(jnp.int32, (TILE, span), 0)
        col = lax.broadcasted_iota(jnp.int32, (TILE, span), 1)
        offset = col - row
        key_pos = pos0 + t * TILE - HALF + col
        allowed = (offset >= 0) & (offset <= 2 * HALF) & (key_pos >= 0) & ((key_pos < length) | (offset == HALF))
        bias = jnp.where(allowed, 0.0, masked_score).astype(F32)
        bias = jnp.concatenate([bias, bias], axis=0)
        low_head = head_masks((TILE, LANES))
        for j in chunks:
            lanes = slice(j * LANES, (j + 1) * LANES)
            q2 = split_heads(q_ref[pl.ds(r0 + HALF, TILE), lanes], low_head)
            scores = nt(q2, k_ref[pl.ds(r0, span), lanes]) + bias
            terms = jnp.exp(scores - jnp.max(scores, axis=-1, keepdims=True))
            probs = (terms * (1.0 / jnp.sum(terms, axis=-1, keepdims=True))).astype(BF16)
            p_ref[t, j] = probs
            out = nn(probs, v_ref[pl.ds(r0, span), lanes])
            ctx_ref[pl.ds(r0, TILE), lanes] = jnp.where(low_head, out[:TILE], out[TILE:]).astype(BF16)
        return carry

    lax.fori_loop(lo, hi, body, 0)


def phase_mlp(x_ref, cot_ref, ctx_ref, gain_ref, wo_ref, wi_ref, wm_ref, out_ref, gml_ref, go_ref, nm_ref, hid_ref, dgu_ref, dctx_ref, gg_ref, pos0, length, rows):
    ff = wm_ref.shape[0]
    half = hid_ref.shape[1]
    gg_ref[...] = jnp.zeros_like(gg_ref)

    def body(t, carry):
        r0 = pl.multiple_of(t * rows, rows)
        here = pl.ds(r0, rows)
        gain = gain_ref[...].astype(F32)
        middle = x_ref[here, :].astype(F32) + nn(ctx_ref[here, :], wo_ref[...])
        xhat, inv = layer_stats(middle)
        nm = (xhat * gain).astype(BF16)
        nm_ref[here, :] = nm
        gate = nt(nm, wi_ref[:ff, :])
        up = nt(nm, wi_ref[ff:, :])
        cdf = 0.5 + 0.5 * lax.erf(gate * math.sqrt(0.5))
        gelu = gate * cdf
        slope = cdf + gate * (jnp.exp(-0.5 * gate * gate) * (1.0 / math.sqrt(2.0 * math.pi)))
        hidden = (gelu * up).astype(BF16)
        hid_ref[here, :] = hidden[:, :half]
        valid = pos0 + r0 + lax.broadcasted_iota(jnp.int32, (rows, 1), 0) < length
        out_ref[here, :] = jnp.where(valid, middle + nn(hidden, wm_ref[...]), 0.0).astype(BF16)
        grad_out = jnp.where(valid, cot_ref[here, :].astype(F32), 0.0)
        grad_low = grad_out.astype(BF16)
        go_ref[here, :] = grad_low
        grad_hidden = nt(grad_low, wm_ref[...])
        grad_gate = (grad_hidden * up * slope).astype(BF16)
        grad_up = (grad_hidden * gelu).astype(BF16)
        dgu_ref[here, :half] = grad_gate[:, :half]
        dgu_ref[here, half:] = grad_up[:, :half]
        grad_nm = nn(grad_gate, wi_ref[:ff, :]) + nn(grad_up, wi_ref[ff:, :])
        gg_ref[...] += jnp.sum((grad_nm * xhat).reshape(rows // 8, 8, -1), axis=0)
        grad_middle = grad_out + layer_back(grad_nm * gain, xhat, inv)
        gm_low = grad_middle.astype(BF16)
        gml_ref[here, :] = gm_low
        dctx_ref[here, :] = nt(gm_low, wo_ref[...]).astype(BF16)
        return carry

    lax.fori_loop(0, ctx_ref.shape[0] // rows, body, 0)


def phase_attend_back(q_ref, k_ref, v_ref, p_ref, ctx_ref, dctx_ref, tables, dqkv_ref, dk_ref, dv_ref, block0, lo, hi):
    width = q_ref.shape[1]
    half = width // 2
    span = TILE + 2 * HALF
    scaling = 1.0 / math.sqrt(HD)

    def body(t, carry):
        r0 = pl.multiple_of(t * TILE, TILE)
        low_head = head_masks((TILE, LANES))
        cosine, sine, first = rope_tile(tables, block0 + 1 + t * (TILE // HALF))
        cosine, sine = cosine * scaling, sine * -scaling
        keys = pl.ds(r0, span)
        for j in range(width // LANES):
            lanes = slice(j * LANES, (j + 1) * LANES)
            probs = p_ref[t, j]
            kc = k_ref[keys, lanes]
            dc = dctx_ref[pl.ds(r0, TILE), lanes]
            row_term = dc.astype(F32) * ctx_ref[pl.ds(r0, TILE), lanes].astype(F32)
            row_low = jnp.sum(jnp.where(low_head, row_term, 0.0), axis=-1, keepdims=True)
            row_high = jnp.sum(jnp.where(low_head, 0.0, row_term), axis=-1, keepdims=True)
            row_term = jnp.concatenate([row_low, row_high], axis=0)
            dc2 = split_heads(dc, low_head)
            grad_probs = nt(dc2, v_ref[keys, lanes])
            grad_scores = (probs.astype(F32) * (grad_probs - row_term)).astype(BF16)
            dq2 = nn(grad_scores, kc)
            dq = jnp.where(low_head, dq2[:TILE], dq2[TILE:])
            at = 3 * half * (j * LANES // half) + j * LANES % half
            dqkv_ref[pl.ds(r0, TILE), at : at + LANES] = turn(dq, cosine, sine, first).astype(BF16)
            q2 = split_heads(q_ref[pl.ds(r0 + HALF, TILE), lanes], low_head)
            dk_ref[keys, lanes] += tn(grad_scores, q2)
            dv_ref[keys, lanes] += tn(probs, dc2)
        return carry

    lax.fori_loop(lo, hi, body, 0)


def phase_pack(dk_ref, dv_ref, tables, dqkv_ref, block0, lo, hi):
    width = dk_ref.shape[1]
    half = width // 2

    def body(t, carry):
        r0 = pl.multiple_of(t * TILE, TILE)
        cosine, sine, first = rope_tile(tables, block0 + 1 + t * (TILE // HALF))
        ext = pl.ds(r0 + HALF, TILE)
        for j in range(width // LANES):
            lanes = slice(j * LANES, (j + 1) * LANES)
            at = 3 * half * (j * LANES // half) + j * LANES % half
            dqkv_ref[pl.ds(r0, TILE), at + half : at + half + LANES] = turn(dk_ref[ext, lanes], cosine, -sine, first).astype(BF16)
            dqkv_ref[pl.ds(r0, TILE), at + 2 * half : at + 2 * half + LANES] = dv_ref[ext, lanes].astype(BF16)
        return carry

    lax.fori_loop(lo, hi, body, 0)


def phase_input(x_ref, gm_ref, gain_ref, w_ref, dqkv_ref, out_ref, gg_ref, r0, rows):
    here = pl.ds(r0, rows)
    gain = gain_ref[:1, :].astype(F32)
    grad_normed = nn(dqkv_ref[here, :], w_ref[...])
    xhat, inv = layer_stats(x_ref[here, :].astype(F32))
    gg_ref[...] += jnp.sum((grad_normed * xhat).reshape(rows // 8, 8, -1), axis=0)
    out_ref[here, :] = (gm_ref[here, :].astype(F32) + layer_back(grad_normed * gain, xhat, inv)).astype(BF16)


def weight_grad(a_ref, b, out_ref, columns, at=0, count=None):
    for c in range(0, a_ref.shape[1] if count is None else count, columns):
        out_ref[c : c + columns, :] = tn(a_ref[:, at + c : at + c + columns], b).astype(out_ref.dtype)


def slot_of(at, of):
    return (of + 2 * (at // 2)) % 4


class Place:
    def __init__(self, n_shard):
        self.split = n_shard == 2
        self.x = lax.axis_index("shard")
        self.c = lax.axis_index("ctx")
        self.z = lax.axis_index("tp")
        self.k = self.c % 2
        self.y = self.c // 2
        self.up = (self.z + 1) % 4
        self.down = (self.z + 3) % 4
        self.mate = self.z + 1 - 2 * (self.z % 2)
        self.core = self.c + 1 - 2 * self.k
        self.across = (self.c + 2) % 4
        self.to_x = {"shard": 1 - self.x}
        self.to_up = {"tp": self.up}
        self.to_down = {"tp": self.down}
        self.to_mate = {"tp": self.mate}
        self.to_core = {"ctx": self.core}
        self.to_y = {"ctx": self.across}
        self.to_next = {"ctx": (self.c + 1) % 4}
        self.to_prev = {"ctx": (self.c + 3) % 4}

    def meet(self, partners):
        barrier = pltpu.get_barrier_semaphore()
        for device in partners:
            pl.semaphore_signal(barrier, inc=1, device_id=device, device_id_type=pl.DeviceIdType.MESH)
        pl.semaphore_wait(barrier, len(partners))


class Wires:
    def __init__(self, send, recv, base=0):
        self.send, self.recv, self.next, self.open = send, recv, base, []

    def go(self, src, dst, device):
        i = self.next
        self.next += 1
        copy = pltpu.make_async_remote_copy(
            src_ref=src, dst_ref=dst, send_sem=self.send.at[i], recv_sem=self.recv.at[i], device_id=device, device_id_type=pl.DeviceIdType.MESH
        )
        copy.start()
        self.open.append(copy)
        return copy

    def own(self, src, dst):
        i = self.next
        self.next += 1
        copy = pltpu.make_async_copy(src, dst, self.recv.at[i])
        copy.start()
        return copy

    def close(self):
        for copy in self.open:
            copy.wait_send()
        self.open = []


def landed(copies):
    for copy in copies:
        copy.wait_recv()


class Gather:
    def __init__(self, shard, full, which, wires, here):
        self.shard, self.full, self.which, self.wires, self.here = shard, full, which, wires, here
        rows = shard.shape[0] // 6
        self.mine = pl.ds(rows * here.c, rows)
        self.rest = pl.ds(rows * (4 + here.k), rows)
        self.theirs = pl.ds(rows * here.across, rows)
        other = (here.z + 2) % 4
        self.to = ([here.mate] if which != 1 else []) + ([other, other + 1 - 2 * (other % 2)] if which != 0 else [])
        self.base = 2 if which == 1 else 0

    def cols(self, x):
        cols = self.shard.shape[1]
        return pl.ds(pl.multiple_of(x * cols, LANES), cols) if self.here.split else pl.ds(0, cols)

    def begin(self):
        h, go = self.here, self.wires.go
        cols = self.cols(h.x)
        self.kept, self.spread = [], []
        for rows in (self.rest, self.mine):
            src = self.shard.at[rows, :]
            for to in self.to:
                self.spread.append(go(src, self.full.at[slot_of(to, h.z) - self.base, rows, cols], {"tp": to}))
            if self.which != 1:
                self.kept.append(self.wires.own(src, self.full.at[slot_of(h.z, h.z), rows, cols]))

    def cross(self):
        landed(self.spread)
        for copy in self.kept:
            copy.wait()
        self.crossed = []
        if self.here.split:
            cols = self.cols(self.here.x)
            for rows in (self.rest, self.mine):
                block = self.full.at[:, rows, cols]
                self.crossed.append(self.wires.go(block, block, self.here.to_x))

    def share(self):
        h, go = self.here, self.wires.go
        landed(self.crossed)
        mine, rest = self.full.at[:, self.mine, :], self.full.at[:, self.rest, :]
        self.level = go(mine, mine, h.to_y)
        self.pooled = [go(rest, rest, h.to_core), go(mine, mine, h.to_core)]

    def relay(self):
        landed([self.level])
        theirs = self.full.at[:, self.theirs, :]
        self.pooled.append(self.wires.go(theirs, theirs, self.here.to_core))

    def end(self):
        landed(self.pooled)


class Reduce:
    def __init__(self, grad, out, bufs, wires, here, x_first):
        self.grad, self.out, self.wires, self.here = grad, out, wires, here
        self.a, self.b, self.d, self.e, self.s1, self.s2, self.s3 = bufs
        self.x_first = x_first and here.split
        rows = grad.shape[2] // 2
        self.keep = pl.ds(rows * here.k, rows)
        self.give = pl.ds(rows * (1 - here.k), rows)
        self.zs = here.z % 2

    @staticmethod
    def scratch(shape, n_shard, x_first):
        k, two, rows, width = shape
        split = n_shard == 2
        cols = width // n_shard if split else width
        half = rows // 2
        if split and x_first:
            middle = (k, two, half, cols)
        else:
            middle = (k, half, width)
        last = (k, half, cols)
        shapes = [(k, two, half, width), middle, last, last, (k, two, half, width), middle, last]
        return [pltpu.VMEM(s, BF16) for s in shapes]

    def cols(self, x):
        cols = self.out.shape[2]
        return pl.ds(pl.multiple_of(x * cols, LANES), cols)

    def begin(self):
        self.copy = self.wires.go(self.grad.at[:, :, self.give, :], self.a, self.here.to_core)

    def first(self):
        h = self.here
        landed([self.copy])
        self.s1[...] = (self.grad[:, :, self.keep, :].astype(F32) + self.a[...].astype(F32)).astype(BF16)
        if self.x_first:
            self.copy = self.wires.go(self.s1.at[:, :, :, self.cols(1 - h.x)], self.b, h.to_x)
        else:
            self.copy = self.wires.go(self.s1.at[:, 1 - self.zs, :, :], self.b, h.to_mate)

    def second(self):
        h = self.here
        landed([self.copy])
        if self.x_first:
            own = self.s1[:, :, :, self.cols(h.x)]
        else:
            own = self.s1[:, self.zs, :, :]
        total = (own.astype(F32) + self.b[...].astype(F32)).astype(BF16)
        if not h.split:
            self.s3[...] = total
            self.copy = None
            return
        self.s2[...] = total
        if self.x_first:
            self.copy = self.wires.go(self.s2.at[:, 1 - self.zs, :, :], self.d, h.to_mate)
        else:
            self.copy = self.wires.go(self.s2.at[:, :, self.cols(1 - h.x)], self.d, h.to_x)

    def third(self):
        h = self.here
        if self.copy is not None:
            landed([self.copy])
            if self.x_first:
                own = self.s2[:, self.zs, :, :]
            else:
                own = self.s2[:, :, self.cols(h.x)]
            self.s3[...] = (own.astype(F32) + self.d[...].astype(F32)).astype(BF16)
        self.copy = self.wires.go(self.s3, self.e, h.to_y)

    def fourth(self):
        landed([self.copy])
        self.out[:, self.keep, :] = (self.s3[...].astype(F32) + self.e[...].astype(F32)).astype(BF16)
        done = self.out.at[:, self.keep, :]
        self.copy = self.wires.go(done, done, self.here.to_core)

    def end(self):
        landed([self.copy])


REDUCE_COPIES = 5


def wavefront(jobs, names):
    for step in range(len(jobs) + len(names) - 1):
        for i, job in enumerate(jobs):
            if 0 <= step - i < len(names):
                getattr(job, names[step - i])()


REDUCE_STAGES = ("begin", "first", "second", "third", "fourth", "end")


def attend_kernel(n_shard, s_ref, x_ref, gains_ref, *refs):
    shards, tables, refs = refs[:4], refs[4:8], refs[8:]
    wqkv, wo, wi, wm, gains, normed, q, k, v, p, ctx, ext, send, recv = refs
    h = Place(n_shard)
    near = [{"tp": (h.z + i) % 4} for i in (1, 2, 3)] + [{"ctx": (h.c + i) % 4} for i in (1, 2, 3)]
    if h.split:
        near.append(h.to_x)
    h.meet(near)
    wires = Wires(send, recv)
    local = x_ref.shape[2]
    seq = x_ref.at[0, h.z % 2]
    kept = [wires.own(seq, ext.at[pl.ds(HALF, local), :])]
    rims = [
        wires.go(seq.at[pl.ds(0, HALF), :], ext.at[pl.ds(HALF + local, HALF), :], h.to_prev),
        wires.go(seq.at[pl.ds(local - HALF, HALF), :], ext.at[pl.ds(0, HALF), :], h.to_next),
    ]
    if h.split:
        cols = gains_ref.shape[1]
        mine = gains.at[:, pl.ds(pl.multiple_of(h.x * cols, LANES), cols)]
        kept.append(wires.own(gains_ref, mine))
        rims.append(wires.go(gains_ref, mine, h.to_x))
    else:
        kept.append(wires.own(gains_ref, gains))
    near_jobs = [Gather(shards[0].at[i], wqkv.at[0, i], 0, wires, h) for i in range(3)]
    far_jobs = [Gather(shards[0].at[i], wqkv.at[1, i], 1, wires, h) for i in range(3)]
    late = [(1, wo, 0), (2, wi, 0), (2, wi, 1), (3, wm, 0)]
    late = [Gather(shards[i].at[part], full.at[part], None, wires, h) for i, full, part in late]
    run(near_jobs, "begin")
    run(far_jobs, "begin")
    run(late, "begin")
    for copy in kept:
        copy.wait()
    landed(rims)
    phase_norm(ext, gains, normed)
    run(near_jobs, "cross")
    run(near_jobs, "share")
    run(near_jobs, "relay")
    run(near_jobs, "end")
    run(far_jobs, "cross")
    qkv = functools.partial(phase_qkv, normed, wqkv, tables, q, k, v, s_ref[2], 384)
    attend = functools.partial(phase_attend, q, k, v, p, ctx, s_ref[1], s_ref[0])
    tiles = local // TILE
    half = p.shape[1] // 2
    qkv(0)
    run(far_jobs, "share")
    run(late[:1], "cross")
    attend(range(half), 0, tiles // 2)
    run(far_jobs, "relay")
    run(late[:1], "share")
    run(late[1:2], "cross")
    attend(range(half), tiles // 2, tiles)
    run(far_jobs, "end")
    run(late[:1], "relay")
    run(late[1:2], "share")
    run(late[2:3], "cross")
    qkv(1)
    run(late[:1], "end")
    run(late[1:2], "relay")
    run(late[2:3], "share")
    run(late[3:4], "cross")
    attend(range(half, 2 * half), 0, tiles // 2)
    run(late[2:3], "relay")
    run(late[3:4], "share")
    attend(range(half, 2 * half), tiles // 2, tiles)
    run(late[3:4], "relay")
    run(late[1:4], "end")
    wires.close()


def run(jobs, stage):
    for job in jobs:
        getattr(job, stage)()


def back_kernel(n_shard, s_ref, q, k, v, p, ctx, dctx, gml, normed, gains_ref, wqkv, dwi, dwm, dwo, gain2, *refs):
    tables, (x_ref, layer_ref), outs, refs = refs[:4], refs[4:6], refs[6:13], refs[13:]
    layer_all, input_all, out_qkv, out_wi, out_wm, out_wo, out_gain = outs
    x, dk, dv, dqkv, given, rim_out, rim_in, dw, gg, gbuf, send, recv = refs[:12]
    bufs = refs[12:]
    h = Place(n_shard)
    near = [h.to_mate] + [{"ctx": (h.c + i) % 4} for i in (1, 2, 3)]
    if h.split:
        near.append(h.to_x)
    h.meet(near)
    wires = Wires(send, recv)
    m = h.z % 2
    local, width = x.shape
    kept = [wires.own(x_ref.at[0, m], x), wires.own(layer_ref, layer_all.at[m])]
    swaps = [wires.go(layer_ref, layer_all.at[m], h.to_mate)]
    jobs = [Reduce(g, o, bufs[7 * i : 7 * i + 7], wires, h, True) for i, (g, o) in enumerate(((dwi, out_wi), (dwm, out_wm), (dwo, out_wo)))]
    late = [Reduce(dw.at[pl.ds(i, 1)], out_qkv.at[pl.ds(i, 1)], bufs[7 * (3 + i) : 7 * (4 + i)], wires, h, True) for i in range(3)]
    late.append(Reduce(gbuf, out_gain, bufs[42:49], wires, h, True))
    run(jobs, "begin")
    dk[...] = jnp.zeros_like(dk)
    dv[...] = jnp.zeros_like(dv)
    gg[...] = jnp.zeros_like(gg)
    tiles = local // TILE
    back = functools.partial(phase_attend_back, q, k, v, p, ctx, dctx, tables, dqkv, dk, dv, s_ref[2])
    pack = functools.partial(phase_pack, dk, dv, tables, dqkv, s_ref[2])
    rows = 2 * TILE

    def finish(i):
        r0 = i * rows
        phase_input(x, gml, gains_ref, wqkv, dqkv, given, gg, r0, rows)
        piece = given.at[pl.ds(r0, rows), :]
        target = input_all.at[m, pl.ds(r0, rows), :]
        kept.append(wires.own(piece, target))
        swaps.append(wires.go(piece, target, h.to_mate))

    back(tiles - 1, tiles)
    back(0, 1)
    ext = local + 2 * HALF
    for i, ref in enumerate((dk, dv)):
        rim_out[0, i] = ref[:HALF, :].astype(BF16)
        rim_out[1, i] = ref[ext - HALF :, :].astype(BF16)
    rims = [wires.go(rim_out.at[0], rim_in.at[0], h.to_prev), wires.go(rim_out.at[1], rim_in.at[1], h.to_next)]
    run(jobs, "first")
    back(1, 3)
    landed(rims)
    for i, ref in enumerate((dk, dv)):
        ref[HALF : 2 * HALF, :] += rim_in[1, i].astype(F32)
        ref[ext - 2 * HALF : ext - HALF, :] += rim_in[0, i].astype(F32)
    kept[0].wait()
    run(jobs, "second")
    pack(0, 2)
    finish(0)
    run(jobs, "third")
    back(3, 5)
    run(jobs, "fourth")
    pack(2, 4)
    finish(1)
    run(jobs, "end")
    back(5, 7)
    pack(4, 8)
    half = width // 2
    own = normed[HALF : HALF + local, :]
    for i in range(3):
        weight_grad(dqkv, own, dw.at[i].reshape(half, width), LANES, at=i * half, count=half)
        late[i].begin()
    finish(2)
    run(late[:3], "first")
    finish(3)
    gain_rows = jnp.concatenate([gg[...], gain2[...]], axis=0).astype(BF16)
    gain_rows = jnp.concatenate([gain_rows, gain_rows], axis=0)
    gbuf[0, 0] = gain_rows
    gbuf[0, 1] = gain_rows
    late[3].begin()
    for stage in REDUCE_STAGES[1:]:
        if stage != "first":
            run(late[:3], stage)
        run(late[3:], stage)
    landed(swaps)
    for copy in kept[1:]:
        copy.wait()
    wires.close()


def call(kernel, outs, *args, scratch=(), name=None):
    vmem = pl.BlockSpec(memory_space=pltpu.VMEM)
    smem = pl.BlockSpec(memory_space=pltpu.SMEM)
    return pl.pallas_call(
        kernel,
        out_shape=[jax.ShapeDtypeStruct(s, d) for s, d in outs],
        in_specs=[smem if a.dtype == jnp.int32 else vmem for a in args],
        out_specs=[vmem] * len(outs),
        scratch_shapes=list(scratch),
        compiler_params=pltpu.CompilerParams(vmem_limit_bytes=VMEM_LIMIT),
        name=name,
    )(*args)


def on_device(inputs, lengths, attn_gain, mlp_gain, qkv_weight, attn_weight, mlp_in_weight, mlp_out_weight, cotangent):
    n_tp = lax.axis_size("tp")
    n_ctx = lax.axis_size("ctx")
    tp = lax.axis_index("tp")
    ctx = lax.axis_index("ctx")
    seqs, local = inputs.shape[1], inputs.shape[2]
    width = inputs.shape[3]
    group = n_tp // 2
    mine = tp % seqs
    pair = tp // 2
    tables = tuple(jnp.asarray(t) for t in rope_constants(local * n_ctx))

    n_shard = lax.axis_size("shard")
    shards = [jnp.transpose(qkv_weight, (1, 2, 0)), attn_weight[None], jnp.transpose(mlp_in_weight, (1, 2, 0)), mlp_out_weight[None]]
    gains = jnp.pad(jnp.stack([attn_gain, mlp_gain]), ((0, 14), (0, 0)))
    if n_shard != 2:
        shards = [lax.all_gather(s, "shard", axis=2, tiled=True) for s in shards]
        gains = lax.all_gather(gains, "shard", axis=1, tiled=True)
    hbm = pl.BlockSpec(memory_space=pl.ANY)
    vmem = pl.BlockSpec(memory_space=pltpu.VMEM)
    smem = pl.BlockSpec(memory_space=pltpu.SMEM)
    length = lax.dynamic_index_in_dim(lengths[0], mine, 0, keepdims=True)
    block0 = ctx * (local // HALF) - 1
    pos0 = ctx * local
    scalars = jnp.stack([length[0], pos0.astype(jnp.int32), block0.astype(jnp.int32)])
    ext = local + 2 * HALF
    tiles = local // TILE
    chunks = width // LANES
    span = TILE + 2 * HALF
    wide = ((ext, width), BF16)
    tall = ((local, width), BF16)
    outs = [
        ((2, 3, 2, shards[0].shape[1], width), BF16),
        *(((s.shape[0], n_tp, s.shape[1], width), BF16) for s in shards[1:]),
        ((16, width), BF16),
        wide, wide, wide, wide,
        ((tiles, chunks, 2 * TILE, span), BF16),
        tall,
    ]
    copies = 124
    wqkv, wo, wi, wm, gains, normed, q, k, v, probs, context = pl.pallas_call(
        functools.partial(attend_kernel, n_shard),
        out_shape=[jax.ShapeDtypeStruct(*o) for o in outs],
        in_specs=[smem] + [hbm] * 6 + [vmem] * 4,
        out_specs=[vmem] + [hbm] * 3 + [vmem] * 7,
        scratch_shapes=[pltpu.VMEM((ext, width), BF16), pltpu.SemaphoreType.DMA((copies,)), pltpu.SemaphoreType.DMA((copies,))],
        compiler_params=pltpu.CompilerParams(collective_id=0, has_side_effects=True, vmem_limit_bytes=VMEM_LIMIT),
        name="attend",
    )(scalars, inputs, gains, *shards, *tables)
    wqkv, wo, wi, wm = (f.reshape(-1, width) for f in (wqkv, wo, wi, wm))
    gain1, gain2 = gains[:1], gains[1:2]
    x_own = lax.dynamic_index_in_dim(inputs[0], mine, 0, keepdims=False)
    cot = lax.dynamic_index_in_dim(cotangent[0], mine, 0, keepdims=False)
    ff = wm.shape[0]
    ff_half = ff // 2

    def kernel_d(s_ref, x_ref, cot_ref, ctx_ref, g_ref, wo_ref, wi_ref, wm_ref, out, gml, dctx, gg, dwm, dwi, dwo, go, nm, hid, dgu):
        phase_mlp(x_ref, cot_ref, ctx_ref, g_ref, wo_ref, wi_ref, wm_ref, out, gml, go, nm, hid, dgu, dctx, gg, s_ref[1], s_ref[0], 256)
        weight_grad(hid, go[...], dwm, 192)
        weight_grad(dgu, nm[...], dwi, 384)
        weight_grad(ctx_ref, gml[...], dwo, LANES, count=width // 2)

    layer_own, gml, dctx, gain2_part, dwm, dwi, dwo = call(
        kernel_d,
        [tall, tall, tall, ((8, width), F32), ((ff_half, width), BF16), ((2 * ff_half, width), BF16), ((width // 2, width), BF16)],
        scalars, x_own, cot, context, gain2, wo, wi, wm,
        scratch=[pltpu.VMEM((local, width), BF16), pltpu.VMEM((local, width), BF16), pltpu.VMEM((local, ff_half), BF16), pltpu.VMEM((local, 2 * ff_half), BF16)],
        name="feed_forward",
    )
    width_half = width // 2
    cols = width // n_shard if n_shard == 2 else width
    grads = [(3, 2, width_half // 2, width), (2, 2, ff_half // 2, width), (1, 2, ff_half // 2, width), (1, 2, width_half // 2, width), (1, 2, 32, width)]
    dwi, dwm, dwo = (g.reshape(shape) for g, shape in zip((dwi, dwm, dwo), grads[1:]))
    jobs = grads[1:4] + [(1, *grads[0][1:])] * 3 + grads[4:]
    sends = 64
    layer_out, input_grad, *owned = pl.pallas_call(
        functools.partial(back_kernel, n_shard),
        out_shape=[jax.ShapeDtypeStruct((seqs, local, width), BF16)] * 2 + [jax.ShapeDtypeStruct((g[0], g[2], cols), BF16) for g in grads],
        in_specs=[smem] + [vmem] * 18 + [hbm] * 2,
        out_specs=[hbm] * 2 + [vmem] * len(grads),
        scratch_shapes=[
            pltpu.VMEM((local, width), BF16),
            pltpu.VMEM((ext, width), F32),
            pltpu.VMEM((ext, width), F32),
            pltpu.VMEM((local, 3 * width), BF16),
            pltpu.VMEM((local, width), BF16),
            pltpu.VMEM((2, 2, HALF, width), BF16),
            pltpu.VMEM((2, 2, HALF, width), BF16),
            pltpu.VMEM(grads[0], BF16),
            pltpu.VMEM((8, width), F32),
            pltpu.VMEM(grads[4], BF16),
            pltpu.SemaphoreType.DMA((sends,)),
            pltpu.SemaphoreType.DMA((sends,)),
        ]
        + [b for g in jobs for b in Reduce.scratch(g, n_shard, True)],
        compiler_params=pltpu.CompilerParams(collective_id=1, has_side_effects=True, vmem_limit_bytes=VMEM_LIMIT),
        name="back",
    )(scalars, q, k, v, probs, context, dctx, gml, normed, gains, wqkv, dwi, dwm, dwo, gain2_part, *tables, inputs, layer_own)
    owned = [g.astype(F32) for g in owned]
    if n_shard != 2:
        owned = [lax.psum_scatter(g, "shard", scatter_dimension=2, tiled=True) for g in owned]
    qkv_grad = jnp.transpose(owned[0], (2, 0, 1))
    mlp_in_grad = jnp.transpose(owned[1], (2, 0, 1))
    mlp_out_grad, attn_grad = owned[2][0], owned[3][0]
    share = owned[4].shape[2] // n_tp
    gains = lax.dynamic_slice_in_dim(owned[4][0, :16], tp * share, share, axis=1)
    gains = jnp.sum(gains.reshape(2, 8, share), axis=1)
    return (layer_out[None], input_grad[None], qkv_grad, attn_grad, mlp_in_grad, mlp_out_grad, gains[0], gains[1])


def solution(mesh):
    in_specs = (
        P("shard", None, "ctx", None),
        P("shard", None),
        P("shard"),
        P("shard"),
        P("shard", None, "tp"),
        P("tp", "shard"),
        P("shard", None, "tp"),
        P("tp", "shard"),
        P("shard", None, "ctx", None),
    )
    out_specs = (
        P("shard", None, "ctx", None),
        P("shard", None, "ctx", None),
        P("shard", None, "tp"),
        P("tp", "shard"),
        P("shard", None, "tp"),
        P("tp", "shard"),
        P(("shard", "tp")),
        P(("shard", "tp")),
    )
    return jax.shard_map(on_device, mesh=mesh, in_specs=in_specs, out_specs=out_specs, check_vma=False)
```

```python
import functools
import math

import numpy as np

import jax
import jax.numpy as jnp
from jax import lax
from jax.experimental import pallas as pl
from jax.experimental.pallas import tpu as pltpu
from jax.sharding import PartitionSpec as P

HD = 64
HALF = 64
TILE = 128
LANES = 128
norm_eps = 1e-05
rope_base = 10000.0
masked_score = -1e30
F32 = jnp.float32
BF16 = jnp.bfloat16
VMEM_LIMIT = 60 * 1024 * 1024


def nt(a, b):
    return lax.dot_general(a, b, (((1,), (1,)), ((), ())), preferred_element_type=F32)


def nn(a, b):
    return lax.dot_general(a, b, (((1,), (0,)), ((), ())), preferred_element_type=F32)


def tn(a, b):
    return lax.dot_general(a, b, (((0,), (0,)), ((), ())), preferred_element_type=F32)


def rope_constants(seq):
    w = rope_base ** (-np.arange(0, HD, 2) / HD)
    w = np.tile(w, 2 * LANES // HD)
    rows = np.arange(TILE)[:, None] * w
    blocks = (np.arange(seq // HALF + 4)[:, None] - 1) * HALF * w
    tables = (np.cos(rows), np.sin(rows), np.cos(blocks), np.sin(blocks))
    return tuple(t.astype(np.float32) for t in tables)


def rope_tile(tables, block):
    cos_r, sin_r, cos_b, sin_b = tables
    cb = cos_b[pl.ds(block + 1, 1), :]
    sb = sin_b[pl.ds(block + 1, 1), :]
    cr = cos_r[...]
    sr = sin_r[...]
    cosine = cr * cb - sr * sb
    sine = sr * cb + cr * sb
    first = lax.broadcasted_iota(jnp.int32, sine.shape, 1) % HD < HD // 2
    return cosine, jnp.where(first, -sine, sine), first


def turn(u, cosine, sine, first):
    other = jnp.where(first, pltpu.roll(u, LANES - HD // 2, 1), pltpu.roll(u, HD // 2, 1))
    return u * cosine + other * sine


def layer_stats(z):
    center = z - jnp.mean(z, axis=-1, keepdims=True)
    inv = lax.rsqrt(jnp.mean(center * center, axis=-1, keepdims=True) + norm_eps)
    return center * inv, inv


def layer_back(e, xhat, inv):
    return (e - jnp.mean(e, axis=-1, keepdims=True) - xhat * jnp.mean(e * xhat, axis=-1, keepdims=True)) * inv


def head_masks(shape):
    lane = lax.broadcasted_iota(jnp.int32, shape, 1)
    return lane < HD


def split_heads(c, low_head):
    zero = jnp.zeros_like(c)
    return jnp.concatenate([jnp.where(low_head, c, zero), jnp.where(low_head, zero, c)], axis=0)


def phase_norm(x_ref, gain_ref, normed_ref):
    def body(t, carry):
        r0 = pl.multiple_of(t * TILE, TILE)
        xhat, _ = layer_stats(x_ref[pl.ds(r0, TILE), :].astype(F32))
        normed_ref[pl.ds(r0, TILE), :] = (xhat * gain_ref[:1, :].astype(F32)).astype(BF16)
        return carry

    lax.fori_loop(0, x_ref.shape[0] // TILE, body, 0)


def phase_qkv(normed_ref, w_ref, tables, q_ref, k_ref, v_ref, block0, rows, which, after):
    width = normed_ref.shape[1]
    half = width // 2
    scaling = 1.0 / math.sqrt(HD)

    def body(t, carry):
        r0 = pl.multiple_of(t * rows, rows)
        out = nt(normed_ref[pl.ds(r0, rows), :], w_ref[which].reshape(3 * half, width))
        for s in range(rows // TILE):
            here = pl.ds(r0 + s * TILE, TILE)
            cosine, sine, first = rope_tile(tables, block0 + t * (rows // HALF) + s * (TILE // HALF))
            for part, ref in enumerate((q_ref, k_ref)):
                if part == 0:
                    turns = cosine * scaling, sine * scaling, first
                else:
                    turns = cosine, sine, first
                for j in range(half // LANES):
                    u = out[s * TILE : (s + 1) * TILE, part * half + j * LANES : part * half + (j + 1) * LANES]
                    ref[here, which * half + j * LANES : which * half + (j + 1) * LANES] = turn(u, *turns).astype(BF16)
        v_ref[pl.ds(r0, rows), which * half : (which + 1) * half] = out[:, 2 * half :].astype(BF16)
        after(t)
        return carry

    lax.fori_loop(0, normed_ref.shape[0] // rows, body, 0)


def phase_attend(q_ref, k_ref, v_ref, p_ref, ctx_ref, pos0, length, chunks, lo, hi, after):
    span = TILE + 2 * HALF

    def body(t, carry):
        r0 = pl.multiple_of(t * TILE, TILE)
        row = lax.broadcasted_iota(jnp.int32, (TILE, span), 0)
        col = lax.broadcasted_iota(jnp.int32, (TILE, span), 1)
        offset = col - row
        key_pos = pos0 + t * TILE - HALF + col
        allowed = (offset >= 0) & (offset <= 2 * HALF) & (key_pos >= 0) & ((key_pos < length) | (offset == HALF))
        bias = jnp.where(allowed, 0.0, masked_score).astype(F32)
        bias = jnp.concatenate([bias, bias], axis=0)
        low_head = head_masks((TILE, LANES))
        for j in chunks:
            lanes = slice(j * LANES, (j + 1) * LANES)
            q2 = split_heads(q_ref[pl.ds(r0 + HALF, TILE), lanes], low_head)
            scores = nt(q2, k_ref[pl.ds(r0, span), lanes]) + bias
            terms = jnp.exp(scores - jnp.max(scores, axis=-1, keepdims=True))
            probs = (terms * (1.0 / jnp.sum(terms, axis=-1, keepdims=True))).astype(BF16)
            p_ref[t, j] = probs
            out = nn(probs, v_ref[pl.ds(r0, span), lanes])
            ctx_ref[pl.ds(r0, TILE), lanes] = jnp.where(low_head, out[:TILE], out[TILE:]).astype(BF16)
        after(t)
        return carry

    lax.fori_loop(lo, hi, body, 0)


def phase_mlp(x_ref, cot_ref, ctx_ref, gain_ref, wo_ref, wi_ref, wm_ref, out_ref, gml_ref, nm_ref, hid_ref, dgu_ref, dctx_ref, gg_ref, pos0, length, rows, ready):
    ff = wm_ref.shape[0]
    half = hid_ref.shape[1]
    gg_ref[...] = jnp.zeros_like(gg_ref)

    def body(t, carry):
        r0 = pl.multiple_of(t * rows, rows)
        here = pl.ds(r0, rows)
        gain = gain_ref[1:2, :].astype(F32)
        middle = x_ref[pl.ds(r0 + HALF, rows), :].astype(F32) + nn(ctx_ref[here, :], wo_ref[...])
        xhat, inv = layer_stats(middle)
        nm = (xhat * gain).astype(BF16)
        nm_ref[here, :] = nm
        gate = nt(nm, wi_ref[:ff, :])
        up = nt(nm, wi_ref[ff:, :])
        cdf = 0.5 + 0.5 * lax.erf(gate * math.sqrt(0.5))
        gelu = gate * cdf
        slope = cdf + gate * (jnp.exp(-0.5 * gate * gate) * (1.0 / math.sqrt(2.0 * math.pi)))
        hidden = (gelu * up).astype(BF16)
        hid_ref[here, :] = hidden[:, :half]
        valid = pos0 + r0 + lax.broadcasted_iota(jnp.int32, (rows, 1), 0) < length
        out_ref[here, :] = jnp.where(valid, middle + nn(hidden, wm_ref[...]), 0.0).astype(BF16)
        ready(t)
        grad_out = jnp.where(valid, cot_ref[here, :].astype(F32), 0.0)
        grad_low = grad_out.astype(BF16)
        cot_ref[here, :] = grad_low
        grad_hidden = nt(grad_low, wm_ref[...])
        grad_gate = (grad_hidden * up * slope).astype(BF16)
        grad_up = (grad_hidden * gelu).astype(BF16)
        dgu_ref[here, :half] = grad_gate[:, :half]
        dgu_ref[here, half:] = grad_up[:, :half]
        grad_nm = nn(grad_gate, wi_ref[:ff, :]) + nn(grad_up, wi_ref[ff:, :])
        gg_ref[...] += jnp.sum((grad_nm * xhat).reshape(rows // 8, 8, -1), axis=0)
        grad_middle = grad_out + layer_back(grad_nm * gain, xhat, inv)
        gm_low = grad_middle.astype(BF16)
        gml_ref[here, :] = gm_low
        dctx_ref[here, :] = nt(gm_low, wo_ref[...]).astype(BF16)
        return carry

    lax.fori_loop(0, ctx_ref.shape[0] // rows, body, 0)


def phase_attend_back(q_ref, k_ref, v_ref, p_ref, ctx_ref, dctx_ref, tables, dqkv_ref, dk_ref, dv_ref, block0, lo, hi, after):
    width = q_ref.shape[1]
    half = width // 2
    span = TILE + 2 * HALF
    scaling = 1.0 / math.sqrt(HD)

    def body(t, carry):
        r0 = pl.multiple_of(t * TILE, TILE)
        low_head = head_masks((TILE, LANES))
        cosine, sine, first = rope_tile(tables, block0 + 1 + t * (TILE // HALF))
        cosine, sine = cosine * scaling, sine * -scaling
        keys = pl.ds(r0, span)
        for j in range(width // LANES):
            lanes = slice(j * LANES, (j + 1) * LANES)
            probs = p_ref[t, j]
            kc = k_ref[keys, lanes]
            dc = dctx_ref[pl.ds(r0, TILE), lanes]
            row_term = dc.astype(F32) * ctx_ref[pl.ds(r0, TILE), lanes].astype(F32)
            row_low = jnp.sum(jnp.where(low_head, row_term, 0.0), axis=-1, keepdims=True)
            row_high = jnp.sum(jnp.where(low_head, 0.0, row_term), axis=-1, keepdims=True)
            row_term = jnp.concatenate([row_low, row_high], axis=0)
            dc2 = split_heads(dc, low_head)
            grad_probs = nt(dc2, v_ref[keys, lanes])
            grad_scores = (probs.astype(F32) * (grad_probs - row_term)).astype(BF16)
            dq2 = nn(grad_scores, kc)
            dq = jnp.where(low_head, dq2[:TILE], dq2[TILE:])
            at = 3 * half * (j * LANES // half) + j * LANES % half
            dqkv_ref[pl.ds(r0, TILE), at : at + LANES] = turn(dq, cosine, sine, first).astype(BF16)
            q2 = split_heads(q_ref[pl.ds(r0 + HALF, TILE), lanes], low_head)
            dk_ref[keys, lanes] += tn(grad_scores, q2)
            dv_ref[keys, lanes] += tn(probs, dc2)
        after(t)
        return carry

    lax.fori_loop(lo, hi, body, 0)


def phase_pack(dk_ref, dv_ref, tables, dqkv_ref, block0, lo, hi):
    width = dk_ref.shape[1]
    half = width // 2

    def body(t, carry):
        r0 = pl.multiple_of(t * TILE, TILE)
        cosine, sine, first = rope_tile(tables, block0 + 1 + t * (TILE // HALF))
        ext = pl.ds(r0 + HALF, TILE)
        for j in range(width // LANES):
            lanes = slice(j * LANES, (j + 1) * LANES)
            at = 3 * half * (j * LANES // half) + j * LANES % half
            dqkv_ref[pl.ds(r0, TILE), at + half : at + half + LANES] = turn(dk_ref[ext, lanes], cosine, -sine, first).astype(BF16)
            dqkv_ref[pl.ds(r0, TILE), at + 2 * half : at + 2 * half + LANES] = dv_ref[ext, lanes].astype(BF16)
        return carry

    lax.fori_loop(lo, hi, body, 0)


def phase_input(x_ref, gm_ref, gain_ref, w_ref, dqkv_ref, out_ref, gg_ref, r0, rows):
    here = pl.ds(r0, rows)
    gain = gain_ref[:1, :].astype(F32)
    grad_normed = nn(dqkv_ref[here, :], w_ref[...])
    xhat, inv = layer_stats(x_ref[here, :].astype(F32))
    gg_ref[...] += jnp.sum((grad_normed * xhat).reshape(rows // 8, 8, -1), axis=0)
    out_ref[here, :] = (gm_ref[here, :].astype(F32) + layer_back(grad_normed * gain, xhat, inv)).astype(BF16)


def weight_grad(a_ref, b, out_ref, columns, at=0, count=None):
    for c in range(0, a_ref.shape[1] if count is None else count, columns):
        out_ref[c : c + columns, :] = tn(a_ref[:, at + c : at + c + columns], b).astype(out_ref.dtype)


def slot_of(at, of):
    return (of + 2 * (at // 2)) % 4


class Place:
    def __init__(self, n_shard):
        self.split = n_shard == 2
        self.x = lax.axis_index("shard")
        self.c = lax.axis_index("ctx")
        self.z = lax.axis_index("tp")
        self.k = self.c % 2
        self.y = self.c // 2
        self.up = (self.z + 1) % 4
        self.down = (self.z + 3) % 4
        self.mate = self.z + 1 - 2 * (self.z % 2)
        self.core = self.c + 1 - 2 * self.k
        self.across = (self.c + 2) % 4
        self.to_x = {"shard": 1 - self.x}
        self.to_up = {"tp": self.up}
        self.to_down = {"tp": self.down}
        self.to_mate = {"tp": self.mate}
        self.to_core = {"ctx": self.core}
        self.to_y = {"ctx": self.across}
        self.to_next = {"ctx": (self.c + 1) % 4}
        self.to_prev = {"ctx": (self.c + 3) % 4}

    def meet(self, partners):
        barrier = pltpu.get_barrier_semaphore()
        for device in partners:
            pl.semaphore_signal(barrier, inc=1, device_id=device, device_id_type=pl.DeviceIdType.MESH)
        pl.semaphore_wait(barrier, len(partners))


class Wires:
    def __init__(self, send, recv):
        self.send, self.recv, self.next, self.open = send, recv, 0, []

    def block(self, count):
        base = self.next
        self.next += count
        return base

    def remote(self, i, src, dst, device):
        return pltpu.make_async_remote_copy(
            src_ref=src, dst_ref=dst, send_sem=self.send.at[i], recv_sem=self.recv.at[i], device_id=device, device_id_type=pl.DeviceIdType.MESH
        )

    def local(self, i, src, dst):
        return pltpu.make_async_copy(src, dst, self.recv.at[i])

    def go(self, src, dst, device):
        copy = self.remote(self.block(1), src, dst, device)
        copy.start()
        self.open.append(copy)
        return copy

    def own(self, src, dst):
        copy = self.local(self.block(1), src, dst)
        copy.start()
        return copy

    @staticmethod
    def done(copies):
        for copy in copies:
            copy.wait()

    def close(self):
        for copy in self.open:
            copy.wait_send()


def started(copies):
    for copy in copies:
        copy.start()


class Stream:
    def __init__(self, wires, here, stage, target, rows, count, shift=0):
        self.wires, self.here, self.stage, self.target, self.rows, self.count, self.shift = wires, here, stage, target, rows, count, shift
        self.base = wires.block(2 * count)

    def pair(self, t):
        rows = pl.ds(pl.multiple_of(t * self.rows, self.rows), self.rows)
        to = pl.ds(pl.multiple_of((t + self.shift) * self.rows, self.rows), self.rows)
        src, dst = self.stage.at[rows, :], self.target.at[self.here.z % 2, to, :]
        return self.wires.remote(self.base + t, src, dst, self.here.to_mate), self.wires.local(self.base + self.count + t, src, dst)

    def start(self, t):
        started(self.pair(t))

    def finish(self):
        for t in range(self.count):
            self.wires.done(self.pair(t))


def landed(copies):
    for copy in copies:
        copy.wait_recv()


class Gather:
    SEMS = 12

    def __init__(self, shard, full, which, wires, here):
        self.shard, self.full, self.wires, self.here = shard, full, wires, here
        rows = shard.shape[0] // 6
        self.mine = pl.ds(rows * here.c, rows)
        self.rest = pl.ds(rows * (4 + here.k), rows)
        self.theirs = pl.ds(rows * here.across, rows)
        other = (here.z + 2) % 4
        self.to = [other, other + 1 - 2 * (other % 2)] if which else [here.mate]
        self.slots = [slot_of(to, here.z) - 2 * which for to in self.to]
        self.keeps = which == 0
        self.own_slot = here.z % 2
        self.base = wires.block(self.SEMS)

    def cols(self, x):
        cols = self.shard.shape[1]
        return pl.ds(pl.multiple_of(x * cols, LANES), cols) if self.here.split else pl.ds(0, cols)

    def spread(self):
        cols = self.cols(self.here.x)
        jobs = [(rows, to, slot) for rows in (self.rest, self.mine) for to, slot in zip(self.to, self.slots)]
        return [
            self.wires.remote(self.base + i, self.shard.at[rows, :], self.full.at[slot, rows, cols], {"tp": to})
            for i, (rows, to, slot) in enumerate(jobs)
        ]

    def kept(self):
        cols = self.cols(self.here.x)
        if not self.keeps:
            return []
        return [
            self.wires.local(self.base + 4 + i, self.shard.at[rows, :], self.full.at[self.own_slot, rows, cols])
            for i, rows in enumerate((self.rest, self.mine))
        ]

    def crossed(self):
        if not self.here.split:
            return []
        cols = self.cols(self.here.x)
        blocks = [self.full.at[:, rows, cols] for rows in (self.rest, self.mine)]
        return [self.wires.remote(self.base + 6 + i, block, block, self.here.to_x) for i, block in enumerate(blocks)]

    def level(self):
        block = self.full.at[:, self.mine, :]
        return [self.wires.remote(self.base + 8, block, block, self.here.to_y)]

    def pooled(self):
        blocks = [self.full.at[:, rows, :] for rows in (self.rest, self.mine)]
        return [self.wires.remote(self.base + 9 + i, block, block, self.here.to_core) for i, block in enumerate(blocks)]

    def passed(self):
        block = self.full.at[:, self.theirs, :]
        return [self.wires.remote(self.base + 11, block, block, self.here.to_core)]

    def stage(self, number):
        if number == 0:
            started(self.spread())
            started(self.kept())
        elif number == 1:
            landed(self.spread())
            self.wires.done(self.kept())
            started(self.crossed())
        elif number == 2:
            landed(self.crossed())
            started(self.level())
            started(self.pooled())
        elif number == 3:
            landed(self.level())
            started(self.passed())
        else:
            landed(self.pooled())
            landed(self.passed())

    def close(self):
        for copy in self.spread() + self.crossed() + self.level() + self.pooled() + self.passed():
            copy.wait_send()


def fire(jobs, *events):
    for event in events:
        jobs[event % 100].stage(event // 100)


def between(jobs, table):
    def after(t):
        for step, events in table.items():
            pl.when(t == step)(functools.partial(fire, jobs, *events))

    return after


class Reduce:
    SEMS = 5

    def __init__(self, grad, out, bufs, wires, here):
        self.grad, self.out, self.wires, self.here = grad, out, wires, here
        self.a, self.b, self.d, self.e = bufs
        rows = grad.shape[2] // 2
        self.keep = pl.ds(rows * here.k, rows)
        self.give = pl.ds(rows * (1 - here.k), rows)
        self.zs = here.z % 2
        self.base = wires.block(self.SEMS)

    @staticmethod
    def scratch(shape, n_shard):
        k, two, rows, width = shape
        cols = width // n_shard if n_shard == 2 else width
        half = rows // 2
        return [pltpu.VMEM(s, BF16) for s in ((k, two, half, width), (k, two, half, cols), (k, half, cols), (k, half, cols))]

    def cols(self, x):
        cols = self.out.shape[2]
        return pl.ds(pl.multiple_of(x * cols, LANES), cols)

    def copy(self, number):
        h, remote = self.here, self.wires.remote
        if number == 0:
            return remote(self.base, self.grad.at[:, :, self.give, :], self.a, h.to_core)
        if number == 1:
            return remote(self.base + 1, self.a.at[:, :, :, self.cols(1 - h.x)], self.b, h.to_x)
        if number == 2:
            return remote(self.base + 2, self.b.at[:, 1 - self.zs, :, :], self.d, h.to_mate)
        if number == 3:
            return remote(self.base + 3, self.d, self.e, h.to_y)
        done = self.out.at[:, self.keep, :]
        return remote(self.base + 4, done, done, h.to_core)

    def stage(self, number):
        if number > 0 and (self.here.split or number != 2):
            self.copy(number - 1).wait_recv()
        if number == 1:
            total = (self.grad[:, :, self.keep, :].astype(F32) + self.a[...].astype(F32)).astype(BF16)
            if not self.here.split:
                self.b[...] = total
                return
            self.a[...] = total
        elif number == 2 and self.here.split:
            self.b[...] = (self.a[:, :, :, self.cols(self.here.x)].astype(F32) + self.b[...].astype(F32)).astype(BF16)
        elif number == 3:
            self.d[...] = (self.b[:, self.zs, :, :].astype(F32) + self.d[...].astype(F32)).astype(BF16)
        elif number == 4:
            self.out[:, self.keep, :] = (self.d[...].astype(F32) + self.e[...].astype(F32)).astype(BF16)
        if number < 5:
            self.copy(number).start()

    def close(self):
        for number in range(5):
            if self.here.split or number != 1:
                self.copy(number).wait_send()


def front_kernel(n_shard, s_ref, x_ref, cot_hbm, gains_ref, *refs):
    shards, tables, refs = refs[:4], refs[4:8], refs[8:]
    saved, (layer_all, layer_tail, gains, dctx, gml, gg, dwm, dwi, dwo), refs = refs[:7], refs[7:16], refs[16:]
    wqkv, normed, q, k, v, p, ctx, wo, wi, wm, ext, cot, out, nm, hid, dgu, send, recv = refs
    h = Place(n_shard)
    near = [{"tp": (h.z + i) % 4} for i in (1, 2, 3)] + [{"ctx": (h.c + i) % 4} for i in (1, 2, 3)]
    if h.split:
        near.append(h.to_x)
    h.meet(near)
    wires = Wires(send, recv)
    local = x_ref.shape[2]
    seq = x_ref.at[0, h.z % 2]
    kept = [wires.own(seq, ext.at[pl.ds(HALF, local), :]), wires.own(cot_hbm.at[0, h.z % 2], cot)]
    rims = [
        wires.go(seq.at[pl.ds(0, HALF), :], ext.at[pl.ds(HALF + local, HALF), :], h.to_prev),
        wires.go(seq.at[pl.ds(local - HALF, HALF), :], ext.at[pl.ds(0, HALF), :], h.to_next),
    ]
    if h.split:
        cols = gains_ref.shape[1]
        mine = gains.at[:, pl.ds(pl.multiple_of(h.x * cols, LANES), cols)]
        kept.append(wires.own(gains_ref, mine))
        rims.append(wires.go(gains_ref, mine, h.to_x))
    else:
        kept.append(wires.own(gains_ref, gains))
    others = [(shards[1], wo, 0), (shards[2], wi, 0), (shards[2], wi, 1), (shards[3], wm, 0)]
    jobs = [Gather(shards[0].at[i], wqkv.at[which, i], which, wires, h) for which in range(2) for i in range(3)]
    jobs += [Gather(src.at[part], full.at[part, pl.ds(2 * which, 2)], which, wires, h) for which in range(2) for src, full, part in others]
    stream = Stream(wires, h, out, layer_all, 2 * TILE, local // (2 * TILE) - 1)
    fire(jobs, *range(9))
    wires.done(kept)
    landed(rims)
    phase_norm(ext, gains, normed)
    fire(jobs, 100, 9, 101, 102, 106, 103, 200, 107, 108, 10, 201, 109, 104, 202, 300, 400, 11, 206, 301, 105, 401, 203, 302, 402)
    qkv = functools.partial(phase_qkv, normed, wqkv, tables, q, k, v, s_ref[2], 384)
    attend = functools.partial(phase_attend, q, k, v, p, ctx, s_ref[1], s_ref[0])
    tiles = local // TILE
    half = p.shape[1] // 2
    qkv(0, between(jobs, {0: (306, 207), 1: (303, 406, 110, 12), 2: (403, 208)}))
    attend(
        range(half),
        0,
        tiles,
        between(
            jobs,
            {
                1: (307,),
                2: (209, 111),
                3: (407, 13),
                4: (204,),
                5: (308,),
                6: (205,),
                7: (408, 210, 309, 112, 409, 304, 211, 404, 305, 405),
            },
        ),
    )
    qkv(1, between(jobs, {0: (310, 212, 113), 1: (410,), 2: (311,)}))
    attend(range(half, 2 * half), 0, tiles, between(jobs, {1: (411,), 2: (312, 213), 4: (412,), 7: (313, 413)}))
    stores = [wires.own(src, dst) for src, dst in zip((wqkv, normed, q, k, v, p, ctx), saved)]
    wo, wi, wm = (w.reshape(-1, w.shape[-1]) for w in (wo, wi, wm))
    blocks = local // (2 * TILE)

    def ready(t):
        pl.when(t < blocks - 1)(functools.partial(stream.start, t))

    phase_mlp(ext, cot, ctx, gains, wo, wi, wm, out, gml, nm, hid, dgu, dctx, gg, s_ref[1], s_ref[0], 2 * TILE, ready)
    stores.append(wires.own(out.at[pl.ds(local - 2 * TILE, 2 * TILE), :], layer_tail))
    weight_grad(hid, cot[...], dwm, 192)
    weight_grad(dgu, nm[...], dwi, 384)
    weight_grad(ctx, gml[...], dwo, LANES, count=dwo.shape[0])
    wires.done(stores)
    stream.finish()
    for job in jobs:
        job.close()
    wires.close()


def back_kernel(n_shard, s_ref, gains_ref, gain2, *refs):
    tables, homes, (x_ref, layer_in, layer_tail), outs, refs = refs[:4], refs[4:16], refs[16:19], refs[19:26], refs[26:]
    layer_all, input_all, out_qkv, out_wi, out_wm, out_wo, out_gain = outs
    q, k, v, p, ctx, dctx, gml, normed, wqkv, dwi, dwm, dwo, x = refs[:13]
    dk, dv, dqkv, given, rim_out, rim_in, dw, gg, gbuf, send, recv = refs[13:24]
    bufs = refs[24:]
    h = Place(n_shard)
    wires = Wires(send, recv)
    q_home, k_home, v_home, p_home, ctx_home, dctx_home, gml_home, normed_home, wqkv_home, dwi_home, dwm_home, dwo_home = homes
    local, width = x.shape
    tiles = local // TILE
    loads = [wires.own(src, dst) for src, dst in ((k_home, k), (v_home, v), (q_home, q), (dctx_home, dctx), (ctx_home, ctx))]
    order = [tiles - 1, *range(tiles - 1)]
    tile_loads = {t: wires.own(p_home.at[t], p.at[t]) for t in order[:3]}
    grad_loads = [wires.own(src, dst) for src, dst in ((dwi_home, dwi), (dwm_home, dwm), (dwo_home, dwo))]
    tile_loads.update({t: wires.own(p_home.at[t], p.at[t]) for t in order[3:]})
    late_loads = [wires.own(src, dst) for src, dst in ((x_ref.at[0, h.z % 2], x), (gml_home, gml), (wqkv_home, wqkv), (normed_home, normed))]
    near = [h.to_mate] + [{"ctx": (h.c + i) % 4} for i in (1, 2, 3)]
    if h.split:
        near.append(h.to_x)
    h.meet(near)
    dw_parts = [(dwi.at[pl.ds(0, 1)], out_wi.at[pl.ds(0, 1)]), (dwi.at[pl.ds(1, 1)], out_wi.at[pl.ds(1, 1)]), (dwm, out_wm), (dwo, out_wo)]
    dw_parts += [(dw.at[pl.ds(i, 1)], out_qkv.at[pl.ds(i, 1)]) for i in range(3)] + [(gbuf, out_gain)]
    jobs = [Reduce(g, o, bufs[4 * i : 4 * i + 4], wires, h) for i, (g, o) in enumerate(dw_parts)]
    rows = 2 * TILE
    last = Stream(wires, h, layer_tail, layer_all, rows, 1, local // rows - 1)
    last.start(0)
    stream = Stream(wires, h, given, input_all, rows, local // rows)
    dk[...] = jnp.zeros_like(dk)
    dv[...] = jnp.zeros_like(dv)
    gg[...] = jnp.zeros_like(gg)
    wires.done(loads)
    wires.done(tile_loads[t] for t in order[:2])
    weights = wqkv.reshape(-1, width)

    def back(lo, hi, table):
        phase_attend_back(q, k, v, p, ctx, dctx, tables, dqkv, dk, dv, s_ref[2], lo, hi, between(jobs, table))

    def pack(lo, hi):
        phase_pack(dk, dv, tables, dqkv, s_ref[2], lo, hi)

    def finish(i):
        phase_input(x, gml, gains_ref, weights, dqkv, given, gg, i * rows, rows)
        stream.start(i)

    back(tiles - 1, tiles, {})
    wires.done(grad_loads)
    fire(jobs, 0, 1, 2, 3)
    back(0, 1, {})
    ext = local + 2 * HALF
    for i, ref in enumerate((dk, dv)):
        rim_out[0, i] = ref[:HALF, :].astype(BF16)
        rim_out[1, i] = ref[ext - HALF :, :].astype(BF16)
    rims = [wires.go(rim_out.at[0], rim_in.at[0], h.to_prev), wires.go(rim_out.at[1], rim_in.at[1], h.to_next)]
    fire(jobs, 100, 101)
    wires.done(tile_loads[t] for t in order[2:])
    back(1, 3, {1: (102, 103)})
    landed(rims)
    for i, ref in enumerate((dk, dv)):
        ref[HALF : 2 * HALF, :] += rim_in[1, i].astype(F32)
        ref[ext - 2 * HALF : ext - HALF, :] += rim_in[0, i].astype(F32)
    pack(0, 2)
    wires.done(late_loads)
    finish(0)
    back(3, 5, {3: (200, 201), 4: (202, 203)})
    pack(2, 4)
    finish(1)
    back(5, 7, {5: (300, 301), 6: (302, 303)})
    pack(4, 8)
    half = width // 2
    own = normed[HALF : HALF + local, :]
    for i in range(3):
        weight_grad(dqkv, own, dw.at[i].reshape(half, width), LANES, at=i * half, count=half)
        fire(jobs, 4 + i)
    finish(2)
    fire(jobs, 104, 105, 106)
    finish(3)
    gain_rows = jnp.concatenate([gg[...], gain2[...]], axis=0).astype(BF16)
    gain_rows = jnp.concatenate([gain_rows, gain_rows], axis=0)
    gbuf[0, 0] = gain_rows
    gbuf[0, 1] = gain_rows
    fire(jobs, 7, 400, 401, 402, 403, 107, 204, 207, 205, 206, 500, 501, 502, 503, 304, 307, 305, 306, 404, 407, 405, 406, 504, 507, 505, 506)
    stream.finish()
    last.finish()
    for job in jobs:
        job.close()
    wires.close()


def on_device(inputs, lengths, attn_gain, mlp_gain, qkv_weight, attn_weight, mlp_in_weight, mlp_out_weight, cotangent):
    n_tp = lax.axis_size("tp")
    n_ctx = lax.axis_size("ctx")
    tp = lax.axis_index("tp")
    ctx = lax.axis_index("ctx")
    seqs, local = inputs.shape[1], inputs.shape[2]
    width = inputs.shape[3]
    group = n_tp // 2
    mine = tp % seqs
    pair = tp // 2
    tables = tuple(jnp.asarray(t) for t in rope_constants(local * n_ctx))

    n_shard = lax.axis_size("shard")
    shards = [jnp.transpose(qkv_weight, (1, 2, 0)), attn_weight[None], jnp.transpose(mlp_in_weight, (1, 2, 0)), mlp_out_weight[None]]
    gains = jnp.pad(jnp.stack([attn_gain, mlp_gain]), ((0, 14), (0, 0)))
    if n_shard != 2:
        shards = [lax.all_gather(s, "shard", axis=2, tiled=True) for s in shards]
        gains = lax.all_gather(gains, "shard", axis=1, tiled=True)
    hbm = pl.BlockSpec(memory_space=pl.ANY)
    vmem = pl.BlockSpec(memory_space=pltpu.VMEM)
    smem = pl.BlockSpec(memory_space=pltpu.SMEM)
    length = lax.dynamic_index_in_dim(lengths[0], mine, 0, keepdims=True)
    block0 = ctx * (local // HALF) - 1
    pos0 = ctx * local
    scalars = jnp.stack([length[0], pos0.astype(jnp.int32), block0.astype(jnp.int32)])
    ext = local + 2 * HALF
    tiles = local // TILE
    chunks = width // LANES
    span = TILE + 2 * HALF
    wide = ((ext, width), BF16)
    tall = ((local, width), BF16)
    full_shapes = [(s.shape[0], n_tp, s.shape[1], width) for s in shards]
    ff_half = 2 * mlp_out_weight.shape[0]
    width_half = width // 2
    saved = [
        ((2, 3, 2, shards[0].shape[1], width), BF16),
        wide, wide, wide, wide,
        ((tiles, chunks, 2 * TILE, span), BF16),
        tall,
    ]
    outs = [
        ((2 * TILE, width), BF16),
        ((16, width), BF16),
        tall, tall,
        ((8, width), F32),
        ((ff_half, width), BF16), ((2 * ff_half, width), BF16), ((width_half, width), BF16),
    ]
    both = ((seqs, local, width), BF16)
    copies = 14 * Gather.SEMS + 24
    results = pl.pallas_call(
        functools.partial(front_kernel, n_shard),
        out_shape=[jax.ShapeDtypeStruct(*o) for o in saved + [both] + outs],
        in_specs=[smem] + [hbm] * 7 + [vmem] * 4,
        out_specs=[hbm] * 9 + [vmem] * 7,
        scratch_shapes=[pltpu.VMEM(*o) for o in saved]
        + [pltpu.VMEM(f, BF16) for f in full_shapes[1:]]
        + [
            pltpu.VMEM(*wide),
            pltpu.VMEM(*tall),
            pltpu.VMEM(*tall),
            pltpu.VMEM(*tall),
            pltpu.VMEM((local, ff_half), BF16),
            pltpu.VMEM((local, 2 * ff_half), BF16),
            pltpu.SemaphoreType.DMA((copies,)),
            pltpu.SemaphoreType.DMA((copies,)),
        ],
        compiler_params=pltpu.CompilerParams(collective_id=0, has_side_effects=True, vmem_limit_bytes=VMEM_LIMIT),
        name="front",
    )(scalars, inputs, cotangent, gains, *shards, *tables)
    wqkv, normed, q, k, v, probs, context, layer_all, layer_tail, gains, dctx, gml, gain2_part, dwm, dwi, dwo = results
    cols = width // n_shard if n_shard == 2 else width
    grads = [(3, 2, width_half // 2, width), (2, 2, ff_half // 2, width), (1, 2, ff_half // 2, width), (1, 2, width_half // 2, width), (1, 2, 32, width)]
    dwi, dwm, dwo = (g.reshape(shape) for g, shape in zip((dwi, dwm, dwo), grads[1:]))
    jobs = [(1, *grads[1][1:])] * 2 + grads[2:4] + [(1, *grads[0][1:])] * 3 + grads[4:]
    sends = 96
    homes = (q, k, v, probs, context, dctx, gml, normed, wqkv, dwi, dwm, dwo)
    layer_out, input_grad, *owned = pl.pallas_call(
        functools.partial(back_kernel, n_shard),
        out_shape=[jax.ShapeDtypeStruct(*both)] * 2 + [jax.ShapeDtypeStruct((g[0], g[2], cols), BF16) for g in grads],
        in_specs=[smem] + [vmem] * 6 + [hbm] * 15,
        out_specs=[hbm] * 2 + [vmem] * len(grads),
        input_output_aliases={20: 0},
        scratch_shapes=[pltpu.VMEM(a.shape, a.dtype) for a in homes]
        + [
            pltpu.VMEM(*tall),
            pltpu.VMEM((ext, width), F32),
            pltpu.VMEM((ext, width), F32),
            pltpu.VMEM((local, 3 * width), BF16),
            pltpu.VMEM(*tall),
            pltpu.VMEM((2, 2, HALF, width), BF16),
            pltpu.VMEM((2, 2, HALF, width), BF16),
            pltpu.VMEM(grads[0], BF16),
            pltpu.VMEM((8, width), F32),
            pltpu.VMEM(grads[4], BF16),
            pltpu.SemaphoreType.DMA((sends,)),
            pltpu.SemaphoreType.DMA((sends,)),
        ]
        + [b for g in jobs for b in Reduce.scratch(g, n_shard)],
        compiler_params=pltpu.CompilerParams(collective_id=1, has_side_effects=True, vmem_limit_bytes=VMEM_LIMIT),
        name="back",
    )(scalars, gains, gain2_part, *tables, *homes, inputs, layer_all, layer_tail)
    owned = [g.astype(F32) for g in owned]
    if n_shard != 2:
        owned = [lax.psum_scatter(g, "shard", scatter_dimension=2, tiled=True) for g in owned]
    qkv_grad = jnp.transpose(owned[0], (2, 0, 1))
    mlp_in_grad = jnp.transpose(owned[1], (2, 0, 1))
    mlp_out_grad, attn_grad = owned[2][0], owned[3][0]
    share = owned[4].shape[2] // n_tp
    gains = lax.dynamic_slice_in_dim(owned[4][0, :16], tp * share, share, axis=1)
    gains = jnp.sum(gains.reshape(2, 8, share), axis=1)
    return (layer_out[None], input_grad[None], qkv_grad, attn_grad, mlp_in_grad, mlp_out_grad, gains[0], gains[1])


def solution(mesh):
    in_specs = (
        P("shard", None, "ctx", None),
        P("shard", None),
        P("shard"),
        P("shard"),
        P("shard", None, "tp"),
        P("tp", "shard"),
        P("shard", None, "tp"),
        P("tp", "shard"),
        P("shard", None, "ctx", None),
    )
    out_specs = (
        P("shard", None, "ctx", None),
        P("shard", None, "ctx", None),
        P("shard", None, "tp"),
        P("tp", "shard"),
        P("shard", None, "tp"),
        P("tp", "shard"),
        P(("shard", "tp")),
        P(("shard", "tp")),
    )
    return jax.shard_map(on_device, mesh=mesh, in_specs=in_specs, out_specs=out_specs, check_vma=False)
```

```python
import functools
import math

import numpy as np

import jax
import jax.numpy as jnp
from jax import lax
from jax.experimental import pallas as pl
from jax.experimental.pallas import tpu as pltpu
from jax.sharding import PartitionSpec as P

HD = 64
HALF = 64
TILE = 128
LANES = 128
norm_eps = 1e-05
rope_base = 10000.0
masked_score = -1e30
F32 = jnp.float32
BF16 = jnp.bfloat16
FRONT_BLOCKS = 2
FORWARD = (
    (100, 101, 102, 106, 103, 200, 201, 104, 202, 300, 206, 400, 301, 105, 203, 401, 302, 204, 402),
    {0: (306, 107, 108, 109, 110), 1: (303, 205)},
    {0: (304,), 1: (207,), 3: (305, 111), 4: (208,), 6: (307,), 7: (403, 404, 405, 209)},
    {0: (112,), 1: (308, 210)},
    {2: (309, 211), 3: (113,), 4: (212, 310), 7: (406, 407, 408, 409, 410, 311)},
    {0: (213, 312, 313, 411, 412, 413)},
)
VMEM_LIMIT = 60 * 1024 * 1024


def nt(a, b):
    return lax.dot_general(a, b, (((1,), (1,)), ((), ())), preferred_element_type=F32)


def nn(a, b):
    return lax.dot_general(a, b, (((1,), (0,)), ((), ())), preferred_element_type=F32)


def tn(a, b):
    return lax.dot_general(a, b, (((0,), (0,)), ((), ())), preferred_element_type=F32)


def rope_constants(seq):
    w = rope_base ** (-np.arange(0, HD, 2) / HD)
    w = np.tile(w, 2 * LANES // HD)
    rows = np.arange(TILE)[:, None] * w
    blocks = (np.arange(seq // HALF + 4)[:, None] - 1) * HALF * w
    tables = (np.cos(rows), np.sin(rows), np.cos(blocks), np.sin(blocks))
    return tuple(t.astype(np.float32) for t in tables)


def rope_tile(tables, block):
    cos_r, sin_r, cos_b, sin_b = tables
    cb = cos_b[pl.ds(block + 1, 1), :]
    sb = sin_b[pl.ds(block + 1, 1), :]
    cr = cos_r[...]
    sr = sin_r[...]
    cosine = cr * cb - sr * sb
    sine = sr * cb + cr * sb
    first = lax.broadcasted_iota(jnp.int32, sine.shape, 1) % HD < HD // 2
    return cosine, jnp.where(first, -sine, sine), first


def turn(u, cosine, sine, first):
    other = jnp.where(first, pltpu.roll(u, LANES - HD // 2, 1), pltpu.roll(u, HD // 2, 1))
    return u * cosine + other * sine


def layer_stats(z):
    center = z - jnp.mean(z, axis=-1, keepdims=True)
    inv = lax.rsqrt(jnp.mean(center * center, axis=-1, keepdims=True) + norm_eps)
    return center * inv, inv


def layer_back(e, xhat, inv):
    return (e - jnp.mean(e, axis=-1, keepdims=True) - xhat * jnp.mean(e * xhat, axis=-1, keepdims=True)) * inv


def head_masks(shape):
    lane = lax.broadcasted_iota(jnp.int32, shape, 1)
    return lane < HD


def split_heads(c, low_head):
    zero = jnp.zeros_like(c)
    return jnp.concatenate([jnp.where(low_head, c, zero), jnp.where(low_head, zero, c)], axis=0)


def phase_norm(x_ref, gain_ref, normed_ref):
    def body(t, carry):
        r0 = pl.multiple_of(t * TILE, TILE)
        xhat, _ = layer_stats(x_ref[pl.ds(r0, TILE), :].astype(F32))
        normed_ref[pl.ds(r0, TILE), :] = (xhat * gain_ref[:1, :].astype(F32)).astype(BF16)
        return carry

    lax.fori_loop(0, x_ref.shape[0] // TILE, body, 0)


def phase_qkv(normed_ref, w_ref, tables, q_ref, k_ref, v_ref, block0, rows, which, after):
    width = normed_ref.shape[1]
    half = width // 2
    scaling = 1.0 / math.sqrt(HD)

    def body(t, carry):
        r0 = pl.multiple_of(t * rows, rows)
        out = nt(normed_ref[pl.ds(r0, rows), :], w_ref[which].reshape(3 * half, width))
        for s in range(rows // TILE):
            here = pl.ds(r0 + s * TILE, TILE)
            cosine, sine, first = rope_tile(tables, block0 + t * (rows // HALF) + s * (TILE // HALF))
            for part, ref in enumerate((q_ref, k_ref)):
                if part == 0:
                    turns = cosine * scaling, sine * scaling, first
                else:
                    turns = cosine, sine, first
                for j in range(half // LANES):
                    u = out[s * TILE : (s + 1) * TILE, part * half + j * LANES : part * half + (j + 1) * LANES]
                    ref[here, which * half + j * LANES : which * half + (j + 1) * LANES] = turn(u, *turns).astype(BF16)
        v_ref[pl.ds(r0, rows), which * half : (which + 1) * half] = out[:, 2 * half :].astype(BF16)
        after(t)
        return carry

    lax.fori_loop(0, normed_ref.shape[0] // rows, body, 0)


def phase_attend(q_ref, k_ref, v_ref, p_ref, ctx_ref, pos0, length, chunks, lo, hi, after):
    span = TILE + 2 * HALF

    def body(t, carry):
        r0 = pl.multiple_of(t * TILE, TILE)
        row = lax.broadcasted_iota(jnp.int32, (TILE, span), 0)
        col = lax.broadcasted_iota(jnp.int32, (TILE, span), 1)
        offset = col - row
        key_pos = pos0 + t * TILE - HALF + col
        allowed = (offset >= 0) & (offset <= 2 * HALF) & (key_pos >= 0) & ((key_pos < length) | (offset == HALF))
        bias = jnp.where(allowed, 0.0, masked_score).astype(F32)
        bias = jnp.concatenate([bias, bias], axis=0)
        low_head = head_masks((TILE, LANES))
        for j in chunks:
            lanes = slice(j * LANES, (j + 1) * LANES)
            q2 = split_heads(q_ref[pl.ds(r0 + HALF, TILE), lanes], low_head)
            scores = nt(q2, k_ref[pl.ds(r0, span), lanes]) + bias
            terms = jnp.exp(scores - jnp.max(scores, axis=-1, keepdims=True))
            probs = (terms * (1.0 / jnp.sum(terms, axis=-1, keepdims=True))).astype(BF16)
            p_ref[t, j] = probs
            out = nn(probs, v_ref[pl.ds(r0, span), lanes])
            ctx_ref[pl.ds(r0, TILE), lanes] = jnp.where(low_head, out[:TILE], out[TILE:]).astype(BF16)
        after(t)
        return carry

    lax.fori_loop(lo, hi, body, 0)


def units(nm, grad_low, wg, wu, wm):
    gate = nt(nm, wg)
    up = nt(nm, wu)
    cdf = 0.5 + 0.5 * lax.erf(gate * math.sqrt(0.5))
    gelu = gate * cdf
    slope = cdf + gate * (jnp.exp(-0.5 * gate * gate) * (1.0 / math.sqrt(2.0 * math.pi)))
    grad_hidden = nt(grad_low, wm)
    return (gelu * up).astype(BF16), (grad_hidden * up * slope).astype(BF16), (grad_hidden * gelu).astype(BF16)


def phase_mlp(x_ref, cot_ref, ctx_ref, gain_ref, wo_ref, wi_refs, wm_refs, out_ref, gml_ref, nm_ref, hid_ref, dgu_ref, dctx_ref, gg_ref, pos0, length, rows, between_halves, ready):
    half = wm_refs[0].shape[0]
    gg_ref[...] = jnp.zeros_like(gg_ref)

    def body(t, carry):
        r0 = pl.multiple_of(t * rows, rows)
        here = pl.ds(r0, rows)
        gain = gain_ref[1:2, :].astype(F32)
        middle = x_ref[pl.ds(r0 + HALF, rows), :].astype(F32) + nn(ctx_ref[here, :], wo_ref[...])
        xhat, inv = layer_stats(middle)
        nm = (xhat * gain).astype(BF16)
        nm_ref[here, :] = nm
        valid = pos0 + r0 + lax.broadcasted_iota(jnp.int32, (rows, 1), 0) < length
        grad_low = jnp.where(valid, cot_ref[here, :].astype(F32), 0.0).astype(BF16)
        cot_ref[here, :] = grad_low
        wg, wu, wm = wi_refs[0][:half, :], wi_refs[0][half:, :], wm_refs[0][...]
        hidden, grad_gate, grad_up = units(nm, grad_low, wg, wu, wm)
        hid_ref[here, :] = hidden
        dgu_ref[here, :half] = grad_gate
        dgu_ref[here, half:] = grad_up
        mlp = nn(hidden, wm)
        grad_nm = nn(grad_gate, wg) + nn(grad_up, wu)
        between_halves(t)
        wg, wu, wm = wi_refs[1][:half, :], wi_refs[1][half:, :], wm_refs[1][...]
        hidden, grad_gate, grad_up = units(nm, grad_low, wg, wu, wm)
        out_ref[here, :] = jnp.where(valid, middle + (mlp + nn(hidden, wm)), 0.0).astype(BF16)
        ready(t)
        grad_nm = grad_nm + nn(grad_gate, wg) + nn(grad_up, wu)
        gg_ref[...] += jnp.sum((grad_nm * xhat).reshape(rows // 8, 8, -1), axis=0)
        gm_low = (grad_low.astype(F32) + layer_back(grad_nm * gain, xhat, inv)).astype(BF16)
        gml_ref[here, :] = gm_low
        dctx_ref[here, :] = nt(gm_low, wo_ref[...]).astype(BF16)
        return carry

    lax.fori_loop(0, ctx_ref.shape[0] // rows, body, 0)


def phase_attend_back(q_ref, k_ref, v_ref, p_ref, ctx_ref, dctx_ref, tables, dqkv_ref, dk_ref, dv_ref, block0, lo, hi, after):
    width = q_ref.shape[1]
    half = width // 2
    span = TILE + 2 * HALF
    scaling = 1.0 / math.sqrt(HD)

    def body(t, carry):
        r0 = pl.multiple_of(t * TILE, TILE)
        low_head = head_masks((TILE, LANES))
        cosine, sine, first = rope_tile(tables, block0 + 1 + t * (TILE // HALF))
        cosine, sine = cosine * scaling, sine * -scaling
        keys = pl.ds(r0, span)
        for j in range(width // LANES):
            lanes = slice(j * LANES, (j + 1) * LANES)
            probs = p_ref[t, j]
            kc = k_ref[keys, lanes]
            dc = dctx_ref[pl.ds(r0, TILE), lanes]
            row_term = dc.astype(F32) * ctx_ref[pl.ds(r0, TILE), lanes].astype(F32)
            row_low = jnp.sum(jnp.where(low_head, row_term, 0.0), axis=-1, keepdims=True)
            row_high = jnp.sum(jnp.where(low_head, 0.0, row_term), axis=-1, keepdims=True)
            row_term = jnp.concatenate([row_low, row_high], axis=0)
            dc2 = split_heads(dc, low_head)
            grad_probs = nt(dc2, v_ref[keys, lanes])
            grad_scores = (probs.astype(F32) * (grad_probs - row_term)).astype(BF16)
            dq2 = nn(grad_scores, kc)
            dq = jnp.where(low_head, dq2[:TILE], dq2[TILE:])
            at = 3 * half * (j * LANES // half) + j * LANES % half
            dqkv_ref[pl.ds(r0, TILE), at : at + LANES] = turn(dq, cosine, sine, first).astype(BF16)
            q2 = split_heads(q_ref[pl.ds(r0 + HALF, TILE), lanes], low_head)
            dk_ref[keys, lanes] += tn(grad_scores, q2)
            dv_ref[keys, lanes] += tn(probs, dc2)
        after(t)
        return carry

    lax.fori_loop(lo, hi, body, 0)


def phase_pack(dk_ref, dv_ref, tables, dqkv_ref, block0, lo, hi):
    width = dk_ref.shape[1]
    half = width // 2

    def body(t, carry):
        r0 = pl.multiple_of(t * TILE, TILE)
        cosine, sine, first = rope_tile(tables, block0 + 1 + t * (TILE // HALF))
        ext = pl.ds(r0 + HALF, TILE)
        for j in range(width // LANES):
            lanes = slice(j * LANES, (j + 1) * LANES)
            at = 3 * half * (j * LANES // half) + j * LANES % half
            dqkv_ref[pl.ds(r0, TILE), at + half : at + half + LANES] = turn(dk_ref[ext, lanes], cosine, -sine, first).astype(BF16)
            dqkv_ref[pl.ds(r0, TILE), at + 2 * half : at + 2 * half + LANES] = dv_ref[ext, lanes].astype(BF16)
        return carry

    lax.fori_loop(lo, hi, body, 0)


def phase_input(x_ref, gm_ref, gain_ref, w_ref, dqkv_ref, out_ref, gg_ref, r0, rows):
    here = pl.ds(r0, rows)
    gain = gain_ref[:1, :].astype(F32)
    grad_normed = nn(dqkv_ref[here, :], w_ref[...])
    xhat, inv = layer_stats(x_ref[here, :].astype(F32))
    gg_ref[...] += jnp.sum((grad_normed * xhat).reshape(rows // 8, 8, -1), axis=0)
    out_ref[here, :] = (gm_ref[here, :].astype(F32) + layer_back(grad_normed * gain, xhat, inv)).astype(BF16)


def weight_grad(a_ref, b, out_ref, columns, at=0, count=None):
    for c in range(0, a_ref.shape[1] if count is None else count, columns):
        out_ref[c : c + columns, :] = tn(a_ref[:, at + c : at + c + columns], b).astype(out_ref.dtype)


def slot_of(at, of):
    return (of + 2 * (at // 2)) % 4


class Place:
    def __init__(self, n_shard):
        self.split = n_shard == 2
        self.x = lax.axis_index("shard")
        self.c = lax.axis_index("ctx")
        self.z = lax.axis_index("tp")
        self.k = self.c % 2
        self.y = self.c // 2
        self.up = (self.z + 1) % 4
        self.down = (self.z + 3) % 4
        self.mate = self.z + 1 - 2 * (self.z % 2)
        self.core = self.c + 1 - 2 * self.k
        self.across = (self.c + 2) % 4
        self.to_x = {"shard": 1 - self.x}
        self.to_up = {"tp": self.up}
        self.to_down = {"tp": self.down}
        self.to_mate = {"tp": self.mate}
        self.to_core = {"ctx": self.core}
        self.to_y = {"ctx": self.across}
        self.to_next = {"ctx": (self.c + 1) % 4}
        self.to_prev = {"ctx": (self.c + 3) % 4}

    def meet(self, partners):
        barrier = pltpu.get_barrier_semaphore()
        for device in partners:
            pl.semaphore_signal(barrier, inc=1, device_id=device, device_id_type=pl.DeviceIdType.MESH)
        pl.semaphore_wait(barrier, len(partners))


class Wires:
    def __init__(self, send, recv):
        self.send, self.recv, self.next, self.open = send, recv, 0, []

    def block(self, count):
        base = self.next
        self.next += count
        return base

    def remote(self, i, src, dst, device):
        return pltpu.make_async_remote_copy(
            src_ref=src, dst_ref=dst, send_sem=self.send.at[i], recv_sem=self.recv.at[i], device_id=device, device_id_type=pl.DeviceIdType.MESH
        )

    def local(self, i, src, dst):
        return pltpu.make_async_copy(src, dst, self.recv.at[i])

    def go(self, src, dst, device):
        copy = self.remote(self.block(1), src, dst, device)
        copy.start()
        self.open.append(copy)
        return copy

    def own(self, src, dst):
        copy = self.local(self.block(1), src, dst)
        copy.start()
        return copy

    @staticmethod
    def done(copies):
        for copy in copies:
            copy.wait()

    def close(self):
        for copy in self.open:
            copy.wait_send()


def started(copies):
    for copy in copies:
        copy.start()


class Stream:
    def __init__(self, wires, here, stage, target, rows, sent):
        self.wires, self.here, self.stage, self.target, self.rows, self.sent = wires, here, stage, target, rows, sent
        self.count = target.shape[1] // rows
        self.base = wires.block(2 * self.count)

    def block(self, t):
        rows = pl.ds(pl.multiple_of(t * self.rows, self.rows), self.rows)
        dst = self.target.at[self.here.z % 2, rows, :]
        return dst if self.stage is None else self.stage.at[rows, :], dst

    def remote(self, t):
        return self.wires.remote(self.base + t, *self.block(t), self.here.to_mate)

    def local(self, t):
        return self.wires.local(self.base + self.count + t, *self.block(t))

    def start(self, t):
        self.local(t).start()
        pl.when(t < self.sent)(lambda: self.remote(t).start())

    def finish(self):
        for t in range(self.count):
            self.local(t).wait()
        for t in range(self.sent):
            self.remote(t).wait()


def landed(copies):
    for copy in copies:
        copy.wait_recv()


class Gather:
    SEMS = 7

    def __init__(self, shard, full, which, wires, here):
        self.shard, self.full, self.wires, self.here = shard, full, wires, here
        rows = shard.shape[0] // 6
        self.carried = pl.ds(rows * (3 * here.k + here.y), 2 * rows)
        self.mine = pl.ds(rows * (3 * here.k + 2 * here.y), rows)
        self.theirs = pl.ds(rows * (3 * here.k + 2 - 2 * here.y), rows)
        other = (here.z + 2) % 4
        self.to = [other, other + 1 - 2 * (other % 2)] if which else [here.mate]
        self.slots = [slot_of(to, here.z) - 2 * which for to in self.to]
        self.keeps = which == 0
        self.own_slot = here.z % 2
        self.base = wires.block(self.SEMS)

    def cols(self, x):
        cols = self.shard.shape[1]
        return pl.ds(pl.multiple_of(x * cols, LANES), cols) if self.here.split else pl.ds(0, cols)

    def spread(self):
        src, cols = self.shard.at[self.carried, :], self.cols(self.here.x)
        return [
            self.wires.remote(self.base + i, src, self.full.at[slot, self.carried, cols], {"tp": to})
            for i, (to, slot) in enumerate(zip(self.to, self.slots))
        ]

    def kept(self):
        if not self.keeps:
            return []
        dst = self.full.at[self.own_slot, self.carried, self.cols(self.here.x)]
        return [self.wires.local(self.base + 2, self.shard.at[self.carried, :], dst)]

    def crossed(self):
        if not self.here.split:
            return []
        block = self.full.at[:, self.carried, self.cols(self.here.x)]
        return [self.wires.remote(self.base + 3, block, block, self.here.to_x)]

    def level(self):
        block = self.full.at[:, self.mine, :]
        return [self.wires.remote(self.base + 4, block, block, self.here.to_y)]

    def pooled(self):
        block = self.full.at[:, self.carried, :]
        return [self.wires.remote(self.base + 5, block, block, self.here.to_core)]

    def passed(self):
        block = self.full.at[:, self.theirs, :]
        return [self.wires.remote(self.base + 6, block, block, self.here.to_core)]

    def stage(self, number):
        if number == 0:
            started(self.spread())
            started(self.kept())
        elif number == 1:
            landed(self.spread())
            self.wires.done(self.kept())
            started(self.crossed())
        elif number == 2:
            landed(self.crossed())
            started(self.level())
            started(self.pooled())
        elif number == 3:
            landed(self.level())
            started(self.passed())
        else:
            landed(self.pooled())
            landed(self.passed())

    def close(self):
        for copy in self.spread() + self.crossed() + self.level() + self.pooled() + self.passed():
            copy.wait_send()


def fire(jobs, *events):
    for event in events:
        jobs[event % 100].stage(event // 100)


def between(jobs, table):
    def after(t):
        for step, events in table.items():
            pl.when(t == step)(functools.partial(fire, jobs, *events))

    return after


class Reduce:
    SEMS = 5

    def __init__(self, grad, out, bufs, wires, here):
        self.grad, self.out, self.wires, self.here = grad, out, wires, here
        self.a, self.b, self.d, self.e = bufs
        rows = grad.shape[2] // 2
        self.keep = pl.ds(rows * here.k, rows)
        self.give = pl.ds(rows * (1 - here.k), rows)
        self.zs = here.z % 2
        self.base = wires.block(self.SEMS)

    @staticmethod
    def scratch(shape, n_shard):
        k, two, rows, width = shape
        cols = width // n_shard if n_shard == 2 else width
        half = rows // 2
        return [pltpu.VMEM(s, BF16) for s in ((k, two, half, width), (k, two, half, cols), (k, half, cols), (k, half, cols))]

    def cols(self, x):
        cols = self.out.shape[2]
        return pl.ds(pl.multiple_of(x * cols, LANES), cols)

    def copy(self, number):
        h, remote = self.here, self.wires.remote
        if number == 0:
            return remote(self.base, self.grad.at[:, :, self.give, :], self.a, h.to_core)
        if number == 1:
            return remote(self.base + 1, self.a.at[:, :, :, self.cols(1 - h.x)], self.b, h.to_x)
        if number == 2:
            return remote(self.base + 2, self.b.at[:, 1 - self.zs, :, :], self.d, h.to_mate)
        if number == 3:
            return remote(self.base + 3, self.d, self.e, h.to_y)
        done = self.out.at[:, self.keep, :]
        return remote(self.base + 4, done, done, h.to_core)

    def stage(self, number):
        if number > 0 and (self.here.split or number != 2):
            self.copy(number - 1).wait_recv()
        if number == 1:
            total = (self.grad[:, :, self.keep, :].astype(F32) + self.a[...].astype(F32)).astype(BF16)
            if not self.here.split:
                self.b[...] = total
                return
            self.a[...] = total
        elif number == 2 and self.here.split:
            self.b[...] = (self.a[:, :, :, self.cols(self.here.x)].astype(F32) + self.b[...].astype(F32)).astype(BF16)
        elif number == 3:
            self.d[...] = (self.b[:, self.zs, :, :].astype(F32) + self.d[...].astype(F32)).astype(BF16)
        elif number == 4:
            self.out[:, self.keep, :] = (self.d[...].astype(F32) + self.e[...].astype(F32)).astype(BF16)
        if number < 5:
            self.copy(number).start()

    def close(self):
        for number in range(5):
            if self.here.split or number != 1:
                self.copy(number).wait_send()


def front_kernel(n_shard, len_ref, x_ref, cot_hbm, gains_ref, *refs):
    shards, tables, refs = refs[:4], refs[4:8], refs[8:]
    saved, (layer_all, gains, dctx, gml, gg, dwm, dwi, dwo), refs = refs[:7], refs[7:15], refs[15:]
    wqkv, normed, q, k, v, p, ctx, wo, wi, wm, ext, cot, out, nm, hid, dgu, send, recv = refs
    h = Place(n_shard)
    near = [{"tp": (h.z + i) % 4} for i in (1, 2, 3)] + [{"ctx": (h.c + i) % 4} for i in (1, 2, 3)]
    if h.split:
        near.append(h.to_x)
    h.meet(near)
    wires = Wires(send, recv)
    local = x_ref.shape[2]
    length, pos0, block0 = len_ref[0, h.z % 2], h.c * local, h.c * (local // HALF) - 1
    seq = x_ref.at[0, h.z % 2]
    kept = [wires.own(seq, ext.at[pl.ds(HALF, local), :]), wires.own(cot_hbm.at[0, h.z % 2], cot)]
    rims = [
        wires.go(seq.at[pl.ds(0, HALF), :], ext.at[pl.ds(HALF + local, HALF), :], h.to_prev),
        wires.go(seq.at[pl.ds(local - HALF, HALF), :], ext.at[pl.ds(0, HALF), :], h.to_next),
    ]
    if h.split:
        cols = gains_ref.shape[1]
        mine = gains.at[:, pl.ds(pl.multiple_of(h.x * cols, LANES), cols)]
        kept.append(wires.own(gains_ref, mine))
        rims.append(wires.go(gains_ref, mine, h.to_x))
    else:
        kept.append(wires.own(gains_ref, gains))
    jobs = [Gather(shards[0].at[i], wqkv.at[which, i], which, wires, h) for which in range(2) for i in range(3)]
    jobs += [Gather(shards[1].at[0], wo.at[which], which, wires, h) for which in range(2)]
    for which in range(2):
        jobs += [Gather(shards[2].at[i], wi.at[which, i], which, wires, h) for i in range(2)]
        jobs.append(Gather(shards[3].at[0], wm.at[which], which, wires, h))
    stream = Stream(wires, h, out, layer_all, 2 * TILE, FRONT_BLOCKS)
    fire(jobs, *range(14))
    wires.done(kept)
    landed(rims)
    phase_norm(ext, gains, normed)
    fire(jobs, *FORWARD[0])
    qkv = functools.partial(phase_qkv, normed, wqkv, tables, q, k, v, block0, 384)
    attend = functools.partial(phase_attend, q, k, v, p, ctx, pos0, length)
    tiles = local // TILE
    half = p.shape[1] // 2
    qkv(0, between(jobs, FORWARD[1]))
    attend(range(half), 0, tiles, between(jobs, FORWARD[2]))
    qkv(1, between(jobs, FORWARD[3]))
    attend(range(half, 2 * half), 0, tiles, between(jobs, FORWARD[4]))
    stores = [wires.own(src, dst) for src, dst in zip((wqkv, normed, q, k, v, p, ctx), saved)]
    width = wo.shape[-1]
    wo = wo.reshape(-1, width)
    wi_near, wi_far = (wi.at[i].reshape(-1, width) for i in range(2))
    wm_near, wm_far = (wm.at[i].reshape(-1, width) for i in range(2))
    rows = 2 * TILE
    wis, wms = (wi_near, wi_far), (wm_near, wm_far)
    phase_mlp(ext, cot, ctx, gains, wo, wis, wms, out, gml, nm, hid, dgu, dctx, gg, pos0, length, rows, between(jobs, FORWARD[5]), stream.start)
    weight_grad(hid, cot[...], dwm, 192)
    weight_grad(dgu, nm[...], dwi, 384)
    weight_grad(ctx, gml[...], dwo, LANES, count=dwo.shape[0])
    wires.done(stores)
    stream.finish()
    for job in jobs:
        job.close()
    wires.close()


def back_kernel(n_shard, gains_ref, gain2, *refs):
    tables, homes, (x_ref, layer_in), outs, refs = refs[:4], refs[4:16], refs[16:18], refs[18:25], refs[25:]
    layer_all, input_all, out_qkv, out_wi, out_wm, out_wo, out_gain = outs
    q, k, v, p, ctx, dctx, gml, normed, wqkv, dwi, dwm, dwo, x = refs[:13]
    dk, dv, dqkv, given, rim_out, rim_in, dw, gg, gbuf, send, recv = refs[13:24]
    bufs = refs[24:]
    h = Place(n_shard)
    wires = Wires(send, recv)
    q_home, k_home, v_home, p_home, ctx_home, dctx_home, gml_home, normed_home, wqkv_home, dwi_home, dwm_home, dwo_home = homes
    local, width = x.shape
    block0 = h.c * (local // HALF) - 1
    tiles = local // TILE
    loads = [wires.own(src, dst) for src, dst in ((k_home, k), (v_home, v), (q_home, q), (dctx_home, dctx), (ctx_home, ctx))]
    order = [tiles - 1, *range(tiles - 1)]
    tile_loads = {t: wires.own(p_home.at[t], p.at[t]) for t in order[:3]}
    grad_loads = [wires.own(src, dst) for src, dst in ((dwi_home, dwi), (dwm_home, dwm), (dwo_home, dwo))]
    tile_loads.update({t: wires.own(p_home.at[t], p.at[t]) for t in order[3:]})
    late_loads = [wires.own(src, dst) for src, dst in ((x_ref.at[0, h.z % 2], x), (gml_home, gml), (wqkv_home, wqkv), (normed_home, normed))]
    near = [h.to_mate] + [{"ctx": (h.c + i) % 4} for i in (1, 2, 3)]
    if h.split:
        near.append(h.to_x)
    h.meet(near)
    dw_parts = [(dwi.at[pl.ds(0, 1)], out_wi.at[pl.ds(0, 1)]), (dwi.at[pl.ds(1, 1)], out_wi.at[pl.ds(1, 1)]), (dwm, out_wm), (dwo, out_wo)]
    dw_parts += [(dw.at[pl.ds(i, 1)], out_qkv.at[pl.ds(i, 1)]) for i in range(3)] + [(gbuf, out_gain)]
    jobs = [Reduce(g, o, bufs[4 * i : 4 * i + 4], wires, h) for i, (g, o) in enumerate(dw_parts)]
    rows = 2 * TILE
    last = Stream(wires, h, None, layer_all, rows, local // rows)
    for t in range(FRONT_BLOCKS, last.count):
        last.remote(t).start()
    stream = Stream(wires, h, given, input_all, rows, local // rows)
    dk[...] = jnp.zeros_like(dk)
    dv[...] = jnp.zeros_like(dv)
    gg[...] = jnp.zeros_like(gg)
    wires.done(loads)
    wires.done(tile_loads[t] for t in order[:2])
    weights = wqkv.reshape(-1, width)

    def back(lo, hi, table):
        phase_attend_back(q, k, v, p, ctx, dctx, tables, dqkv, dk, dv, block0, lo, hi, between(jobs, table))

    def pack(lo, hi):
        phase_pack(dk, dv, tables, dqkv, block0, lo, hi)

    def finish(i):
        phase_input(x, gml, gains_ref, weights, dqkv, given, gg, i * rows, rows)

    wires.done(grad_loads)
    fire(jobs, 0, 1, 2, 3)
    back(tiles - 1, tiles, {})
    fire(jobs, 100, 101)
    back(0, 1, {})
    ext = local + 2 * HALF
    for i, ref in enumerate((dk, dv)):
        rim_out[0, i] = ref[:HALF, :].astype(BF16)
        rim_out[1, i] = ref[ext - HALF :, :].astype(BF16)
    rims = [wires.go(rim_out.at[0], rim_in.at[0], h.to_prev), wires.go(rim_out.at[1], rim_in.at[1], h.to_next)]
    fire(jobs, 102, 103)
    wires.done(tile_loads[t] for t in order[2:])
    back(1, tiles - 1, {4: (200,), 6: (201,)})
    landed(rims)
    for i, ref in enumerate((dk, dv)):
        ref[HALF : 2 * HALF, :] += rim_in[1, i].astype(F32)
        ref[ext - 2 * HALF : ext - HALF, :] += rim_in[0, i].astype(F32)
    pack(0, tiles)
    wires.done(late_loads)
    finish(0)
    stream.start(0)
    half = width // 2
    own = normed[HALF : HALF + local, :]
    for i in range(3):
        weight_grad(dqkv, own, dw.at[i].reshape(half, width), LANES, at=i * half, count=half)
        fire(jobs, 4 + i)
    fire(jobs, 202, 203)
    finish(1)
    stream.start(1)
    fire(jobs, 104, 105, 106)
    finish(2)
    finish(3)
    gain_rows = jnp.concatenate([gg[...], gain2[...]], axis=0).astype(BF16)
    gain_rows = jnp.concatenate([gain_rows, gain_rows], axis=0)
    gbuf[0, 0] = gain_rows
    gbuf[0, 1] = gain_rows
    fire(jobs, 7, 300, 301, 107, 204, 205, 207, 206)
    stream.start(2)
    stream.start(3)
    fire(jobs, 302, 303, 400, 401, 402, 403, 304, 305, 307, 306, 500, 501, 502, 503, 404, 405, 407, 406, 504, 505, 507, 506)
    stream.finish()
    for t in range(FRONT_BLOCKS, last.count):
        last.remote(t).wait()
    for job in jobs:
        job.close()
    wires.close()


def last_kernel(layer_ref, input_ref, *refs):
    *refs, layer_buf, input_buf, sems = refs
    n = len(refs) // 2 - 1
    grads, (layer_out, input_out), outs = refs[:n], refs[n : n + 2], refs[n + 2 :]
    ways = ((layer_ref, layer_buf, layer_out), (input_ref, input_buf, input_out))
    parts = [(i, j, pl.ds(j * 4 * TILE, 4 * TILE)) for i in range(2) for j in range(layer_buf.shape[0] // (4 * TILE))]
    loads = [pltpu.make_async_copy(ways[i][0].at[rows, :], ways[i][1].at[rows, :], sems.at[0, i, j]) for i, j, rows in parts]
    stores = [pltpu.make_async_copy(ways[i][1].at[rows, :], ways[i][2].at[rows, :], sems.at[1, i, j]) for i, j, rows in parts]
    started(loads)
    for grad, out in zip(grads, outs):
        out[...] = grad[...].astype(F32)
    for load, store in zip(loads, stores):
        load.wait()
        store.start()
    Wires.done(stores)


def on_device(inputs, lengths, attn_gain, mlp_gain, qkv_weight, attn_weight, mlp_in_weight, mlp_out_weight, cotangent):
    n_tp = lax.axis_size("tp")
    n_ctx = lax.axis_size("ctx")
    tp = lax.axis_index("tp")
    ctx = lax.axis_index("ctx")
    seqs, local = inputs.shape[1], inputs.shape[2]
    width = inputs.shape[3]
    group = n_tp // 2
    mine = tp % seqs
    pair = tp // 2
    tables = tuple(jnp.asarray(t) for t in rope_constants(local * n_ctx))

    n_shard = lax.axis_size("shard")
    shards = [jnp.transpose(qkv_weight, (1, 2, 0)), attn_weight[None], jnp.transpose(mlp_in_weight, (1, 2, 0)), mlp_out_weight[None]]
    gains = jnp.pad(jnp.stack([attn_gain, mlp_gain]), ((0, 14), (0, 0)))
    if n_shard != 2:
        shards = [lax.all_gather(s, "shard", axis=2, tiled=True) for s in shards]
        gains = lax.all_gather(gains, "shard", axis=1, tiled=True)
    hbm = pl.BlockSpec(memory_space=pl.ANY)
    vmem = pl.BlockSpec(memory_space=pltpu.VMEM)
    smem = pl.BlockSpec(memory_space=pltpu.SMEM)
    ext = local + 2 * HALF
    tiles = local // TILE
    chunks = width // LANES
    span = TILE + 2 * HALF
    wide = ((ext, width), BF16)
    tall = ((local, width), BF16)
    heads_rows, ff_rows = attn_weight.shape[0], mlp_out_weight.shape[0]
    full_shapes = [(2, 2, heads_rows, width), (2, 2, 2, ff_rows, width), (2, 2, ff_rows, width)]
    ff_half = 2 * mlp_out_weight.shape[0]
    width_half = width // 2
    saved = [
        ((2, 3, 2, shards[0].shape[1], width), BF16),
        wide, wide, wide, wide,
        ((tiles, chunks, 2 * TILE, span), BF16),
        tall,
    ]
    outs = [
        ((16, width), BF16),
        tall, tall,
        ((8, width), F32),
        ((ff_half, width), BF16), ((2 * ff_half, width), BF16), ((width_half, width), BF16),
    ]
    both = ((seqs, local, width), BF16)
    copies = 14 * Gather.SEMS + 24
    results = pl.pallas_call(
        functools.partial(front_kernel, n_shard),
        out_shape=[jax.ShapeDtypeStruct(*o) for o in saved + [both] + outs],
        in_specs=[smem] + [hbm] * 7 + [vmem] * 4,
        out_specs=[hbm] * 8 + [vmem] * 7,
        scratch_shapes=[pltpu.VMEM(*o) for o in saved]
        + [pltpu.VMEM(f, BF16) for f in full_shapes]
        + [
            pltpu.VMEM(*wide),
            pltpu.VMEM(*tall),
            pltpu.VMEM(*tall),
            pltpu.VMEM(*tall),
            pltpu.VMEM((local, ff_half), BF16),
            pltpu.VMEM((local, 2 * ff_half), BF16),
            pltpu.SemaphoreType.DMA((copies,)),
            pltpu.SemaphoreType.DMA((copies,)),
        ],
        compiler_params=pltpu.CompilerParams(collective_id=0, has_side_effects=True, vmem_limit_bytes=VMEM_LIMIT),
        name="front",
    )(lengths, inputs, cotangent, gains, *shards, *tables)
    wqkv, normed, q, k, v, probs, context, layer_all, gains, dctx, gml, gain2_part, dwm, dwi, dwo = results
    cols = width // n_shard if n_shard == 2 else width
    grads = [(3, 2, width_half // 2, width), (2, 2, ff_half // 2, width), (1, 2, ff_half // 2, width), (1, 2, width_half // 2, width), (1, 2, 32, width)]
    dwi, dwm, dwo = (g.reshape(shape) for g, shape in zip((dwi, dwm, dwo), grads[1:]))
    jobs = [(1, *grads[1][1:])] * 2 + grads[2:4] + [(1, *grads[0][1:])] * 3 + grads[4:]
    sends = 96
    homes = (q, k, v, probs, context, dctx, gml, normed, wqkv, dwi, dwm, dwo)
    layer_out, input_grad, *owned = pl.pallas_call(
        functools.partial(back_kernel, n_shard),
        out_shape=[jax.ShapeDtypeStruct(*both)] * 2 + [jax.ShapeDtypeStruct((g[0], g[2], cols), BF16) for g in grads],
        in_specs=[vmem] * 6 + [hbm] * 14,
        out_specs=[hbm] * 2 + [vmem] * len(grads),
        input_output_aliases={19: 0},
        scratch_shapes=[pltpu.VMEM(a.shape, a.dtype) for a in homes]
        + [
            pltpu.VMEM(*tall),
            pltpu.VMEM((ext, width), F32),
            pltpu.VMEM((ext, width), F32),
            pltpu.VMEM((local, 3 * width), BF16),
            pltpu.VMEM(*tall),
            pltpu.VMEM((2, 2, HALF, width), BF16),
            pltpu.VMEM((2, 2, HALF, width), BF16),
            pltpu.VMEM(grads[0], BF16),
            pltpu.VMEM((8, width), F32),
            pltpu.VMEM(grads[4], BF16),
            pltpu.SemaphoreType.DMA((sends,)),
            pltpu.SemaphoreType.DMA((sends,)),
        ]
        + [b for g in jobs for b in Reduce.scratch(g, n_shard)],
        compiler_params=pltpu.CompilerParams(collective_id=1, has_side_effects=True, vmem_limit_bytes=VMEM_LIMIT),
        name="back",
    )(gains, gain2_part, *tables, *homes, inputs, layer_all)
    gain_sums = owned.pop()
    flat = jax.ShapeDtypeStruct((seqs * local, width), BF16)
    layer_out, input_grad, *owned = pl.pallas_call(
        last_kernel,
        out_shape=[flat] * 2 + [jax.ShapeDtypeStruct(g.shape, F32) for g in owned],
        in_specs=[hbm] * 2 + [vmem] * len(owned),
        out_specs=[hbm] * 2 + [vmem] * len(owned),
        scratch_shapes=[pltpu.VMEM(flat.shape, BF16), pltpu.VMEM(flat.shape, BF16), pltpu.SemaphoreType.DMA((2, 2, flat.shape[0] // (4 * TILE)))],
        compiler_params=pltpu.CompilerParams(vmem_limit_bytes=VMEM_LIMIT),
        name="last",
    )(layer_out.reshape(flat.shape), input_grad.reshape(flat.shape), *owned)
    layer_out, input_grad = (a.reshape(both[0]) for a in (layer_out, input_grad))
    owned.append(gain_sums.astype(F32))
    if n_shard != 2:
        owned = [lax.psum_scatter(g, "shard", scatter_dimension=2, tiled=True) for g in owned]
    qkv_grad = jnp.transpose(owned[0], (2, 0, 1))
    mlp_in_grad = jnp.transpose(owned[1], (2, 0, 1))
    mlp_out_grad, attn_grad = owned[2][0], owned[3][0]
    share = owned[4].shape[2] // n_tp
    gains = lax.dynamic_slice_in_dim(owned[4][0, :16], tp * share, share, axis=1)
    gains = jnp.sum(gains.reshape(2, 8, share), axis=1)
    return (layer_out[None], input_grad[None], qkv_grad, attn_grad, mlp_in_grad, mlp_out_grad, gains[0], gains[1])


def solution(mesh):
    in_specs = (
        P("shard", None, "ctx", None),
        P("shard", None),
        P("shard"),
        P("shard"),
        P("shard", None, "tp"),
        P("tp", "shard"),
        P("shard", None, "tp"),
        P("tp", "shard"),
        P("shard", None, "ctx", None),
    )
    out_specs = (
        P("shard", None, "ctx", None),
        P("shard", None, "ctx", None),
        P("shard", None, "tp"),
        P("tp", "shard"),
        P("shard", None, "tp"),
        P("tp", "shard"),
        P(("shard", "tp")),
        P(("shard", "tp")),
    )
    return jax.shard_map(on_device, mesh=mesh, in_specs=in_specs, out_specs=out_specs, check_vma=False)
```

```python
import functools
import math

import numpy as np

import jax
import jax.numpy as jnp
from jax import lax
from jax.experimental import pallas as pl
from jax.experimental.pallas import tpu as pltpu
from jax.sharding import PartitionSpec as P

HD = 64
HALF = 64
TILE = 128
LANES = 128
norm_eps = 1e-05
rope_base = 10000.0
masked_score = -1e30
F32 = jnp.float32
BF16 = jnp.bfloat16
FRONT_BLOCKS = 2
FORWARD = (
    (100, 101, 102, 106, 103, 200, 201, 104, 202, 300, 206, 400, 301, 105, 203, 401, 302, 204, 402, 306),
    {0: (107, 108, 109, 110), 1: (303, 205), 2: (304,)},
    {1: (207,), 2: (305, 111), 4: (208,), 5: (307,), 6: (209,), 7: (403, 404, 405)},
    {0: (112,), 1: (308, 210)},
    {1: (309, 211), 2: (113,), 3: (212, 310), 6: (311,), 7: (406, 407, 408, 409, 410, 213)},
    {0: (312, 313, 411, 412, 413)},
)
VMEM_LIMIT = 60 * 1024 * 1024


def nt(a, b):
    return lax.dot_general(a, b, (((1,), (1,)), ((), ())), preferred_element_type=F32)


def nn(a, b):
    return lax.dot_general(a, b, (((1,), (0,)), ((), ())), preferred_element_type=F32)


def tn(a, b):
    return lax.dot_general(a, b, (((0,), (0,)), ((), ())), preferred_element_type=F32)


def rope_constants(seq):
    w = rope_base ** (-np.arange(0, HD, 2) / HD)
    w = np.tile(w, 2 * LANES // HD)
    rows = np.arange(TILE)[:, None] * w
    blocks = (np.arange(seq // HALF + 4)[:, None] - 1) * HALF * w
    tables = (np.cos(rows), np.sin(rows), np.cos(blocks), np.sin(blocks))
    return tuple(t.astype(np.float32) for t in tables)


def rope_tile(tables, block):
    cos_r, sin_r, cos_b, sin_b = tables
    cb = cos_b[pl.ds(block + 1, 1), :]
    sb = sin_b[pl.ds(block + 1, 1), :]
    cr = cos_r[...]
    sr = sin_r[...]
    cosine = cr * cb - sr * sb
    sine = sr * cb + cr * sb
    first = lax.broadcasted_iota(jnp.int32, sine.shape, 1) % HD < HD // 2
    return cosine, jnp.where(first, -sine, sine), first


def turn(u, cosine, sine, first):
    other = jnp.where(first, pltpu.roll(u, LANES - HD // 2, 1), pltpu.roll(u, HD // 2, 1))
    return u * cosine + other * sine


def layer_stats(z):
    center = z - jnp.mean(z, axis=-1, keepdims=True)
    inv = lax.rsqrt(jnp.mean(center * center, axis=-1, keepdims=True) + norm_eps)
    return center * inv, inv


def layer_back(e, xhat, inv):
    return (e - jnp.mean(e, axis=-1, keepdims=True) - xhat * jnp.mean(e * xhat, axis=-1, keepdims=True)) * inv


def head_masks(shape):
    lane = lax.broadcasted_iota(jnp.int32, shape, 1)
    return lane < HD


def split_heads(c, low_head):
    zero = jnp.zeros_like(c)
    return jnp.concatenate([jnp.where(low_head, c, zero), jnp.where(low_head, zero, c)], axis=0)


def phase_norm(x_ref, gain_ref, normed_ref):
    def body(t, carry):
        r0 = pl.multiple_of(t * TILE, TILE)
        xhat, _ = layer_stats(x_ref[pl.ds(r0, TILE), :].astype(F32))
        normed_ref[pl.ds(r0, TILE), :] = (xhat * gain_ref[:1, :].astype(F32)).astype(BF16)
        return carry

    lax.fori_loop(0, x_ref.shape[0] // TILE, body, 0)


def phase_qkv(normed_ref, w_ref, tables, q_ref, k_ref, v_ref, block0, rows, which, after):
    width = normed_ref.shape[1]
    half = width // 2
    scaling = 1.0 / math.sqrt(HD)

    def body(t, carry):
        r0 = pl.multiple_of(t * rows, rows)
        out = nt(normed_ref[pl.ds(r0, rows), :], w_ref[which].reshape(3 * half, width))
        for s in range(rows // TILE):
            here = pl.ds(r0 + s * TILE, TILE)
            cosine, sine, first = rope_tile(tables, block0 + t * (rows // HALF) + s * (TILE // HALF))
            for part, ref in enumerate((q_ref, k_ref)):
                if part == 0:
                    turns = cosine * scaling, sine * scaling, first
                else:
                    turns = cosine, sine, first
                for j in range(half // LANES):
                    u = out[s * TILE : (s + 1) * TILE, part * half + j * LANES : part * half + (j + 1) * LANES]
                    ref[here, which * half + j * LANES : which * half + (j + 1) * LANES] = turn(u, *turns).astype(BF16)
        v_ref[pl.ds(r0, rows), which * half : (which + 1) * half] = out[:, 2 * half :].astype(BF16)
        after(t)
        return carry

    lax.fori_loop(0, normed_ref.shape[0] // rows, body, 0)


def phase_attend(q_ref, k_ref, v_ref, p_ref, ctx_ref, pos0, length, chunks, lo, hi, after):
    span = TILE + 2 * HALF

    def body(t, carry):
        r0 = pl.multiple_of(t * TILE, TILE)
        row = lax.broadcasted_iota(jnp.int32, (TILE, span), 0)
        col = lax.broadcasted_iota(jnp.int32, (TILE, span), 1)
        offset = col - row
        key_pos = pos0 + t * TILE - HALF + col
        allowed = (offset >= 0) & (offset <= 2 * HALF) & (key_pos >= 0) & ((key_pos < length) | (offset == HALF))
        bias = jnp.where(allowed, 0.0, masked_score).astype(F32)
        bias = jnp.concatenate([bias, bias], axis=0)
        low_head = head_masks((TILE, LANES))
        lanes = [slice(j * LANES, (j + 1) * LANES) for j in chunks]
        queries = [split_heads(q_ref[pl.ds(r0 + HALF, TILE), at], low_head) for at in lanes]
        scores = [nt(q2, k_ref[pl.ds(r0, span), at]) + bias for q2, at in zip(queries, lanes)]
        terms = [jnp.exp(s - jnp.max(s, axis=-1, keepdims=True)) for s in scores]
        probs = [(e * (1.0 / jnp.sum(e, axis=-1, keepdims=True))).astype(BF16) for e in terms]
        outs = [nn(p, v_ref[pl.ds(r0, span), at]) for p, at in zip(probs, lanes)]
        for j, p, out, at in zip(chunks, probs, outs, lanes):
            p_ref[t, j] = p
            ctx_ref[pl.ds(r0, TILE), at] = jnp.where(low_head, out[:TILE], out[TILE:]).astype(BF16)
        after(t)
        return carry

    lax.fori_loop(lo, hi, body, 0)


def units(nm, grad_low, wg, wu, wm):
    gate = nt(nm, wg)
    up = nt(nm, wu)
    cdf = 0.5 + 0.5 * lax.erf(gate * math.sqrt(0.5))
    gelu = gate * cdf
    slope = cdf + gate * (jnp.exp(-0.5 * gate * gate) * (1.0 / math.sqrt(2.0 * math.pi)))
    grad_hidden = nt(grad_low, wm)
    return (gelu * up).astype(BF16), (grad_hidden * up * slope).astype(BF16), (grad_hidden * gelu).astype(BF16)


def phase_mlp(x_ref, cot_ref, ctx_ref, gain_ref, wo_ref, wi_refs, wm_refs, out_ref, gml_ref, nm_ref, hid_ref, dgu_ref, dctx_ref, gg_ref, pos0, length, rows, between_halves, ready):
    half = wm_refs[0].shape[0]
    gg_ref[...] = jnp.zeros_like(gg_ref)

    def body(t, carry):
        r0 = pl.multiple_of(t * rows, rows)
        here = pl.ds(r0, rows)
        gain = gain_ref[1:2, :].astype(F32)
        middle = x_ref[pl.ds(r0 + HALF, rows), :].astype(F32) + nn(ctx_ref[here, :], wo_ref[...])
        xhat, inv = layer_stats(middle)
        nm = (xhat * gain).astype(BF16)
        nm_ref[here, :] = nm
        valid = pos0 + r0 + lax.broadcasted_iota(jnp.int32, (rows, 1), 0) < length
        grad_low = jnp.where(valid, cot_ref[here, :].astype(F32), 0.0).astype(BF16)
        cot_ref[here, :] = grad_low
        wg, wu, wm = wi_refs[0][:half, :], wi_refs[0][half:, :], wm_refs[0][...]
        hidden, grad_gate, grad_up = units(nm, grad_low, wg, wu, wm)
        hid_ref[here, :] = hidden
        dgu_ref[here, :half] = grad_gate
        dgu_ref[here, half:] = grad_up
        mlp = nn(hidden, wm)
        grad_nm = nn(grad_gate, wg) + nn(grad_up, wu)
        between_halves(t)
        wg, wu, wm = wi_refs[1][:half, :], wi_refs[1][half:, :], wm_refs[1][...]
        hidden, grad_gate, grad_up = units(nm, grad_low, wg, wu, wm)
        out_ref[here, :] = jnp.where(valid, middle + (mlp + nn(hidden, wm)), 0.0).astype(BF16)
        ready(t)
        grad_nm = grad_nm + nn(grad_gate, wg) + nn(grad_up, wu)
        gg_ref[...] += jnp.sum((grad_nm * xhat).reshape(rows // 8, 8, -1), axis=0)
        gm_low = (grad_low.astype(F32) + layer_back(grad_nm * gain, xhat, inv)).astype(BF16)
        gml_ref[here, :] = gm_low
        dctx_ref[here, :] = nt(gm_low, wo_ref[...]).astype(BF16)
        return carry

    lax.fori_loop(0, ctx_ref.shape[0] // rows, body, 0)


def phase_attend_back(q_ref, k_ref, v_ref, p_ref, ctx_ref, dctx_ref, tables, dqkv_ref, dk_ref, dv_ref, block0, lo, hi, after):
    width = q_ref.shape[1]
    half = width // 2
    span = TILE + 2 * HALF
    scaling = 1.0 / math.sqrt(HD)

    def body(t, carry):
        r0 = pl.multiple_of(t * TILE, TILE)
        low_head = head_masks((TILE, LANES))
        cosine, sine, first = rope_tile(tables, block0 + 1 + t * (TILE // HALF))
        cosine, sine = cosine * scaling, sine * -scaling
        keys = pl.ds(r0, span)
        for j in range(width // LANES):
            lanes = slice(j * LANES, (j + 1) * LANES)
            probs = p_ref[t, j]
            kc = k_ref[keys, lanes]
            dc = dctx_ref[pl.ds(r0, TILE), lanes]
            row_term = dc.astype(F32) * ctx_ref[pl.ds(r0, TILE), lanes].astype(F32)
            row_low = jnp.sum(jnp.where(low_head, row_term, 0.0), axis=-1, keepdims=True)
            row_high = jnp.sum(jnp.where(low_head, 0.0, row_term), axis=-1, keepdims=True)
            row_term = jnp.concatenate([row_low, row_high], axis=0)
            dc2 = split_heads(dc, low_head)
            grad_probs = nt(dc2, v_ref[keys, lanes])
            grad_scores = (probs.astype(F32) * (grad_probs - row_term)).astype(BF16)
            dq2 = nn(grad_scores, kc)
            dq = jnp.where(low_head, dq2[:TILE], dq2[TILE:])
            at = 3 * half * (j * LANES // half) + j * LANES % half
            dqkv_ref[pl.ds(r0, TILE), at : at + LANES] = turn(dq, cosine, sine, first).astype(BF16)
            q2 = split_heads(q_ref[pl.ds(r0 + HALF, TILE), lanes], low_head)
            dk_ref[keys, lanes] += tn(grad_scores, q2)
            dv_ref[keys, lanes] += tn(probs, dc2)
        after(t)
        return carry

    lax.fori_loop(lo, hi, body, 0)


def phase_pack(dk_ref, dv_ref, tables, dqkv_ref, block0, lo, hi):
    width = dk_ref.shape[1]
    half = width // 2

    def body(t, carry):
        r0 = pl.multiple_of(t * TILE, TILE)
        cosine, sine, first = rope_tile(tables, block0 + 1 + t * (TILE // HALF))
        ext = pl.ds(r0 + HALF, TILE)
        for j in range(width // LANES):
            lanes = slice(j * LANES, (j + 1) * LANES)
            at = 3 * half * (j * LANES // half) + j * LANES % half
            dqkv_ref[pl.ds(r0, TILE), at + half : at + half + LANES] = turn(dk_ref[ext, lanes], cosine, -sine, first).astype(BF16)
            dqkv_ref[pl.ds(r0, TILE), at + 2 * half : at + 2 * half + LANES] = dv_ref[ext, lanes].astype(BF16)
        return carry

    lax.fori_loop(lo, hi, body, 0)


def phase_input(x_ref, gm_ref, gain_ref, w_ref, dqkv_ref, out_ref, gg_ref, r0, rows):
    here = pl.ds(r0, rows)
    gain = gain_ref[:1, :].astype(F32)
    grad_normed = nn(dqkv_ref[here, :], w_ref[...])
    xhat, inv = layer_stats(x_ref[here, :].astype(F32))
    gg_ref[...] += jnp.sum((grad_normed * xhat).reshape(rows // 8, 8, -1), axis=0)
    out_ref[here, :] = (gm_ref[here, :].astype(F32) + layer_back(grad_normed * gain, xhat, inv)).astype(BF16)


def weight_grad(a_ref, b, out_ref, columns, at=0, count=None):
    for c in range(0, a_ref.shape[1] if count is None else count, columns):
        out_ref[c : c + columns, :] = tn(a_ref[:, at + c : at + c + columns], b).astype(out_ref.dtype)


def slot_of(at, of):
    return (of + 2 * (at // 2)) % 4


class Place:
    def __init__(self, n_shard):
        self.split = n_shard == 2
        self.x = lax.axis_index("shard")
        self.c = lax.axis_index("ctx")
        self.z = lax.axis_index("tp")
        self.k = self.c % 2
        self.y = self.c // 2
        self.up = (self.z + 1) % 4
        self.down = (self.z + 3) % 4
        self.mate = self.z + 1 - 2 * (self.z % 2)
        self.core = self.c + 1 - 2 * self.k
        self.across = (self.c + 2) % 4
        self.to_x = {"shard": 1 - self.x}
        self.to_up = {"tp": self.up}
        self.to_down = {"tp": self.down}
        self.to_mate = {"tp": self.mate}
        self.to_core = {"ctx": self.core}
        self.to_y = {"ctx": self.across}
        self.to_next = {"ctx": (self.c + 1) % 4}
        self.to_prev = {"ctx": (self.c + 3) % 4}

    def meet(self, partners):
        barrier = pltpu.get_barrier_semaphore()
        for device in partners:
            pl.semaphore_signal(barrier, inc=1, device_id=device, device_id_type=pl.DeviceIdType.MESH)
        pl.semaphore_wait(barrier, len(partners))


class Wires:
    def __init__(self, send, recv):
        self.send, self.recv, self.next, self.open = send, recv, 0, []

    def block(self, count):
        base = self.next
        self.next += count
        return base

    def remote(self, i, src, dst, device):
        return pltpu.make_async_remote_copy(
            src_ref=src, dst_ref=dst, send_sem=self.send.at[i], recv_sem=self.recv.at[i], device_id=device, device_id_type=pl.DeviceIdType.MESH
        )

    def local(self, i, src, dst):
        return pltpu.make_async_copy(src, dst, self.recv.at[i])

    def go(self, src, dst, device):
        copy = self.remote(self.block(1), src, dst, device)
        copy.start()
        self.open.append(copy)
        return copy

    def own(self, src, dst):
        copy = self.local(self.block(1), src, dst)
        copy.start()
        return copy

    @staticmethod
    def done(copies):
        for copy in copies:
            copy.wait()

    def close(self):
        for copy in self.open:
            copy.wait_send()


def started(copies):
    for copy in copies:
        copy.start()


class Stream:
    def __init__(self, wires, here, stage, target, rows, sent):
        self.wires, self.here, self.stage, self.target, self.rows, self.sent = wires, here, stage, target, rows, sent
        self.count = target.shape[1] // rows
        self.base = wires.block(2 * self.count)

    def block(self, t):
        rows = pl.ds(pl.multiple_of(t * self.rows, self.rows), self.rows)
        dst = self.target.at[self.here.z % 2, rows, :]
        return dst if self.stage is None else self.stage.at[rows, :], dst

    def remote(self, t):
        return self.wires.remote(self.base + t, *self.block(t), self.here.to_mate)

    def local(self, t):
        return self.wires.local(self.base + self.count + t, *self.block(t))

    def start(self, t):
        self.local(t).start()
        pl.when(t < self.sent)(lambda: self.remote(t).start())

    def finish(self):
        for t in range(self.count):
            self.local(t).wait()
        for t in range(self.sent):
            self.remote(t).wait()


def landed(copies):
    for copy in copies:
        copy.wait_recv()


class Gather:
    SEMS = 7

    def __init__(self, shard, full, which, wires, here):
        self.shard, self.full, self.wires, self.here = shard, full, wires, here
        rows = shard.shape[0] // 6
        self.carried = pl.ds(rows * (3 * here.k + here.y), 2 * rows)
        self.mine = pl.ds(rows * (3 * here.k + 2 * here.y), rows)
        self.theirs = pl.ds(rows * (3 * here.k + 2 - 2 * here.y), rows)
        other = (here.z + 2) % 4
        self.to = [other, other + 1 - 2 * (other % 2)] if which else [here.mate]
        self.slots = [slot_of(to, here.z) - 2 * which for to in self.to]
        self.keeps = which == 0
        self.own_slot = here.z % 2
        self.base = wires.block(self.SEMS)

    def cols(self, x):
        cols = self.shard.shape[1]
        return pl.ds(pl.multiple_of(x * cols, LANES), cols) if self.here.split else pl.ds(0, cols)

    def spread(self):
        src, cols = self.shard.at[self.carried, :], self.cols(self.here.x)
        return [
            self.wires.remote(self.base + i, src, self.full.at[slot, self.carried, cols], {"tp": to})
            for i, (to, slot) in enumerate(zip(self.to, self.slots))
        ]

    def kept(self):
        if not self.keeps:
            return []
        dst = self.full.at[self.own_slot, self.carried, self.cols(self.here.x)]
        return [self.wires.local(self.base + 2, self.shard.at[self.carried, :], dst)]

    def crossed(self):
        if not self.here.split:
            return []
        block = self.full.at[:, self.carried, self.cols(self.here.x)]
        return [self.wires.remote(self.base + 3, block, block, self.here.to_x)]

    def level(self):
        block = self.full.at[:, self.mine, :]
        return [self.wires.remote(self.base + 4, block, block, self.here.to_y)]

    def pooled(self):
        block = self.full.at[:, self.carried, :]
        return [self.wires.remote(self.base + 5, block, block, self.here.to_core)]

    def passed(self):
        block = self.full.at[:, self.theirs, :]
        return [self.wires.remote(self.base + 6, block, block, self.here.to_core)]

    def stage(self, number):
        if number == 0:
            started(self.spread())
            started(self.kept())
        elif number == 1:
            landed(self.spread())
            self.wires.done(self.kept())
            started(self.crossed())
        elif number == 2:
            landed(self.crossed())
            started(self.level())
            started(self.pooled())
        elif number == 3:
            landed(self.level())
            started(self.passed())
        else:
            landed(self.pooled())
            landed(self.passed())

    def close(self):
        for copy in self.spread() + self.crossed() + self.level() + self.pooled() + self.passed():
            copy.wait_send()


def fire(jobs, *events):
    for event in events:
        jobs[event % 100].stage(event // 100)


def between(jobs, table):
    def after(t):
        for step, events in table.items():
            pl.when(t == step)(functools.partial(fire, jobs, *events))

    return after


class Reduce:
    SEMS = 5

    def __init__(self, grad, out, bufs, wires, here):
        self.grad, self.out, self.wires, self.here = grad, out, wires, here
        self.a, self.b, self.d, self.e = bufs
        rows = grad.shape[2] // 2
        self.keep = pl.ds(rows * here.k, rows)
        self.give = pl.ds(rows * (1 - here.k), rows)
        self.zs = here.z % 2
        self.base = wires.block(self.SEMS)

    @staticmethod
    def scratch(shape, n_shard):
        k, two, rows, width = shape
        cols = width // n_shard if n_shard == 2 else width
        half = rows // 2
        return [pltpu.VMEM(s, BF16) for s in ((k, two, half, width), (k, two, half, cols), (k, half, cols), (k, half, cols))]

    def cols(self, x):
        cols = self.out.shape[2]
        return pl.ds(pl.multiple_of(x * cols, LANES), cols)

    def copy(self, number):
        h, remote = self.here, self.wires.remote
        if number == 0:
            return remote(self.base, self.grad.at[:, :, self.give, :], self.a, h.to_core)
        if number == 1:
            return remote(self.base + 1, self.a.at[:, :, :, self.cols(1 - h.x)], self.b, h.to_x)
        if number == 2:
            return remote(self.base + 2, self.b.at[:, 1 - self.zs, :, :], self.d, h.to_mate)
        if number == 3:
            return remote(self.base + 3, self.d, self.e, h.to_y)
        done = self.out.at[:, self.keep, :]
        return remote(self.base + 4, done, done, h.to_core)

    def stage(self, number):
        if number > 0 and (self.here.split or number != 2):
            self.copy(number - 1).wait_recv()
        if number == 1:
            total = (self.grad[:, :, self.keep, :].astype(F32) + self.a[...].astype(F32)).astype(BF16)
            if not self.here.split:
                self.b[...] = total
                return
            self.a[...] = total
        elif number == 2 and self.here.split:
            self.b[...] = (self.a[:, :, :, self.cols(self.here.x)].astype(F32) + self.b[...].astype(F32)).astype(BF16)
        elif number == 3:
            self.d[...] = (self.b[:, self.zs, :, :].astype(F32) + self.d[...].astype(F32)).astype(BF16)
        elif number == 4:
            self.out[:, self.keep, :] = (self.d[...].astype(F32) + self.e[...].astype(F32)).astype(BF16)
        if number < 5:
            self.copy(number).start()

    def close(self):
        for number in range(5):
            if self.here.split or number != 1:
                self.copy(number).wait_send()


def front_kernel(n_shard, len_ref, x_ref, cot_hbm, gains_ref, *refs):
    shards, tables, refs = refs[:4], refs[4:8], refs[8:]
    saved, (layer_all, gains, dctx, gml, gg, dwm, dwi, dwo), refs = refs[:7], refs[7:15], refs[15:]
    wqkv, normed, q, k, v, p, ctx, wo, wi, wm, ext, cot, out, nm, hid, dgu, send, recv = refs
    h = Place(n_shard)
    near = [{"tp": (h.z + i) % 4} for i in (1, 2, 3)] + [{"ctx": (h.c + i) % 4} for i in (1, 2, 3)]
    if h.split:
        near.append(h.to_x)
    h.meet(near)
    wires = Wires(send, recv)
    local = x_ref.shape[2]
    length, pos0, block0 = len_ref[0, h.z % 2], h.c * local, h.c * (local // HALF) - 1
    seq = x_ref.at[0, h.z % 2]
    kept = [wires.own(seq, ext.at[pl.ds(HALF, local), :]), wires.own(cot_hbm.at[0, h.z % 2], cot)]
    rims = [
        wires.go(seq.at[pl.ds(0, HALF), :], ext.at[pl.ds(HALF + local, HALF), :], h.to_prev),
        wires.go(seq.at[pl.ds(local - HALF, HALF), :], ext.at[pl.ds(0, HALF), :], h.to_next),
    ]
    if h.split:
        cols = gains_ref.shape[1]
        mine = gains.at[:, pl.ds(pl.multiple_of(h.x * cols, LANES), cols)]
        kept.append(wires.own(gains_ref, mine))
        rims.append(wires.go(gains_ref, mine, h.to_x))
    else:
        kept.append(wires.own(gains_ref, gains))
    jobs = [Gather(shards[0].at[i], wqkv.at[which, i], which, wires, h) for which in range(2) for i in range(3)]
    jobs += [Gather(shards[1].at[0], wo.at[which], which, wires, h) for which in range(2)]
    for which in range(2):
        jobs += [Gather(shards[2].at[i], wi.at[which, i], which, wires, h) for i in range(2)]
        jobs.append(Gather(shards[3].at[0], wm.at[which], which, wires, h))
    stream = Stream(wires, h, out, layer_all, 2 * TILE, FRONT_BLOCKS)
    fire(jobs, *range(14))
    wires.done(kept)
    landed(rims)
    phase_norm(ext, gains, normed)
    fire(jobs, *FORWARD[0])
    qkv = functools.partial(phase_qkv, normed, wqkv, tables, q, k, v, block0, 384)
    attend = functools.partial(phase_attend, q, k, v, p, ctx, pos0, length)
    tiles = local // TILE
    half = p.shape[1] // 2
    qkv(0, between(jobs, FORWARD[1]))
    attend(range(half), 0, tiles, between(jobs, FORWARD[2]))
    qkv(1, between(jobs, FORWARD[3]))
    attend(range(half, 2 * half), 0, tiles, between(jobs, FORWARD[4]))
    stores = [wires.own(src, dst) for src, dst in zip((wqkv, normed, q, k, v, p, ctx), saved)]
    width = wo.shape[-1]
    wo = wo.reshape(-1, width)
    wi_near, wi_far = (wi.at[i].reshape(-1, width) for i in range(2))
    wm_near, wm_far = (wm.at[i].reshape(-1, width) for i in range(2))
    rows = 2 * TILE
    wis, wms = (wi_near, wi_far), (wm_near, wm_far)
    phase_mlp(ext, cot, ctx, gains, wo, wis, wms, out, gml, nm, hid, dgu, dctx, gg, pos0, length, rows, between(jobs, FORWARD[5]), stream.start)
    weight_grad(hid, cot[...], dwm, 192)
    weight_grad(dgu, nm[...], dwi, 384)
    weight_grad(ctx, gml[...], dwo, LANES, count=dwo.shape[0])
    wires.done(stores)
    stream.finish()
    for job in jobs:
        job.close()
    wires.close()


def back_kernel(n_shard, gains_ref, gain2, *refs):
    tables, homes, (x_ref, layer_in), outs, refs = refs[:4], refs[4:16], refs[16:18], refs[18:25], refs[25:]
    layer_all, input_all, out_qkv, out_wi, out_wm, out_wo, out_gain = outs
    q, k, v, p, ctx, dctx, gml, normed, wqkv, dwi, dwm, dwo, x = refs[:13]
    dk, dv, dqkv, given, rim_out, rim_in, dw, gg, gbuf, send, recv = refs[13:24]
    bufs = refs[24:]
    h = Place(n_shard)
    wires = Wires(send, recv)
    q_home, k_home, v_home, p_home, ctx_home, dctx_home, gml_home, normed_home, wqkv_home, dwi_home, dwm_home, dwo_home = homes
    local, width = x.shape
    block0 = h.c * (local // HALF) - 1
    tiles = local // TILE
    loads = [wires.own(src, dst) for src, dst in ((k_home, k), (v_home, v), (q_home, q), (dctx_home, dctx), (ctx_home, ctx))]
    order = [tiles - 1, *range(tiles - 1)]
    tile_loads = {t: wires.own(p_home.at[t], p.at[t]) for t in order[:3]}
    grad_loads = [wires.own(src, dst) for src, dst in ((dwi_home, dwi), (dwm_home, dwm), (dwo_home, dwo))]
    tile_loads.update({t: wires.own(p_home.at[t], p.at[t]) for t in order[3:]})
    late_loads = [wires.own(src, dst) for src, dst in ((x_ref.at[0, h.z % 2], x), (gml_home, gml), (wqkv_home, wqkv), (normed_home, normed))]
    near = [h.to_mate] + [{"ctx": (h.c + i) % 4} for i in (1, 2, 3)]
    if h.split:
        near.append(h.to_x)
    h.meet(near)
    dw_parts = [(dwi.at[pl.ds(0, 1)], out_wi.at[pl.ds(0, 1)]), (dwi.at[pl.ds(1, 1)], out_wi.at[pl.ds(1, 1)]), (dwm, out_wm), (dwo, out_wo)]
    dw_parts += [(dw.at[pl.ds(i, 1)], out_qkv.at[pl.ds(i, 1)]) for i in range(3)] + [(gbuf, out_gain)]
    jobs = [Reduce(g, o, bufs[4 * i : 4 * i + 4], wires, h) for i, (g, o) in enumerate(dw_parts)]
    rows = 2 * TILE
    last = Stream(wires, h, None, layer_all, rows, local // rows)
    for t in range(FRONT_BLOCKS, last.count):
        last.remote(t).start()
    stream = Stream(wires, h, given, input_all, rows, local // rows)
    dk[...] = jnp.zeros_like(dk)
    dv[...] = jnp.zeros_like(dv)
    gg[...] = jnp.zeros_like(gg)
    wires.done(loads)
    wires.done(tile_loads[t] for t in order[:2])
    weights = wqkv.reshape(-1, width)

    def back(lo, hi, table):
        phase_attend_back(q, k, v, p, ctx, dctx, tables, dqkv, dk, dv, block0, lo, hi, between(jobs, table))

    def pack(lo, hi):
        phase_pack(dk, dv, tables, dqkv, block0, lo, hi)

    def finish(i):
        phase_input(x, gml, gains_ref, weights, dqkv, given, gg, i * rows, rows)

    wires.done(grad_loads)
    fire(jobs, 0, 1, 2, 3)
    back(tiles - 1, tiles, {})
    fire(jobs, 100, 101)
    back(0, 1, {})
    ext = local + 2 * HALF
    for i, ref in enumerate((dk, dv)):
        rim_out[0, i] = ref[:HALF, :].astype(BF16)
        rim_out[1, i] = ref[ext - HALF :, :].astype(BF16)
    rims = [wires.go(rim_out.at[0], rim_in.at[0], h.to_prev), wires.go(rim_out.at[1], rim_in.at[1], h.to_next)]
    fire(jobs, 102, 103)
    wires.done(tile_loads[t] for t in order[2:])
    back(1, tiles - 1, {4: (200,), 6: (201,)})
    landed(rims)
    for i, ref in enumerate((dk, dv)):
        ref[HALF : 2 * HALF, :] += rim_in[1, i].astype(F32)
        ref[ext - 2 * HALF : ext - HALF, :] += rim_in[0, i].astype(F32)
    pack(0, tiles)
    wires.done(late_loads)
    finish(0)
    stream.start(0)
    half = width // 2
    own = normed[HALF : HALF + local, :]
    for i in range(3):
        weight_grad(dqkv, own, dw.at[i].reshape(half, width), LANES, at=i * half, count=half)
        fire(jobs, 4 + i)
    fire(jobs, 202, 203)
    finish(1)
    stream.start(1)
    fire(jobs, 104, 105, 106)
    finish(2)
    finish(3)
    gain_rows = jnp.concatenate([gg[...], gain2[...]], axis=0).astype(BF16)
    gain_rows = jnp.concatenate([gain_rows, gain_rows], axis=0)
    gbuf[0, 0] = gain_rows
    gbuf[0, 1] = gain_rows
    fire(jobs, 7, 300, 301, 107, 204, 205, 207, 206)
    stream.start(2)
    stream.start(3)
    fire(jobs, 302, 303, 400, 401, 402, 403, 304, 305, 307, 306, 500, 501, 502, 503, 404, 405, 407, 406, 504, 505, 507, 506)
    stream.finish()
    for t in range(FRONT_BLOCKS, last.count):
        last.remote(t).wait()
    for job in jobs:
        job.close()
    wires.close()


def last_kernel(n, *refs):
    sources, results, lows, highs, (layer_buf, input_buf, sems) = refs[:n], refs[n : 2 * n], refs[2 * n : 3 * n - 2], refs[3 * n - 2 : 4 * n - 4], refs[4 * n - 4 :]
    parts = []
    for i, (low, high) in enumerate(zip(lows, highs)):
        parts.append((sources[2 + i], low, high, results[2 + i]))
    for i, buf in enumerate((layer_buf, input_buf)):
        for at in range(0, buf.shape[0], 4 * TILE):
            rows = pl.ds(at, 4 * TILE)
            parts.append((sources[i].at[rows, :], buf.at[rows, :], buf.at[rows, :], results[i].at[rows, :]))
    loads = [pltpu.make_async_copy(src, low, sems.at[0, i]) for i, (src, low, _, _) in enumerate(parts)]
    stores = [pltpu.make_async_copy(high, dst, sems.at[1, i]) for i, (_, _, high, dst) in enumerate(parts)]
    started(loads)
    for i, (load, store) in enumerate(zip(loads, stores)):
        load.wait()
        if i < n - 2:
            parts[i][2][...] = parts[i][1][...].astype(F32)
        store.start()
    Wires.done(stores)


def on_device(inputs, lengths, attn_gain, mlp_gain, qkv_weight, attn_weight, mlp_in_weight, mlp_out_weight, cotangent):
    n_tp = lax.axis_size("tp")
    n_ctx = lax.axis_size("ctx")
    tp = lax.axis_index("tp")
    ctx = lax.axis_index("ctx")
    seqs, local = inputs.shape[1], inputs.shape[2]
    width = inputs.shape[3]
    group = n_tp // 2
    mine = tp % seqs
    pair = tp // 2
    tables = tuple(jnp.asarray(t) for t in rope_constants(local * n_ctx))

    n_shard = lax.axis_size("shard")
    shards = [jnp.transpose(qkv_weight, (1, 2, 0)), attn_weight[None], jnp.transpose(mlp_in_weight, (1, 2, 0)), mlp_out_weight[None]]
    gains = jnp.pad(jnp.stack([attn_gain, mlp_gain]), ((0, 14), (0, 0)))
    if n_shard != 2:
        shards = [lax.all_gather(s, "shard", axis=2, tiled=True) for s in shards]
        gains = lax.all_gather(gains, "shard", axis=1, tiled=True)
    hbm = pl.BlockSpec(memory_space=pl.ANY)
    vmem = pl.BlockSpec(memory_space=pltpu.VMEM)
    smem = pl.BlockSpec(memory_space=pltpu.SMEM)
    ext = local + 2 * HALF
    tiles = local // TILE
    chunks = width // LANES
    span = TILE + 2 * HALF
    wide = ((ext, width), BF16)
    tall = ((local, width), BF16)
    heads_rows, ff_rows = attn_weight.shape[0], mlp_out_weight.shape[0]
    full_shapes = [(2, 2, heads_rows, width), (2, 2, 2, ff_rows, width), (2, 2, ff_rows, width)]
    ff_half = 2 * mlp_out_weight.shape[0]
    width_half = width // 2
    saved = [
        ((2, 3, 2, shards[0].shape[1], width), BF16),
        wide, wide, wide, wide,
        ((tiles, chunks, 2 * TILE, span), BF16),
        tall,
    ]
    outs = [
        ((16, width), BF16),
        tall, tall,
        ((8, width), F32),
        ((ff_half, width), BF16), ((2 * ff_half, width), BF16), ((width_half, width), BF16),
    ]
    both = ((seqs, local, width), BF16)
    copies = 14 * Gather.SEMS + 24
    results = pl.pallas_call(
        functools.partial(front_kernel, n_shard),
        out_shape=[jax.ShapeDtypeStruct(*o) for o in saved + [both] + outs],
        in_specs=[smem] + [hbm] * 7 + [vmem] * 4,
        out_specs=[hbm] * 8 + [vmem] * 7,
        scratch_shapes=[pltpu.VMEM(*o) for o in saved]
        + [pltpu.VMEM(f, BF16) for f in full_shapes]
        + [
            pltpu.VMEM(*wide),
            pltpu.VMEM(*tall),
            pltpu.VMEM(*tall),
            pltpu.VMEM(*tall),
            pltpu.VMEM((local, ff_half), BF16),
            pltpu.VMEM((local, 2 * ff_half), BF16),
            pltpu.SemaphoreType.DMA((copies,)),
            pltpu.SemaphoreType.DMA((copies,)),
        ],
        compiler_params=pltpu.CompilerParams(collective_id=0, has_side_effects=True, vmem_limit_bytes=VMEM_LIMIT),
        name="front",
    )(lengths, inputs, cotangent, gains, *shards, *tables)
    wqkv, normed, q, k, v, probs, context, layer_all, gains, dctx, gml, gain2_part, dwm, dwi, dwo = results
    cols = width // n_shard if n_shard == 2 else width
    grads = [(3, 2, width_half // 2, width), (2, 2, ff_half // 2, width), (1, 2, ff_half // 2, width), (1, 2, width_half // 2, width), (1, 2, 32, width)]
    dwi, dwm, dwo = (g.reshape(shape) for g, shape in zip((dwi, dwm, dwo), grads[1:]))
    jobs = [(1, *grads[1][1:])] * 2 + grads[2:4] + [(1, *grads[0][1:])] * 3 + grads[4:]
    sends = 96
    homes = (q, k, v, probs, context, dctx, gml, normed, wqkv, dwi, dwm, dwo)
    layer_out, input_grad, *owned = pl.pallas_call(
        functools.partial(back_kernel, n_shard),
        out_shape=[jax.ShapeDtypeStruct(*both)] * 2 + [jax.ShapeDtypeStruct((g[0], g[2], cols), BF16) for g in grads],
        in_specs=[vmem] * 6 + [hbm] * 14,
        out_specs=[hbm] * 2 + [vmem] * len(grads),
        input_output_aliases={19: 0},
        scratch_shapes=[pltpu.VMEM(a.shape, a.dtype) for a in homes]
        + [
            pltpu.VMEM(*tall),
            pltpu.VMEM((ext, width), F32),
            pltpu.VMEM((ext, width), F32),
            pltpu.VMEM((local, 3 * width), BF16),
            pltpu.VMEM(*tall),
            pltpu.VMEM((2, 2, HALF, width), BF16),
            pltpu.VMEM((2, 2, HALF, width), BF16),
            pltpu.VMEM(grads[0], BF16),
            pltpu.VMEM((8, width), F32),
            pltpu.VMEM(grads[4], BF16),
            pltpu.SemaphoreType.DMA((sends,)),
            pltpu.SemaphoreType.DMA((sends,)),
        ]
        + [b for g in jobs for b in Reduce.scratch(g, n_shard)],
        compiler_params=pltpu.CompilerParams(collective_id=1, has_side_effects=True, vmem_limit_bytes=VMEM_LIMIT),
        name="back",
    )(gains, gain2_part, *tables, *homes, inputs, layer_all)
    gain_sums = owned.pop()
    flat = jax.ShapeDtypeStruct((seqs * local, width), BF16)
    layer_out, input_grad, *owned = pl.pallas_call(
        functools.partial(last_kernel, 2 + len(owned)),
        out_shape=[flat] * 2 + [jax.ShapeDtypeStruct(g.shape, F32) for g in owned],
        in_specs=[hbm] * (2 + len(owned)),
        out_specs=[hbm] * (2 + len(owned)),
        scratch_shapes=[pltpu.VMEM(g.shape, BF16) for g in owned]
        + [pltpu.VMEM(g.shape, F32) for g in owned]
        + [pltpu.VMEM(flat.shape, BF16)] * 2
        + [pltpu.SemaphoreType.DMA((2, len(owned) + 2 * (flat.shape[0] // (4 * TILE))))],
        compiler_params=pltpu.CompilerParams(vmem_limit_bytes=VMEM_LIMIT),
        name="last",
    )(layer_out.reshape(flat.shape), input_grad.reshape(flat.shape), *owned)
    layer_out, input_grad = (a.reshape(both[0]) for a in (layer_out, input_grad))
    owned.append(gain_sums.astype(F32))
    if n_shard != 2:
        owned = [lax.psum_scatter(g, "shard", scatter_dimension=2, tiled=True) for g in owned]
    qkv_grad = jnp.transpose(owned[0], (2, 0, 1))
    mlp_in_grad = jnp.transpose(owned[1], (2, 0, 1))
    mlp_out_grad, attn_grad = owned[2][0], owned[3][0]
    share = owned[4].shape[2] // n_tp
    gains = lax.dynamic_slice_in_dim(owned[4][0, :16], tp * share, share, axis=1)
    gains = jnp.sum(gains.reshape(2, 8, share), axis=1)
    return (layer_out[None], input_grad[None], qkv_grad, attn_grad, mlp_in_grad, mlp_out_grad, gains[0], gains[1])


def solution(mesh):
    in_specs = (
        P("shard", None, "ctx", None),
        P("shard", None),
        P("shard"),
        P("shard"),
        P("shard", None, "tp"),
        P("tp", "shard"),
        P("shard", None, "tp"),
        P("tp", "shard"),
        P("shard", None, "ctx", None),
    )
    out_specs = (
        P("shard", None, "ctx", None),
        P("shard", None, "ctx", None),
        P("shard", None, "tp"),
        P("tp", "shard"),
        P("shard", None, "tp"),
        P("tp", "shard"),
        P(("shard", "tp")),
        P(("shard", "tp")),
    )
    return jax.shard_map(on_device, mesh=mesh, in_specs=in_specs, out_specs=out_specs, check_vma=False)
```

```python
import functools
import math

import numpy as np

import jax
import jax.numpy as jnp
from jax import lax
from jax.experimental import pallas as pl
from jax.experimental.pallas import tpu as pltpu
from jax.sharding import PartitionSpec as P

HD = 64
HALF = 64
TILE = 128
LANES = 128
norm_eps = 1e-05
rope_base = 10000.0
masked_score = -1e30
F32 = jnp.float32
BF16 = jnp.bfloat16
FRONT_BLOCKS = 2
FORWARD = (
    (100, 101, 102, 106, 103, 200, 201, 104, 202, 300, 206, 400, 301, 105, 203, 401, 302, 204, 402, 306),
    {0: (107, 108, 109, 110), 1: (303, 205), 2: (304,)},
    {1: (207,), 2: (305, 111), 4: (208,), 5: (307,), 6: (209,), 7: (403, 404, 405)},
    {0: (112,), 1: (308, 210)},
    {1: (309, 211), 2: (113,), 3: (212, 310), 6: (311,), 7: (406, 407, 408, 409, 410, 213)},
    {0: (312, 313, 411, 412, 413)},
)
VMEM_LIMIT = 60 * 1024 * 1024


def nt(a, b):
    return lax.dot_general(a, b, (((1,), (1,)), ((), ())), preferred_element_type=F32)


def nn(a, b):
    return lax.dot_general(a, b, (((1,), (0,)), ((), ())), preferred_element_type=F32)


def tn(a, b):
    return lax.dot_general(a, b, (((0,), (0,)), ((), ())), preferred_element_type=F32)


def rope_constants(seq):
    w = rope_base ** (-np.arange(0, HD, 2) / HD)
    w = np.tile(w, 2 * LANES // HD)
    rows = np.arange(TILE)[:, None] * w
    blocks = (np.arange(seq // HALF + 4)[:, None] - 1) * HALF * w
    tables = (np.cos(rows), np.sin(rows), np.cos(blocks), np.sin(blocks))
    return tuple(t.astype(np.float32) for t in tables)


def rope_tile(tables, block):
    cos_r, sin_r, cos_b, sin_b = tables
    cb = cos_b[pl.ds(block + 1, 1), :]
    sb = sin_b[pl.ds(block + 1, 1), :]
    cr = cos_r[...]
    sr = sin_r[...]
    cosine = cr * cb - sr * sb
    sine = sr * cb + cr * sb
    first = lax.broadcasted_iota(jnp.int32, sine.shape, 1) % HD < HD // 2
    return cosine, jnp.where(first, -sine, sine), first


def turn(u, cosine, sine, first):
    other = jnp.where(first, pltpu.roll(u, LANES - HD // 2, 1), pltpu.roll(u, HD // 2, 1))
    return u * cosine + other * sine


def layer_stats(z):
    center = z - jnp.mean(z, axis=-1, keepdims=True)
    inv = lax.rsqrt(jnp.mean(center * center, axis=-1, keepdims=True) + norm_eps)
    return center * inv, inv


def layer_back(e, xhat, inv):
    return (e - jnp.mean(e, axis=-1, keepdims=True) - xhat * jnp.mean(e * xhat, axis=-1, keepdims=True)) * inv


def head_masks(shape):
    lane = lax.broadcasted_iota(jnp.int32, shape, 1)
    return lane < HD


def split_heads(c, low_head):
    zero = jnp.zeros_like(c)
    return jnp.concatenate([jnp.where(low_head, c, zero), jnp.where(low_head, zero, c)], axis=0)


def phase_norm(x_ref, gain_ref, normed_ref):
    def body(t, carry):
        r0 = pl.multiple_of(t * TILE, TILE)
        xhat, _ = layer_stats(x_ref[pl.ds(r0, TILE), :].astype(F32))
        normed_ref[pl.ds(r0, TILE), :] = (xhat * gain_ref[:1, :].astype(F32)).astype(BF16)
        return carry

    lax.fori_loop(0, x_ref.shape[0] // TILE, body, 0)


def phase_qkv(normed_ref, w_ref, tables, q_ref, k_ref, v_ref, block0, rows, which, after):
    width = normed_ref.shape[1]
    half = width // 2
    scaling = 1.0 / math.sqrt(HD)

    def body(t, carry):
        r0 = pl.multiple_of(t * rows, rows)
        out = nt(normed_ref[pl.ds(r0, rows), :], w_ref[which].reshape(3 * half, width))
        for s in range(rows // TILE):
            here = pl.ds(r0 + s * TILE, TILE)
            cosine, sine, first = rope_tile(tables, block0 + t * (rows // HALF) + s * (TILE // HALF))
            for part, ref in enumerate((q_ref, k_ref)):
                if part == 0:
                    turns = cosine * scaling, sine * scaling, first
                else:
                    turns = cosine, sine, first
                for j in range(half // LANES):
                    u = out[s * TILE : (s + 1) * TILE, part * half + j * LANES : part * half + (j + 1) * LANES]
                    ref[here, which * half + j * LANES : which * half + (j + 1) * LANES] = turn(u, *turns).astype(BF16)
        v_ref[pl.ds(r0, rows), which * half : (which + 1) * half] = out[:, 2 * half :].astype(BF16)
        after(t)
        return carry

    lax.fori_loop(0, normed_ref.shape[0] // rows, body, 0)


def phase_attend(q_ref, k_ref, v_ref, p_ref, ctx_ref, pos0, length, chunks, lo, hi, after):
    span = TILE + 2 * HALF

    def body(t, carry):
        r0 = pl.multiple_of(t * TILE, TILE)
        row = lax.broadcasted_iota(jnp.int32, (TILE, span), 0)
        col = lax.broadcasted_iota(jnp.int32, (TILE, span), 1)
        offset = col - row
        key_pos = pos0 + t * TILE - HALF + col
        allowed = (offset >= 0) & (offset <= 2 * HALF) & (key_pos >= 0) & ((key_pos < length) | (offset == HALF))
        bias = jnp.where(allowed, 0.0, masked_score).astype(F32)
        bias = jnp.concatenate([bias, bias], axis=0)
        low_head = head_masks((TILE, LANES))
        lanes = [slice(j * LANES, (j + 1) * LANES) for j in chunks]
        queries = [split_heads(q_ref[pl.ds(r0 + HALF, TILE), at], low_head) for at in lanes]
        scores = [nt(q2, k_ref[pl.ds(r0, span), at]) + bias for q2, at in zip(queries, lanes)]
        terms = [jnp.exp(s - jnp.max(s, axis=-1, keepdims=True)) for s in scores]
        probs = [(e * (1.0 / jnp.sum(e, axis=-1, keepdims=True))).astype(BF16) for e in terms]
        outs = [nn(p, v_ref[pl.ds(r0, span), at]) for p, at in zip(probs, lanes)]
        for j, p, out, at in zip(chunks, probs, outs, lanes):
            p_ref[t, j] = p
            ctx_ref[pl.ds(r0, TILE), at] = jnp.where(low_head, out[:TILE], out[TILE:]).astype(BF16)
        after(t)
        return carry

    lax.fori_loop(lo, hi, body, 0)


def units(nm, grad_low, wg, wu, wm):
    gate = nt(nm, wg)
    up = nt(nm, wu)
    cdf = 0.5 + 0.5 * lax.erf(gate * math.sqrt(0.5))
    gelu = gate * cdf
    slope = cdf + gate * (jnp.exp(-0.5 * gate * gate) * (1.0 / math.sqrt(2.0 * math.pi)))
    grad_hidden = nt(grad_low, wm)
    return (gelu * up).astype(BF16), (grad_hidden * up * slope).astype(BF16), (grad_hidden * gelu).astype(BF16)


def phase_mlp(x_ref, cot_ref, ctx_ref, gain_ref, wo_ref, wi_refs, wm_refs, out_ref, gml_ref, nm_ref, hid_ref, dgu_ref, dctx_ref, gg_ref, pos0, length, rows, between_halves, ready):
    half = wm_refs[0].shape[0]
    gg_ref[...] = jnp.zeros_like(gg_ref)

    def body(t, carry):
        r0 = pl.multiple_of(t * rows, rows)
        here = pl.ds(r0, rows)
        gain = gain_ref[1:2, :].astype(F32)
        middle = x_ref[pl.ds(r0 + HALF, rows), :].astype(F32) + nn(ctx_ref[here, :], wo_ref[...])
        xhat, inv = layer_stats(middle)
        nm = (xhat * gain).astype(BF16)
        nm_ref[here, :] = nm
        valid = pos0 + r0 + lax.broadcasted_iota(jnp.int32, (rows, 1), 0) < length
        grad_low = jnp.where(valid, cot_ref[here, :].astype(F32), 0.0).astype(BF16)
        cot_ref[here, :] = grad_low
        wg, wu, wm = wi_refs[0][:half, :], wi_refs[0][half:, :], wm_refs[0][...]
        hidden, grad_gate, grad_up = units(nm, grad_low, wg, wu, wm)
        hid_ref[here, :] = hidden
        dgu_ref[here, :half] = grad_gate
        dgu_ref[here, half:] = grad_up
        mlp = nn(hidden, wm)
        grad_nm = nn(grad_gate, wg) + nn(grad_up, wu)
        between_halves(t)
        wg, wu, wm = wi_refs[1][:half, :], wi_refs[1][half:, :], wm_refs[1][...]
        hidden, grad_gate, grad_up = units(nm, grad_low, wg, wu, wm)
        out_ref[here, :] = jnp.where(valid, middle + (mlp + nn(hidden, wm)), 0.0).astype(BF16)
        ready(t)
        grad_nm = grad_nm + nn(grad_gate, wg) + nn(grad_up, wu)
        gg_ref[...] += jnp.sum((grad_nm * xhat).reshape(rows // 8, 8, -1), axis=0)
        gm_low = (grad_low.astype(F32) + layer_back(grad_nm * gain, xhat, inv)).astype(BF16)
        gml_ref[here, :] = gm_low
        dctx_ref[here, :] = nt(gm_low, wo_ref[...]).astype(BF16)
        return carry

    lax.fori_loop(0, ctx_ref.shape[0] // rows, body, 0)


def phase_attend_back(q_ref, k_ref, v_ref, p_ref, ctx_ref, dctx_ref, tables, dqkv_ref, dk_ref, dv_ref, block0, lo, hi, after):
    width = q_ref.shape[1]
    half = width // 2
    span = TILE + 2 * HALF
    scaling = 1.0 / math.sqrt(HD)

    def body(t, carry):
        r0 = pl.multiple_of(t * TILE, TILE)
        low_head = head_masks((TILE, LANES))
        cosine, sine, first = rope_tile(tables, block0 + 1 + t * (TILE // HALF))
        cosine, sine = cosine * scaling, sine * -scaling
        keys = pl.ds(r0, span)
        for j in range(width // LANES):
            lanes = slice(j * LANES, (j + 1) * LANES)
            probs = p_ref[t, j]
            kc = k_ref[keys, lanes]
            dc = dctx_ref[pl.ds(r0, TILE), lanes]
            row_term = dc.astype(F32) * ctx_ref[pl.ds(r0, TILE), lanes].astype(F32)
            row_low = jnp.sum(jnp.where(low_head, row_term, 0.0), axis=-1, keepdims=True)
            row_high = jnp.sum(jnp.where(low_head, 0.0, row_term), axis=-1, keepdims=True)
            row_term = jnp.concatenate([row_low, row_high], axis=0)
            dc2 = split_heads(dc, low_head)
            grad_probs = nt(dc2, v_ref[keys, lanes])
            grad_scores = (probs.astype(F32) * (grad_probs - row_term)).astype(BF16)
            dq2 = nn(grad_scores, kc)
            dq = jnp.where(low_head, dq2[:TILE], dq2[TILE:])
            at = 3 * half * (j * LANES // half) + j * LANES % half
            dqkv_ref[pl.ds(r0, TILE), at : at + LANES] = turn(dq, cosine, sine, first).astype(BF16)
            q2 = split_heads(q_ref[pl.ds(r0 + HALF, TILE), lanes], low_head)
            dk_ref[keys, lanes] += tn(grad_scores, q2)
            dv_ref[keys, lanes] += tn(probs, dc2)
        after(t)
        return carry

    lax.fori_loop(lo, hi, body, 0)


def phase_pack(dk_ref, dv_ref, tables, dqkv_ref, block0, lo, hi):
    width = dk_ref.shape[1]
    half = width // 2

    def body(t, carry):
        r0 = pl.multiple_of(t * TILE, TILE)
        cosine, sine, first = rope_tile(tables, block0 + 1 + t * (TILE // HALF))
        ext = pl.ds(r0 + HALF, TILE)
        for j in range(width // LANES):
            lanes = slice(j * LANES, (j + 1) * LANES)
            at = 3 * half * (j * LANES // half) + j * LANES % half
            dqkv_ref[pl.ds(r0, TILE), at + half : at + half + LANES] = turn(dk_ref[ext, lanes], cosine, -sine, first).astype(BF16)
            dqkv_ref[pl.ds(r0, TILE), at + 2 * half : at + 2 * half + LANES] = dv_ref[ext, lanes].astype(BF16)
        return carry

    lax.fori_loop(lo, hi, body, 0)


def phase_input(x_ref, gm_ref, gain_ref, w_ref, dqkv_ref, out_ref, gg_ref, r0, rows):
    here = pl.ds(r0, rows)
    gain = gain_ref[:1, :].astype(F32)
    grad_normed = nn(dqkv_ref[here, :], w_ref[...])
    xhat, inv = layer_stats(x_ref[here, :].astype(F32))
    gg_ref[...] += jnp.sum((grad_normed * xhat).reshape(rows // 8, 8, -1), axis=0)
    out_ref[here, :] = (gm_ref[here, :].astype(F32) + layer_back(grad_normed * gain, xhat, inv)).astype(BF16)


def weight_grad(a_ref, b, out_ref, columns, at=0, count=None):
    for c in range(0, a_ref.shape[1] if count is None else count, columns):
        out_ref[c : c + columns, :] = tn(a_ref[:, at + c : at + c + columns], b).astype(out_ref.dtype)


def slot_of(at, of):
    return (of + 2 * (at // 2)) % 4


class Place:
    def __init__(self, n_shard):
        self.split = n_shard == 2
        self.x = lax.axis_index("shard")
        self.c = lax.axis_index("ctx")
        self.z = lax.axis_index("tp")
        self.k = self.c % 2
        self.y = self.c // 2
        self.up = (self.z + 1) % 4
        self.down = (self.z + 3) % 4
        self.mate = self.z + 1 - 2 * (self.z % 2)
        self.core = self.c + 1 - 2 * self.k
        self.across = (self.c + 2) % 4
        self.to_x = {"shard": 1 - self.x}
        self.to_up = {"tp": self.up}
        self.to_down = {"tp": self.down}
        self.to_mate = {"tp": self.mate}
        self.to_core = {"ctx": self.core}
        self.to_y = {"ctx": self.across}
        self.to_next = {"ctx": (self.c + 1) % 4}
        self.to_prev = {"ctx": (self.c + 3) % 4}

    def meet(self, partners):
        barrier = pltpu.get_barrier_semaphore()
        for device in partners:
            pl.semaphore_signal(barrier, inc=1, device_id=device, device_id_type=pl.DeviceIdType.MESH)
        pl.semaphore_wait(barrier, len(partners))


class Wires:
    def __init__(self, send, recv):
        self.send, self.recv, self.next, self.open = send, recv, 0, []

    def block(self, count):
        base = self.next
        self.next += count
        return base

    def remote(self, i, src, dst, device):
        return pltpu.make_async_remote_copy(
            src_ref=src, dst_ref=dst, send_sem=self.send.at[i], recv_sem=self.recv.at[i], device_id=device, device_id_type=pl.DeviceIdType.MESH
        )

    def local(self, i, src, dst):
        return pltpu.make_async_copy(src, dst, self.recv.at[i])

    def go(self, src, dst, device):
        copy = self.remote(self.block(1), src, dst, device)
        copy.start()
        self.open.append(copy)
        return copy

    def own(self, src, dst):
        copy = self.local(self.block(1), src, dst)
        copy.start()
        return copy

    @staticmethod
    def done(copies):
        for copy in copies:
            copy.wait()

    def close(self):
        for copy in self.open:
            copy.wait_send()


def started(copies):
    for copy in copies:
        copy.start()


class Stream:
    def __init__(self, wires, here, stage, target, rows, sent):
        self.wires, self.here, self.stage, self.target, self.rows, self.sent = wires, here, stage, target, rows, sent
        self.count = target.shape[1] // rows
        self.base = wires.block(2 * self.count)

    def block(self, t):
        rows = pl.ds(pl.multiple_of(t * self.rows, self.rows), self.rows)
        dst = self.target.at[self.here.z % 2, rows, :]
        return dst if self.stage is None else self.stage.at[rows, :], dst

    def remote(self, t):
        return self.wires.remote(self.base + t, *self.block(t), self.here.to_mate)

    def local(self, t):
        return self.wires.local(self.base + self.count + t, *self.block(t))

    def start(self, t):
        self.local(t).start()
        pl.when(t < self.sent)(lambda: self.remote(t).start())

    def finish(self):
        for t in range(self.count):
            self.local(t).wait()
        for t in range(self.sent):
            self.remote(t).wait()


def landed(copies):
    for copy in copies:
        copy.wait_recv()


class Gather:
    SEMS = 7

    def __init__(self, shard, full, which, wires, here):
        self.shard, self.full, self.wires, self.here = shard, full, wires, here
        rows = shard.shape[0] // 6
        self.carried = pl.ds(rows * (3 * here.k + here.y), 2 * rows)
        self.mine = pl.ds(rows * (3 * here.k + 2 * here.y), rows)
        self.theirs = pl.ds(rows * (3 * here.k + 2 - 2 * here.y), rows)
        other = (here.z + 2) % 4
        self.to = [other, other + 1 - 2 * (other % 2)] if which else [here.mate]
        self.slots = [slot_of(to, here.z) - 2 * which for to in self.to]
        self.keeps = which == 0
        self.own_slot = here.z % 2
        self.base = wires.block(self.SEMS)

    def cols(self, x):
        cols = self.shard.shape[1]
        return pl.ds(pl.multiple_of(x * cols, LANES), cols) if self.here.split else pl.ds(0, cols)

    def spread(self):
        src, cols = self.shard.at[self.carried, :], self.cols(self.here.x)
        return [
            self.wires.remote(self.base + i, src, self.full.at[slot, self.carried, cols], {"tp": to})
            for i, (to, slot) in enumerate(zip(self.to, self.slots))
        ]

    def kept(self):
        if not self.keeps:
            return []
        dst = self.full.at[self.own_slot, self.carried, self.cols(self.here.x)]
        return [self.wires.local(self.base + 2, self.shard.at[self.carried, :], dst)]

    def crossed(self):
        if not self.here.split:
            return []
        block = self.full.at[:, self.carried, self.cols(self.here.x)]
        return [self.wires.remote(self.base + 3, block, block, self.here.to_x)]

    def level(self):
        block = self.full.at[:, self.mine, :]
        return [self.wires.remote(self.base + 4, block, block, self.here.to_y)]

    def pooled(self):
        block = self.full.at[:, self.carried, :]
        return [self.wires.remote(self.base + 5, block, block, self.here.to_core)]

    def passed(self):
        block = self.full.at[:, self.theirs, :]
        return [self.wires.remote(self.base + 6, block, block, self.here.to_core)]

    def stage(self, number):
        if number == 0:
            started(self.spread())
            started(self.kept())
        elif number == 1:
            landed(self.spread())
            self.wires.done(self.kept())
            started(self.crossed())
        elif number == 2:
            landed(self.crossed())
            started(self.level())
            started(self.pooled())
        elif number == 3:
            landed(self.level())
            started(self.passed())
        else:
            landed(self.pooled())
            landed(self.passed())

    def close(self):
        for copy in self.spread() + self.crossed() + self.level() + self.pooled() + self.passed():
            copy.wait_send()


def fire(jobs, *events):
    for event in events:
        jobs[event % 100].stage(event // 100)


def between(jobs, table):
    def after(t):
        for step, events in table.items():
            pl.when(t == step)(functools.partial(fire, jobs, *events))

    return after


class Reduce:
    SEMS = 5

    def __init__(self, grad, out, bufs, wires, here):
        self.grad, self.out, self.wires, self.here = grad, out, wires, here
        self.a, self.b, self.d, self.e = bufs
        rows = grad.shape[2] // 2
        self.keep = pl.ds(rows * here.k, rows)
        self.give = pl.ds(rows * (1 - here.k), rows)
        self.zs = here.z % 2
        self.base = wires.block(self.SEMS)

    @staticmethod
    def scratch(shape, n_shard):
        k, two, rows, width = shape
        cols = width // n_shard if n_shard == 2 else width
        half = rows // 2
        return [pltpu.VMEM(s, BF16) for s in ((k, two, half, width), (k, two, half, cols), (k, half, cols), (k, half, cols))]

    def cols(self, x):
        cols = self.out.shape[2]
        return pl.ds(pl.multiple_of(x * cols, LANES), cols)

    def copy(self, number):
        h, remote = self.here, self.wires.remote
        if number == 0:
            return remote(self.base, self.grad.at[:, :, self.give, :], self.a, h.to_core)
        if number == 1:
            return remote(self.base + 1, self.a.at[:, :, :, self.cols(1 - h.x)], self.b, h.to_x)
        if number == 2:
            return remote(self.base + 2, self.b.at[:, 1 - self.zs, :, :], self.d, h.to_mate)
        if number == 3:
            return remote(self.base + 3, self.d, self.e, h.to_y)
        done = self.out.at[:, self.keep, :]
        return remote(self.base + 4, done, done, h.to_core)

    def stage(self, number):
        if number > 0 and (self.here.split or number != 2):
            self.copy(number - 1).wait_recv()
        if number == 1:
            total = (self.grad[:, :, self.keep, :].astype(F32) + self.a[...].astype(F32)).astype(BF16)
            if not self.here.split:
                self.b[...] = total
                return
            self.a[...] = total
        elif number == 2 and self.here.split:
            self.b[...] = (self.a[:, :, :, self.cols(self.here.x)].astype(F32) + self.b[...].astype(F32)).astype(BF16)
        elif number == 3:
            self.d[...] = (self.b[:, self.zs, :, :].astype(F32) + self.d[...].astype(F32)).astype(BF16)
        elif number == 4:
            self.out[:, self.keep, :] = (self.d[...].astype(F32) + self.e[...].astype(F32)).astype(BF16)
        if number < 5:
            self.copy(number).start()

    def close(self):
        for number in range(5):
            if self.here.split or number != 1:
                self.copy(number).wait_send()


def front_kernel(n_shard, len_ref, x_ref, cot_hbm, gains_ref, *refs):
    shards, tables, refs = refs[:4], refs[4:8], refs[8:]
    saved, (layer_all, gains, dctx_home, gml_home, gg, dwm_home, dwi_home, dwo_home), refs = refs[:7], refs[7:15], refs[15:]
    wqkv, normed, q, k, v, p, ctx, wo, wi, wm, ext, cot, out, nm, hid, dgu, dctx, gml, dwm, dwi, dwo, send, recv = refs
    h = Place(n_shard)
    near = [{"tp": (h.z + i) % 4} for i in (1, 2, 3)] + [{"ctx": (h.c + i) % 4} for i in (1, 2, 3)]
    if h.split:
        near.append(h.to_x)
    h.meet(near)
    wires = Wires(send, recv)
    local = x_ref.shape[2]
    length, pos0, block0 = len_ref[0, h.z % 2], h.c * local, h.c * (local // HALF) - 1
    seq = x_ref.at[0, h.z % 2]
    kept = [wires.own(seq, ext.at[pl.ds(HALF, local), :]), wires.own(cot_hbm.at[0, h.z % 2], cot)]
    rims = [
        wires.go(seq.at[pl.ds(0, HALF), :], ext.at[pl.ds(HALF + local, HALF), :], h.to_prev),
        wires.go(seq.at[pl.ds(local - HALF, HALF), :], ext.at[pl.ds(0, HALF), :], h.to_next),
    ]
    if h.split:
        cols = gains_ref.shape[1]
        mine = gains.at[:, pl.ds(pl.multiple_of(h.x * cols, LANES), cols)]
        kept.append(wires.own(gains_ref, mine))
        rims.append(wires.go(gains_ref, mine, h.to_x))
    else:
        kept.append(wires.own(gains_ref, gains))
    jobs = [Gather(shards[0].at[i], wqkv.at[which, i], which, wires, h) for which in range(2) for i in range(3)]
    jobs += [Gather(shards[1].at[0], wo.at[which], which, wires, h) for which in range(2)]
    for which in range(2):
        jobs += [Gather(shards[2].at[i], wi.at[which, i], which, wires, h) for i in range(2)]
        jobs.append(Gather(shards[3].at[0], wm.at[which], which, wires, h))
    stream = Stream(wires, h, out, layer_all, 2 * TILE, FRONT_BLOCKS)
    fire(jobs, *range(14))
    wires.done(kept)
    landed(rims)
    phase_norm(ext, gains, normed)
    fire(jobs, *FORWARD[0])
    qkv = functools.partial(phase_qkv, normed, wqkv, tables, q, k, v, block0, 384)
    attend = functools.partial(phase_attend, q, k, v, p, ctx, pos0, length)
    tiles = local // TILE
    half = p.shape[1] // 2
    qkv(0, between(jobs, FORWARD[1]))
    attend(range(half), 0, tiles, between(jobs, FORWARD[2]))
    qkv(1, between(jobs, FORWARD[3]))
    attend(range(half, 2 * half), 0, tiles, between(jobs, FORWARD[4]))
    stores = [wires.own(src, dst) for src, dst in zip((wqkv, normed, q, k, v, p, ctx), saved)]
    width = wo.shape[-1]
    wo = wo.reshape(-1, width)
    wi_near, wi_far = (wi.at[i].reshape(-1, width) for i in range(2))
    wm_near, wm_far = (wm.at[i].reshape(-1, width) for i in range(2))
    rows = 2 * TILE
    wis, wms = (wi_near, wi_far), (wm_near, wm_far)
    phase_mlp(ext, cot, ctx, gains, wo, wis, wms, out, gml, nm, hid, dgu, dctx, gg, pos0, length, rows, between(jobs, FORWARD[5]), stream.start)
    stores += [wires.own(dctx, dctx_home), wires.own(gml, gml_home)]
    weight_grad(dgu, nm[...], dwi, 384)
    stores.append(wires.own(dwi, dwi_home))
    weight_grad(hid, cot[...], dwm, 192)
    stores.append(wires.own(dwm, dwm_home))
    weight_grad(ctx, gml[...], dwo, LANES, count=dwo.shape[0])
    stores.append(wires.own(dwo, dwo_home))
    wires.done(stores)
    stream.finish()
    for job in jobs:
        job.close()
    wires.close()


def back_kernel(n_shard, gains_ref, gain2, *refs):
    tables, homes, (x_ref, layer_in), outs, refs = refs[:4], refs[4:16], refs[16:18], refs[18:25], refs[25:]
    layer_all, input_all, out_qkv, out_wi, out_wm, out_wo, out_gain = outs
    q, k, v, p, ctx, dctx, gml, normed, wqkv, dwi, dwm, dwo, x = refs[:13]
    dk, dv, dqkv, given, rim_out, rim_in, dw, gg, gbuf, send, recv = refs[13:24]
    bufs = refs[24:]
    h = Place(n_shard)
    wires = Wires(send, recv)
    q_home, k_home, v_home, p_home, ctx_home, dctx_home, gml_home, normed_home, wqkv_home, dwi_home, dwm_home, dwo_home = homes
    local, width = x.shape
    block0 = h.c * (local // HALF) - 1
    tiles = local // TILE
    loads = [wires.own(src, dst) for src, dst in ((k_home, k), (v_home, v), (q_home, q), (dctx_home, dctx), (ctx_home, ctx))]
    order = [tiles - 1, *range(tiles - 1)]
    tile_loads = {t: wires.own(p_home.at[t], p.at[t]) for t in order[:3]}
    grad_loads = [wires.own(src, dst) for src, dst in ((dwi_home, dwi), (dwm_home, dwm), (dwo_home, dwo))]
    tile_loads.update({t: wires.own(p_home.at[t], p.at[t]) for t in order[3:]})
    late_loads = [wires.own(src, dst) for src, dst in ((x_ref.at[0, h.z % 2], x), (gml_home, gml), (wqkv_home, wqkv), (normed_home, normed))]
    near = [h.to_mate] + [{"ctx": (h.c + i) % 4} for i in (1, 2, 3)]
    if h.split:
        near.append(h.to_x)
    h.meet(near)
    dw_parts = [(dwi.at[pl.ds(0, 1)], out_wi.at[pl.ds(0, 1)]), (dwi.at[pl.ds(1, 1)], out_wi.at[pl.ds(1, 1)]), (dwm, out_wm), (dwo, out_wo)]
    dw_parts += [(dw.at[pl.ds(i, 1)], out_qkv.at[pl.ds(i, 1)]) for i in range(3)] + [(gbuf, out_gain)]
    jobs = [Reduce(g, o, bufs[4 * i : 4 * i + 4], wires, h) for i, (g, o) in enumerate(dw_parts)]
    rows = 2 * TILE
    last = Stream(wires, h, None, layer_all, rows, local // rows)
    for t in range(FRONT_BLOCKS, last.count):
        last.remote(t).start()
    stream = Stream(wires, h, given, input_all, rows, local // rows)
    dk[...] = jnp.zeros_like(dk)
    dv[...] = jnp.zeros_like(dv)
    gg[...] = jnp.zeros_like(gg)
    wires.done(loads)
    wires.done(tile_loads[t] for t in order[:2])
    weights = wqkv.reshape(-1, width)

    def back(lo, hi, table):
        phase_attend_back(q, k, v, p, ctx, dctx, tables, dqkv, dk, dv, block0, lo, hi, between(jobs, table))

    def pack(lo, hi):
        phase_pack(dk, dv, tables, dqkv, block0, lo, hi)

    def finish(i):
        phase_input(x, gml, gains_ref, weights, dqkv, given, gg, i * rows, rows)

    wires.done(grad_loads)
    fire(jobs, 0, 1, 2, 3)
    back(tiles - 1, tiles, {})
    fire(jobs, 100, 101)
    back(0, 1, {})
    ext = local + 2 * HALF
    for i, ref in enumerate((dk, dv)):
        rim_out[0, i] = ref[:HALF, :].astype(BF16)
        rim_out[1, i] = ref[ext - HALF :, :].astype(BF16)
    rims = [wires.go(rim_out.at[0], rim_in.at[0], h.to_prev), wires.go(rim_out.at[1], rim_in.at[1], h.to_next)]
    fire(jobs, 102, 103)
    wires.done(tile_loads[t] for t in order[2:])
    back(1, tiles - 1, {4: (200,), 6: (201,)})
    landed(rims)
    for i, ref in enumerate((dk, dv)):
        ref[HALF : 2 * HALF, :] += rim_in[1, i].astype(F32)
        ref[ext - 2 * HALF : ext - HALF, :] += rim_in[0, i].astype(F32)
    pack(0, tiles)
    wires.done(late_loads)
    finish(0)
    stream.start(0)
    half = width // 2
    own = normed[HALF : HALF + local, :]
    for i in range(3):
        weight_grad(dqkv, own, dw.at[i].reshape(half, width), LANES, at=i * half, count=half)
        fire(jobs, 4 + i)
    fire(jobs, 202, 203)
    finish(1)
    stream.start(1)
    fire(jobs, 104, 105, 106)
    finish(2)
    finish(3)
    gain_rows = jnp.concatenate([gg[...], gain2[...]], axis=0).astype(BF16)
    gain_rows = jnp.concatenate([gain_rows, gain_rows], axis=0)
    gbuf[0, 0] = gain_rows
    gbuf[0, 1] = gain_rows
    fire(jobs, 7, 300, 301, 107, 204, 205, 207, 206)
    stream.start(2)
    stream.start(3)
    fire(jobs, 302, 303, 400, 401, 402, 403, 304, 305, 307, 306, 500, 501, 502, 503, 404, 405, 407, 406, 504, 505, 507, 506)
    stream.finish()
    for t in range(FRONT_BLOCKS, last.count):
        last.remote(t).wait()
    for job in jobs:
        job.close()
    wires.close()


def last_kernel(n, *refs):
    sources, results, lows, highs, (layer_buf, input_buf, sems) = refs[:n], refs[n : 2 * n], refs[2 * n : 3 * n - 2], refs[3 * n - 2 : 4 * n - 4], refs[4 * n - 4 :]
    parts = []
    for i, (low, high) in enumerate(zip(lows, highs)):
        parts.append((sources[2 + i], low, high, results[2 + i]))
    for i, buf in enumerate((layer_buf, input_buf)):
        for at in range(0, buf.shape[0], 4 * TILE):
            rows = pl.ds(at, 4 * TILE)
            parts.append((sources[i].at[rows, :], buf.at[rows, :], buf.at[rows, :], results[i].at[rows, :]))
    loads = [pltpu.make_async_copy(src, low, sems.at[0, i]) for i, (src, low, _, _) in enumerate(parts)]
    stores = [pltpu.make_async_copy(high, dst, sems.at[1, i]) for i, (_, _, high, dst) in enumerate(parts)]
    started(loads)
    for i, (load, store) in enumerate(zip(loads, stores)):
        load.wait()
        if i < n - 2:
            parts[i][2][...] = parts[i][1][...].astype(F32)
        store.start()
    Wires.done(stores)


def on_device(inputs, lengths, attn_gain, mlp_gain, qkv_weight, attn_weight, mlp_in_weight, mlp_out_weight, cotangent):
    n_tp = lax.axis_size("tp")
    n_ctx = lax.axis_size("ctx")
    tp = lax.axis_index("tp")
    ctx = lax.axis_index("ctx")
    seqs, local = inputs.shape[1], inputs.shape[2]
    width = inputs.shape[3]
    group = n_tp // 2
    mine = tp % seqs
    pair = tp // 2
    tables = tuple(jnp.asarray(t) for t in rope_constants(local * n_ctx))

    n_shard = lax.axis_size("shard")
    shards = [jnp.transpose(qkv_weight, (1, 2, 0)), attn_weight[None], jnp.transpose(mlp_in_weight, (1, 2, 0)), mlp_out_weight[None]]
    gains = jnp.pad(jnp.stack([attn_gain, mlp_gain]), ((0, 14), (0, 0)))
    if n_shard != 2:
        shards = [lax.all_gather(s, "shard", axis=2, tiled=True) for s in shards]
        gains = lax.all_gather(gains, "shard", axis=1, tiled=True)
    hbm = pl.BlockSpec(memory_space=pl.ANY)
    vmem = pl.BlockSpec(memory_space=pltpu.VMEM)
    smem = pl.BlockSpec(memory_space=pltpu.SMEM)
    ext = local + 2 * HALF
    tiles = local // TILE
    chunks = width // LANES
    span = TILE + 2 * HALF
    wide = ((ext, width), BF16)
    tall = ((local, width), BF16)
    heads_rows, ff_rows = attn_weight.shape[0], mlp_out_weight.shape[0]
    full_shapes = [(2, 2, heads_rows, width), (2, 2, 2, ff_rows, width), (2, 2, ff_rows, width)]
    ff_half = 2 * mlp_out_weight.shape[0]
    width_half = width // 2
    saved = [
        ((2, 3, 2, shards[0].shape[1], width), BF16),
        wide, wide, wide, wide,
        ((tiles, chunks, 2 * TILE, span), BF16),
        tall,
    ]
    outs = [
        ((16, width), BF16),
        tall, tall,
        ((8, width), F32),
        ((ff_half, width), BF16), ((2 * ff_half, width), BF16), ((width_half, width), BF16),
    ]
    both = ((seqs, local, width), BF16)
    copies = 14 * Gather.SEMS + 32
    results = pl.pallas_call(
        functools.partial(front_kernel, n_shard),
        out_shape=[jax.ShapeDtypeStruct(*o) for o in saved + [both] + outs],
        in_specs=[smem] + [hbm] * 7 + [vmem] * 4,
        out_specs=[hbm] * 8 + [vmem, hbm, hbm, vmem, hbm, hbm, hbm],
        scratch_shapes=[pltpu.VMEM(*o) for o in saved]
        + [pltpu.VMEM(f, BF16) for f in full_shapes]
        + [
            pltpu.VMEM(*wide),
            pltpu.VMEM(*tall),
            pltpu.VMEM(*tall),
            pltpu.VMEM(*tall),
            pltpu.VMEM((local, ff_half), BF16),
            pltpu.VMEM((local, 2 * ff_half), BF16),
            pltpu.VMEM(*tall),
            pltpu.VMEM(*tall),
            pltpu.VMEM((ff_half, width), BF16),
            pltpu.VMEM((2 * ff_half, width), BF16),
            pltpu.VMEM((width_half, width), BF16),
            pltpu.SemaphoreType.DMA((copies,)),
            pltpu.SemaphoreType.DMA((copies,)),
        ],
        compiler_params=pltpu.CompilerParams(collective_id=0, has_side_effects=True, vmem_limit_bytes=VMEM_LIMIT),
        name="front",
    )(lengths, inputs, cotangent, gains, *shards, *tables)
    wqkv, normed, q, k, v, probs, context, layer_all, gains, dctx, gml, gain2_part, dwm, dwi, dwo = results
    cols = width // n_shard if n_shard == 2 else width
    grads = [(3, 2, width_half // 2, width), (2, 2, ff_half // 2, width), (1, 2, ff_half // 2, width), (1, 2, width_half // 2, width), (1, 2, 32, width)]
    dwi, dwm, dwo = (g.reshape(shape) for g, shape in zip((dwi, dwm, dwo), grads[1:]))
    jobs = [(1, *grads[1][1:])] * 2 + grads[2:4] + [(1, *grads[0][1:])] * 3 + grads[4:]
    sends = 96
    homes = (q, k, v, probs, context, dctx, gml, normed, wqkv, dwi, dwm, dwo)
    layer_out, input_grad, *owned = pl.pallas_call(
        functools.partial(back_kernel, n_shard),
        out_shape=[jax.ShapeDtypeStruct(*both)] * 2 + [jax.ShapeDtypeStruct((g[0], g[2], cols), BF16) for g in grads],
        in_specs=[vmem] * 6 + [hbm] * 14,
        out_specs=[hbm] * 2 + [vmem] * len(grads),
        input_output_aliases={19: 0},
        scratch_shapes=[pltpu.VMEM(a.shape, a.dtype) for a in homes]
        + [
            pltpu.VMEM(*tall),
            pltpu.VMEM((ext, width), F32),
            pltpu.VMEM((ext, width), F32),
            pltpu.VMEM((local, 3 * width), BF16),
            pltpu.VMEM(*tall),
            pltpu.VMEM((2, 2, HALF, width), BF16),
            pltpu.VMEM((2, 2, HALF, width), BF16),
            pltpu.VMEM(grads[0], BF16),
            pltpu.VMEM((8, width), F32),
            pltpu.VMEM(grads[4], BF16),
            pltpu.SemaphoreType.DMA((sends,)),
            pltpu.SemaphoreType.DMA((sends,)),
        ]
        + [b for g in jobs for b in Reduce.scratch(g, n_shard)],
        compiler_params=pltpu.CompilerParams(collective_id=1, has_side_effects=True, vmem_limit_bytes=VMEM_LIMIT),
        name="back",
    )(gains, gain2_part, *tables, *homes, inputs, layer_all)
    gain_sums = owned.pop()
    flat = jax.ShapeDtypeStruct((seqs * local, width), BF16)
    layer_out, input_grad, *owned = pl.pallas_call(
        functools.partial(last_kernel, 2 + len(owned)),
        out_shape=[flat] * 2 + [jax.ShapeDtypeStruct(g.shape, F32) for g in owned],
        in_specs=[hbm] * (2 + len(owned)),
        out_specs=[hbm] * (2 + len(owned)),
        scratch_shapes=[pltpu.VMEM(g.shape, BF16) for g in owned]
        + [pltpu.VMEM(g.shape, F32) for g in owned]
        + [pltpu.VMEM(flat.shape, BF16)] * 2
        + [pltpu.SemaphoreType.DMA((2, len(owned) + 2 * (flat.shape[0] // (4 * TILE))))],
        compiler_params=pltpu.CompilerParams(vmem_limit_bytes=VMEM_LIMIT),
        name="last",
    )(layer_out.reshape(flat.shape), input_grad.reshape(flat.shape), *owned)
    layer_out, input_grad = (a.reshape(both[0]) for a in (layer_out, input_grad))
    owned.append(gain_sums.astype(F32))
    if n_shard != 2:
        owned = [lax.psum_scatter(g, "shard", scatter_dimension=2, tiled=True) for g in owned]
    qkv_grad = jnp.transpose(owned[0], (2, 0, 1))
    mlp_in_grad = jnp.transpose(owned[1], (2, 0, 1))
    mlp_out_grad, attn_grad = owned[2][0], owned[3][0]
    share = owned[4].shape[2] // n_tp
    gains = lax.dynamic_slice_in_dim(owned[4][0, :16], tp * share, share, axis=1)
    gains = jnp.sum(gains.reshape(2, 8, share), axis=1)
    return (layer_out[None], input_grad[None], qkv_grad, attn_grad, mlp_in_grad, mlp_out_grad, gains[0], gains[1])


def solution(mesh):
    in_specs = (
        P("shard", None, "ctx", None),
        P("shard", None),
        P("shard"),
        P("shard"),
        P("shard", None, "tp"),
        P("tp", "shard"),
        P("shard", None, "tp"),
        P("tp", "shard"),
        P("shard", None, "ctx", None),
    )
    out_specs = (
        P("shard", None, "ctx", None),
        P("shard", None, "ctx", None),
        P("shard", None, "tp"),
        P("tp", "shard"),
        P("shard", None, "tp"),
        P("tp", "shard"),
        P(("shard", "tp")),
        P(("shard", "tp")),
    )
    return jax.shard_map(on_device, mesh=mesh, in_specs=in_specs, out_specs=out_specs, check_vma=False)
```
